32 devices in a mesh: dp: 8 (over y, x, core), seq: 4 (over z).
Axes of the slice: x: 2, y: 2, z: 4, core: 2. Of those that a mesh axis runs over, the one named last changes fastest.
Arguments:
- tokens: bfloat16 [24, 1024, 768], P('dp', 'seq'), may hold values from -6 to 6
- init_state: float32 [24, 384, 2], P('dp', 'seq'), may hold values from -6 to 6
- norm_mix: float32 [768], replicated, may hold values from 0.1 to 1.9
- w_in: bfloat16 [768, 768], replicated, may hold values from -0.21875 to 0.21875
- w_forget: bfloat16 [768, 384], replicated, may hold values from -0.21875 to 0.21875
- forget_bias: float32 [384], replicated, may hold values from 2 to 8
- phase: float32 [384], P('seq'), may hold values from -3.140625 to 3.140625
- w_ogate: bfloat16 [768, 768], replicated, may hold values from -0.21875 to 0.21875
- norm_group: float32 [768], replicated, may hold values from 0.1 to 1.9
- w_out: bfloat16 [768, 768], replicated, may hold values from -0.21875 to 0.21875
- norm_ffn: float32 [768], replicated, may hold values from 0.1 to 1.9
- w_gate: bfloat16 [768, 1536], replicated, may hold values from -0.21875 to 0.21875
- w_up: bfloat16 [768, 1536], replicated, may hold values from -0.21875 to 0.21875
- w_down: bfloat16 [1536, 768], replicated, may hold values from -0.15625 to 0.15625
- cotangent: bfloat16 [24, 1024, 768], P('dp', 'seq'), may hold values from -6 to 6
Outputs:
- mixed_out: bfloat16 [24, 1024, 768], P('dp', 'seq')
- grad_tokens: bfloat16 [24, 1024, 768], P('dp', 'seq')
- final_state: float32 [24, 384, 2], P('dp', 'seq')
- grad_norm_mix: float32 [768], P('dp')
- grad_w_in: float32 [768, 768], P('dp')
- grad_w_forget: float32 [768, 384], P('dp')
- grad_forget_bias: float32 [384], P('seq')
- grad_phase: float32 [384], P('seq')
- grad_w_ogate: float32 [768, 768], P('dp')
- grad_norm_group: float32 [768], P('dp')
- grad_w_out: float32 [768, 768], P('dp')
- grad_norm_ffn: float32 [768], P('dp')
- grad_w_gate: float32 [768, 1536], P('dp')
- grad_w_up: float32 [768, 1536], P('dp')
- grad_w_down: float32 [1536, 768], P('dp')
The draws below stay inside these ranges and needn't reach their ends.
All inputs are finite; a program needn't handle non-finite values.
Results may differ from the reference program's by a relative error of at most 0.015.
Values may be sent and summed in bfloat16 or wider, within the bound.
No kernel may reach another device: no remote copies, remote signals or barrier semaphores. Data moves between devices by JAX's collectives and lax.ppermute only.
A program may use at most 192 MiB of HBM per device.

```python
import jax
import jax.numpy as jnp
from jax import lax

D = 768
HC = 384
FF = 1536
GROUPS = 8
SEGS_DEV = 3
SEGMENTS = 24
LEN = 1024


def strengthened(array, stream_key, source, target, shards_of, factor):
    owner, partner = [(jnp.arange(array.shape[dim]) // (array.shape[dim] // shards_of)).reshape([-1 if axis == dim else 1 for axis in range(array.ndim)]) for dim in (source, target)]
    chosen = jax.random.permutation(stream_key, shards_of)[partner]
    strong = (owner == chosen) | (owner == (partner + shards_of // 2) % shards_of)
    return jnp.where(strong, factor * array, array)


def steps_of(stream_key, shape, cuts, least, largest):
    def one(dim, blocks):
        draws = jax.random.uniform(jax.random.fold_in(jax.random.fold_in(stream_key, 6), dim), (blocks,), jnp.float32, least / len(cuts), largest / len(cuts))
        return jnp.repeat(jnp.exp(draws), shape[dim] // blocks).reshape((-1,) + (1,) * (len(shape) - dim - 1))

    level = one(*cuts[0])
    for cut in cuts[1:]:
        level = level * one(*cut)
    return level


def gaussian(own_key, extent, deviation, bound, split=(), dtype=jnp.bfloat16):
    result = deviation * jax.random.normal(own_key, extent, jnp.float32)
    if split:
        result = result * steps_of(own_key, extent, split, -0.22, 0.18)
    return jnp.clip(result, -bound, bound).astype(dtype)


def heavy_noise(stream_key, shape, width, reach, split, heavy, dtype=jnp.bfloat16):
    drawn = width * jax.random.normal(stream_key, shape, jnp.float32)
    if split:
        drawn = drawn * steps_of(stream_key, shape, split, -0.22, 0.18)
    return jnp.clip(strengthened(drawn, jax.random.fold_in(stream_key, 3), *heavy), -reach, reach).astype(dtype)


def setup_inputs(seed: int = 0) -> dict:
    seeds = jax.random.split(jax.random.key(seed), 16)
    tokens = heavy_noise(seeds[0], (SEGMENTS, LEN, D), 1.0, 6.0, ((0, 8), (1, 4)), (0, 2, 8, 2.0))
    init_state = gaussian(seeds[1], (SEGMENTS, HC, 2), 1.0, 6.0, ((0, 8), (1, 4)), jnp.float32)
    norm_mix = jnp.clip(1.0 + 0.18 * jax.random.normal(seeds[2], (D,), jnp.float32), 0.1, 1.9)
    w_in = gaussian(seeds[3], (D, 2 * HC), D ** -0.5, 0.21875)
    w_forget = gaussian(seeds[4], (D, HC), D ** -0.5, 0.21875)
    forget_bias = jnp.clip(jax.random.uniform(seeds[5], (HC,), jnp.float32, 2.0, 8.0), 2.0, 8.0)
    phase = jnp.clip(jax.random.uniform(seeds[6], (HC,), jnp.float32, -3.140625, 3.140625), -3.140625, 3.140625)
    w_ogate = gaussian(seeds[7], (D, D), D ** -0.5, 0.21875)
    norm_group = jnp.clip(1.0 + 0.18 * jax.random.normal(seeds[8], (D,), jnp.float32), 0.1, 1.9)
    w_out = gaussian(seeds[9], (D, D), D ** -0.5, 0.21875)
    norm_ffn = jnp.clip(1.0 + 0.18 * jax.random.normal(seeds[10], (D,), jnp.float32), 0.1, 1.9)
    w_gate = gaussian(seeds[11], (D, FF), D ** -0.5, 0.21875)
    w_up = gaussian(seeds[12], (D, FF), D ** -0.5, 0.21875)
    w_down = gaussian(seeds[13], (FF, D), FF ** -0.5, 0.15625)
    cotangent = gaussian(seeds[14], (SEGMENTS, LEN, D), 1.0, 6.0, ((0, 8), (1, 4)))
    return dict(tokens=tokens, init_state=init_state, norm_mix=norm_mix, w_in=w_in, w_forget=w_forget, forget_bias=forget_bias, phase=phase, w_ogate=w_ogate, norm_group=norm_group, w_out=w_out, norm_ffn=norm_ffn, w_gate=w_gate, w_up=w_up, w_down=w_down, cotangent=cotangent)


@jax.custom_vjp
def low(v):
    return lax.optimization_barrier(v.astype(jnp.bfloat16)).astype(jnp.float32)

@jax.custom_vjp
def low_back(v):
    return v

def low_keep(v):
    return (low(v), None)

def low_pass(kept, grad):
    return (grad,)

def back_keep(v):
    return (v, None)

def back_low(kept, grad):
    return (low(grad),)
low.defvjp(low_keep, low_pass)
low_back.defvjp(back_keep, back_low)
epsilon = 1e-06
highest = lax.Precision.HIGHEST

def combine(former, latter):
    return (latter[0] * former[0] - latter[1] * former[1], latter[0] * former[1] + latter[1] * former[0], latter[0] * former[2] - latter[1] * former[3] + latter[2], latter[0] * former[3] + latter[1] * former[2] + latter[3])

def rms_unit(values):
    return values * lax.rsqrt(lax.optimization_barrier(jnp.mean(values * values, axis=-1, keepdims=True)) + epsilon)

def project(left, right):
    return jnp.einsum('btd,de->bte', left, right, precision=highest)

def forward(token_in, init_state, params):
    norm_mix, w_in, w_forget, forget_bias, phase, w_ogate, norm_group, w_out, norm_ffn, w_gate, w_up, w_down = params
    batch_size, length, model_width = token_in.shape
    channels = w_forget.shape[1]
    normed = low(rms_unit(token_in) * norm_mix)
    drive_in = low(low_back(project(normed, w_in)))
    forget_pre = low(low_back(project(normed, w_forget) + forget_bias))
    pairs = drive_in.reshape(batch_size, length, channels, 2)
    cand_re = jax.nn.silu(pairs[..., 0])
    cand_im = jax.nn.silu(pairs[..., 1])
    forget = jax.nn.sigmoid(forget_pre)
    decay_re = forget * jnp.cos(phase)
    decay_im = forget * jnp.sin(phase)
    drive_re = (1.0 - forget) * cand_re
    drive_im = (1.0 - forget) * cand_im
    start_re = init_state[:, None, :, 0]
    start_im = init_state[:, None, :, 1]
    first_re = drive_re[:, :1] + decay_re[:, :1] * start_re - decay_im[:, :1] * start_im
    first_im = drive_im[:, :1] + decay_re[:, :1] * start_im + decay_im[:, :1] * start_re
    drive_re = jnp.concatenate([first_re, drive_re[:, 1:]], axis=1)
    drive_im = jnp.concatenate([first_im, drive_im[:, 1:]], axis=1)
    scanned = lax.associative_scan(combine, (decay_re, decay_im, drive_re, drive_im), axis=1)
    state_re = scanned[2]
    state_im = scanned[3]
    final_state = jnp.stack([state_re[:, -1], state_im[:, -1]], axis=-1)
    states = low(low_back(jnp.stack([state_re, state_im], axis=-1)))
    grouped = states.reshape(batch_size, length, GROUPS, 2 * channels // GROUPS)
    grouped = grouped * lax.rsqrt(lax.optimization_barrier(jnp.mean(grouped * grouped, axis=-1, keepdims=True)) + epsilon)
    normalized = grouped.reshape(batch_size, length, model_width) * norm_group
    out_gate = low_back(project(normed, w_ogate))
    gated = low(normalized * jax.nn.silu(out_gate))
    branch = low_back(project(gated, w_out))
    middle = token_in + branch
    normed_ffn = low(rms_unit(middle) * norm_ffn)
    gate_val = low_back(project(normed_ffn, w_gate))
    up_val = low_back(project(normed_ffn, w_up))
    hidden = low(jax.nn.silu(gate_val) * up_val)
    ffn_out = low_back(project(hidden, w_down))
    return (middle + ffn_out, final_state)

def reference(tokens, init_state, norm_mix, w_in, w_forget, forget_bias, phase, w_ogate, norm_group, w_out, norm_ffn, w_gate, w_up, w_down, cotangent):
    params = tuple((argument.astype(jnp.float32) for argument in (norm_mix, w_in, w_forget, forget_bias, phase, w_ogate, norm_group, w_out, norm_ffn, w_gate, w_up, w_down)))
    block_count = SEGMENTS // SEGS_DEV
    token_blocks = tokens.astype(jnp.float32).reshape(block_count, SEGS_DEV, LEN, D)
    state_blocks = init_state.astype(jnp.float32).reshape(block_count, SEGS_DEV, HC, 2)
    cot_blocks = cotangent.astype(jnp.float32).reshape(block_count, SEGS_DEV, LEN, D)

    def step(totals, batch_items):
        piece_tokens, start_state, cot_block = batch_items

        def run(token_in, param_in):
            return forward(token_in, start_state, param_in)
        (block_out, final_state), pullback = jax.vjp(run, piece_tokens, params)
        grad_block, grad_params = pullback((cot_block, jnp.zeros_like(final_state)))
        totals = jax.tree.map(lambda left_val, right_val: left_val + right_val, totals, grad_params)
        return (totals, (block_out.astype(jnp.bfloat16), grad_block.astype(jnp.bfloat16), final_state))
    zero_grads = jax.tree.map(jnp.zeros_like, params)
    totals, (outputs, grad_all, finals) = lax.scan(step, zero_grads, (token_blocks, state_blocks, cot_blocks))
    return (outputs.reshape(SEGMENTS, LEN, D), grad_all.reshape(SEGMENTS, LEN, D), finals.reshape(SEGMENTS, HC, 2), totals[0], totals[1], totals[2], totals[3], totals[4], totals[5], totals[6], totals[7], totals[8], totals[9], totals[10], totals[11])
```

```python
import functools

import jax
import jax.numpy as jnp
from jax import lax
from jax.experimental import pallas as pl
from jax.experimental.pallas import tpu as pltpu
from jax.sharding import PartitionSpec as P

GROUPS = 8
CHUNKS = 8
LANES = 128
epsilon = 1e-06
BF = jnp.bfloat16
F32 = jnp.float32


def dot(a, b, dims=((1,), (0,))):
    return lax.dot_general(a, b, (dims, ((), ())), preferred_element_type=F32)


def silu_slope(values, logistic):
    return logistic * (1.0 + values * (1.0 - logistic))


def cmul(ar, ai, br, bi):
    return ar * br - ai * bi, ar * bi + ai * br


def put(ref, value):
    for g in range(ref.shape[0]):
        ref[g] = value[:, g * LANES : (g + 1) * LANES]


def get(ref):
    return jnp.concatenate([ref[g] for g in range(ref.shape[0])], axis=1)


def decays(pre, trig, lam_re, lam_im):
    ch = lam_re.shape[0] * LANES
    forget = jax.nn.sigmoid(pre[:, 2 * ch :])
    put(lam_re, forget * trig[0:1, :])
    put(lam_im, forget * trig[1:2, :])
    return forget


def drives(pre, trig, lam_re, lam_im, drv_re, drv_im):
    ch = lam_re.shape[0] * LANES
    forget = decays(pre, trig, lam_re, lam_im)
    put(drv_re, (1.0 - forget) * jax.nn.silu(pre[:, :ch]))
    put(drv_im, (1.0 - forget) * jax.nn.silu(pre[:, ch : 2 * ch]))


def summary_kernel(pre_ref, trig_ref, chunk_ref, total_ref, lam_re, lam_im, drv_re, drv_im):
    parts, span, _ = lam_re.shape
    step = span // CHUNKS
    drives(pre_ref[...].astype(F32), trig_ref[...], lam_re, lam_im, drv_re, drv_im)
    carried = [None] * parts
    for t in range(step):
        rows = pl.ds(t, CHUNKS, stride=step)
        for g in range(parts):
            lr, li = lam_re[g, rows, :], lam_im[g, rows, :]
            br, bi = drv_re[g, rows, :], drv_im[g, rows, :]
            if t == 0:
                carried[g] = (lr, li, br, bi)
            else:
                pr, pi, hr, hi = carried[g]
                pr, pi = cmul(lr, li, pr, pi)
                hr, hi = cmul(lr, li, hr, hi)
                carried[g] = (pr, pi, hr + br, hi + bi)
    for q in range(4):
        chunk_ref[q] = jnp.concatenate([carried[g][q] for g in range(parts)], axis=1)
    pr, pi, hr, hi = chunk_ref[0], chunk_ref[1], chunk_ref[2], chunk_ref[3]
    tp_r, tp_i, th_r, th_i = pr[0:1], pi[0:1], hr[0:1], hi[0:1]
    for k in range(1, CHUNKS):
        lr, li = pr[k : k + 1], pi[k : k + 1]
        th_r, th_i = cmul(lr, li, th_r, th_i)
        th_r, th_i = th_r + hr[k : k + 1], th_i + hi[k : k + 1]
        tp_r, tp_i = cmul(lr, li, tp_r, tp_i)
    total_ref[...] = jnp.concatenate([tp_r, tp_i, th_r, th_i], axis=0)


def states_kernel(
    rank_ref, pre_ref, trig_ref, chunk_ref, totals_ref, init_ref, perm_ref,
    y_ref, hr_ref, hi_ref, start_ref, final_ref,
    lam_re, lam_im, drv_re, drv_im,
):
    parts, span, _ = lam_re.shape
    step = span // CHUNKS
    ranks = totals_ref.shape[0]
    rank = rank_ref[0]
    drives(pre_ref[...].astype(F32), trig_ref[...], lam_re, lam_im, drv_re, drv_im)
    cr, ci = init_ref[0:1, :], init_ref[1:2, :]

    def after(k, cr, ci, take):
        nr, ni = cmul(totals_ref[k, 0:1, :], totals_ref[k, 1:2, :], cr, ci)
        nr, ni = nr + totals_ref[k, 2:3, :], ni + totals_ref[k, 3:4, :]
        return jnp.where(take, nr, cr), jnp.where(take, ni, ci)

    for k in range(ranks - 1, 0, -1):
        cr, ci = after(k, cr, ci, k <= rank)
    start_ref[...] = jnp.concatenate([cr, ci], axis=0)
    er, ei = after(0, cr, ci, rank >= 0)
    for k in range(ranks - 1, 0, -1):
        er, ei = after(k, er, ei, k > rank)
    final_ref[...] = jnp.concatenate([er, ei], axis=0)
    rows_r, rows_i = [cr], [ci]
    for k in range(CHUNKS - 1):
        cr, ci = cmul(chunk_ref[0, k : k + 1, :], chunk_ref[1, k : k + 1, :], cr, ci)
        cr, ci = cr + chunk_ref[2, k : k + 1, :], ci + chunk_ref[3, k : k + 1, :]
        rows_r.append(cr)
        rows_i.append(ci)
    hr, hi = jnp.concatenate(rows_r, axis=0), jnp.concatenate(rows_i, axis=0)
    carried = [(hr[:, g * LANES : (g + 1) * LANES], hi[:, g * LANES : (g + 1) * LANES]) for g in range(parts)]
    for t in range(step):
        rows = pl.ds(t, CHUNKS, stride=step)
        for g in range(parts):
            hr, hi = cmul(lam_re[g, rows, :], lam_im[g, rows, :], *carried[g])
            hr, hi = hr + drv_re[g, rows, :], hi + drv_im[g, rows, :]
            hr_ref[g, rows, :] = hr
            hi_ref[g, rows, :] = hi
            carried[g] = (hr, hi)
    split = jnp.concatenate([get(hr_ref).astype(BF), get(hi_ref).astype(BF)], axis=1)
    y_ref[...] = dot(split, perm_ref[...], ((1,), (1,))).astype(BF)


def adjoint_summary_kernel(
    pre_ref, trig_ref, dy_ref, perm_ref, chunk_ref, split_ref, total_ref, chain_ref, lam_re, lam_im, dy_re, dy_im
):
    parts, span, _ = lam_re.shape
    ch = parts * LANES
    step = span // CHUNKS
    decays(pre_ref[...].astype(F32), trig_ref[...], lam_re, lam_im)
    split = dot(dy_ref[...], perm_ref[...])
    split_ref[...] = split.astype(BF)
    put(dy_re, split[:, :ch])
    put(dy_im, split[:, ch:])
    carried = [None] * parts
    for t in range(step - 1, -1, -1):
        rows = pl.ds(t, CHUNKS, stride=step)
        for g in range(parts):
            gr, gi = dy_re[g, rows, :], dy_im[g, rows, :]
            if carried[g] is not None:
                gr, gi = gr + carried[g][0], gi + carried[g][1]
            carried[g] = cmul(lam_re[g, rows, :], -lam_im[g, rows, :], gr, gi)
    for q in range(2):
        chain_ref[q] = jnp.concatenate([carried[g][q] for g in range(parts)], axis=1)
    ar, ai = chain_ref[0], chain_ref[1]
    er, ei = ar[CHUNKS - 1 :], ai[CHUNKS - 1 :]
    for k in range(CHUNKS - 2, -1, -1):
        er, ei = cmul(chunk_ref[0, k : k + 1, :], -chunk_ref[1, k : k + 1, :], er, ei)
        er, ei = er + ar[k : k + 1], ei + ai[k : k + 1]
    total_ref[...] = jnp.concatenate([er, ei], axis=0)


def adjoint_kernel(
    rank_ref, pre_ref, trig_ref, dy_ref, hr_ref, hi_ref, start_ref, chunk_ref, chain_ref, totals_ref, adj_ref, perm_ref,
    dpre_ref, sums_ref,
    lam_re, lam_im, dy_re, dy_im,
):
    parts, span, _ = lam_re.shape
    ch = parts * LANES
    step = span // CHUNKS
    ranks = totals_ref.shape[0]
    rank = rank_ref[0]
    pre = pre_ref[...].astype(F32)
    trig = trig_ref[...]
    forget = decays(pre, trig, lam_re, lam_im)
    put(dy_re, dy_ref[:, :ch].astype(F32))
    put(dy_im, dy_ref[:, ch:].astype(F32))
    cr = jnp.zeros((1, ch), F32)
    ci = jnp.zeros((1, ch), F32)
    for k in range(1, ranks):
        nr, ni = cmul(totals_ref[k, 0:1, :], -totals_ref[k, 1:2, :], cr, ci)
        nr, ni = nr + adj_ref[k, 0:1, :], ni + adj_ref[k, 1:2, :]
        cr, ci = jnp.where(k > rank, nr, cr), jnp.where(k > rank, ni, ci)
    rows_r, rows_i = [cr], [ci]
    for k in range(CHUNKS - 1, 0, -1):
        cr, ci = cmul(chunk_ref[0, k : k + 1, :], -chunk_ref[1, k : k + 1, :], cr, ci)
        cr, ci = cr + chain_ref[0, k : k + 1, :], ci + chain_ref[1, k : k + 1, :]
        rows_r.append(cr)
        rows_i.append(ci)
    ar, ai = jnp.concatenate(rows_r[::-1], axis=0), jnp.concatenate(rows_i[::-1], axis=0)
    carried = [(ar[:, g * LANES : (g + 1) * LANES], ai[:, g * LANES : (g + 1) * LANES]) for g in range(parts)]
    for t in range(step - 1, -1, -1):
        rows = pl.ds(t, CHUNKS, stride=step)
        for g in range(parts):
            gr, gi = dy_re[g, rows, :] + carried[g][0], dy_im[g, rows, :] + carried[g][1]
            dy_re[g, rows, :] = gr
            dy_im[g, rows, :] = gi
            carried[g] = cmul(lam_re[g, rows, :], -lam_im[g, rows, :], gr, gi)
    gr, gi = get(dy_re), get(dy_im)
    first = lax.broadcasted_iota(jnp.int32, (span, ch), 0) == 0
    qr = jnp.where(first, start_ref[0:1, :], pltpu.roll(get(hr_ref), 1, 0))
    qi = jnp.where(first, start_ref[1:2, :], pltpu.roll(get(hi_ref), 1, 0))
    pin_re, pin_im = pre[:, :ch], pre[:, ch : 2 * ch]
    sig_re, sig_im = jax.nn.sigmoid(pin_re), jax.nn.sigmoid(pin_im)
    lr = gr * qr + gi * qi
    li = gi * qr - gr * qi
    turned_re = lr * trig[0:1, :] + li * trig[1:2, :]
    turned_im = li * trig[0:1, :] - lr * trig[1:2, :]
    df = turned_re - (gr * pin_re * sig_re + gi * pin_im * sig_im)
    keep = 1.0 - forget
    dre = (keep * gr * silu_slope(pin_re, sig_re)).astype(BF)
    dim = (keep * gi * silu_slope(pin_im, sig_im)).astype(BF)
    dpz = (forget * keep * df).astype(BF)
    joined = dot(jnp.concatenate([dre, dim], axis=1), perm_ref[...], ((1,), (1,)))
    dpre_ref[:, : 2 * ch] = joined.astype(BF)
    dpre_ref[:, 2 * ch :] = dpz
    sums_ref[...] = jnp.concatenate(
        [
            jnp.sum(dpz.astype(F32), axis=0, keepdims=True),
            jnp.sum(forget * turned_im, axis=0, keepdims=True),
        ],
        axis=0,
    )


def seg_spec(*shape):
    zeros = (0,) * len(shape)
    return pl.BlockSpec((None,) + shape, lambda s, *_: (s,) + zeros)


def ranked_spec(n, *shape):
    zeros = (0,) * len(shape)
    return pl.BlockSpec((n, None) + shape, lambda s, *_: (0, s) + zeros)


def whole_spec(*shape):
    zeros = (0,) * len(shape)
    return pl.BlockSpec(shape, lambda s, *_: zeros)


def scan_call(kernel, segs, span, ch, ins, outs, args, scalars=()):
    return pl.pallas_call(
        kernel,
        grid_spec=pltpu.PrefetchScalarGridSpec(
            num_scalar_prefetch=len(scalars),
            grid=(segs,),
            in_specs=ins,
            out_specs=[o[0] for o in outs],
            scratch_shapes=[pltpu.VMEM((ch // LANES, span, LANES), F32)] * 4,
        ),
        out_shape=[jax.ShapeDtypeStruct(o[1], o[2]) for o in outs],
        compiler_params=pltpu.CompilerParams(vmem_limit_bytes=30 * 1024 * 1024),
        cost_estimate=pl.CostEstimate(
            flops=100 * segs * span * ch, bytes_accessed=30 * segs * span * ch, transcendentals=6 * segs * span * ch
        ),
    )(*scalars, *args)


def shift_all(payload, axis, n):
    got = [payload]
    for k in range(1, n):
        got.append(lax.ppermute(payload, axis, [(i, (i + k) % n) for i in range(n)]))
    return jnp.stack(got)


def own_bit(axis, bit):
    return (lax.axis_index(axis) // bit) % 2


def swap(v, axis, n, bit):
    return lax.ppermute(v, axis, [(i, i ^ bit) for i in range(n)])


def halve(buf, dim, axis, n, bit):
    mine = own_bit(axis, bit)
    send = lax.dynamic_index_in_dim(buf, 1 - mine, dim, keepdims=False)
    keep = lax.dynamic_index_in_dim(buf, mine, dim, keepdims=False)
    got = swap(send, axis, n, bit)
    return (keep.astype(F32) + got.astype(F32)).astype(BF)


def rejoin(part, dim, axis, n, bit):
    mine = own_bit(axis, bit)
    other = swap(part, axis, n, bit)
    low = jnp.where(mine == 0, part, other)
    high = jnp.where(mine == 0, other, part)
    return jnp.concatenate([low, high], axis=dim)


def bits_of(n):
    bits, b = [], 1
    while b < n:
        bits.append(b)
        b *= 2
    return bits


def reduce_lane(buf, bits, ndp, zbits, nseq):
    left = sorted(bits, reverse=True)
    for b in bits:
        pos = left.index(b)
        buf = halve(buf, pos, "dp", ndp, b)
        left.remove(b)
    rows, cols = buf.shape
    dims = []
    for i, b in enumerate(zbits):
        dim = i % 2
        shape = list(buf.shape)
        shape[dim : dim + 1] = [2, shape[dim] // 2]
        buf = halve(buf.reshape(shape), dim, "seq", nseq, b)
        dims.append((dim, b))
    for dim, b in reversed(dims):
        buf = rejoin(buf, dim, "seq", nseq, b)
    return buf


def reduce_blocks(buf, ndp, nseq):
    bits, zbits = bits_of(ndp), bits_of(nseq)
    rows, cols = buf.shape[1:]
    buf = buf.reshape([2] * len(bits) + [rows, cols])
    buf = halve(buf, len(bits) - 1, "dp", ndp, 1)
    rest = bits[1:]
    half = (cols // LANES // 2) * LANES
    a = reduce_lane(buf[..., :half], rest, ndp, zbits, nseq)
    b = reduce_lane(buf[..., half:], rest[::-1], ndp, zbits[::-1], nseq)
    return jnp.concatenate([a, b], axis=1)


def local(
    ndp, nseq,
    tokens, init_state, norm_mix, w_in, w_forget, forget_bias, phase, w_ogate,
    norm_group, w_out, norm_ffn, w_gate, w_up, w_down, cotangent,
):
    segs, span, width = tokens.shape
    ch = w_forget.shape[1]
    hidden_width = w_gate.shape[1]
    count = segs * span
    rank = lax.axis_index("seq").astype(jnp.int32)
    mine_ch = ch // nseq

    def rms(v):
        inv = lax.rsqrt(jnp.mean(v * v, axis=-1, keepdims=True) + epsilon)
        return v * inv, inv

    def rms_back(unit, inv, gain, up):
        through = up * gain
        grad = inv * (through - unit * jnp.mean(through * unit, axis=-1, keepdims=True))
        return grad, jnp.sum(up * unit, axis=0)

    own = jnp.concatenate([phase[None, :], init_state.transpose(0, 2, 1).reshape(2 * segs, mine_ch)], axis=0)
    own = jnp.pad(own, ((0, -own.shape[0] % 8), (0, -mine_ch % LANES)))
    got = shift_all(own, "seq", nseq)
    order = (rank - jnp.arange(nseq)) % nseq
    full = jnp.take(got, order, axis=0)[:, :, :mine_ch].transpose(1, 0, 2).reshape(own.shape[0], ch)
    theta = full[0]
    start = full[1 : 1 + 2 * segs].reshape(segs, 2, ch)
    trig = jnp.stack([jnp.cos(theta), jnp.sin(theta)])

    col = jnp.arange(width)
    perm = (col[:, None] == 2 * (col % ch)[None, :] + (col // ch)[None, :]).astype(BF)

    x = tokens.reshape(count, width).astype(F32)
    cot = cotangent.reshape(count, width)
    unit_mix, inv_mix = rms(x)
    normed = (unit_mix * norm_mix).astype(BF)
    w_in_split = dot(w_in, perm).astype(BF)
    pre = jnp.concatenate(
        [dot(normed, w_in_split).astype(BF), (dot(normed, w_forget) + forget_bias).astype(BF)], axis=1
    ).reshape(segs, span, 3 * ch)

    chunk, total = scan_call(
        summary_kernel, segs, span, ch,
        [seg_spec(span, 3 * ch), whole_spec(2, ch)],
        [(seg_spec(4, CHUNKS, ch), (segs, 4, CHUNKS, ch), F32), (seg_spec(4, ch), (segs, 4, ch), F32)],
        (pre, trig),
    )
    totals = shift_all(total, "seq", nseq)
    y, h_re, h_im, begin, final = scan_call(
        states_kernel, segs, span, ch,
        [
            seg_spec(span, 3 * ch), whole_spec(2, ch), seg_spec(4, CHUNKS, ch), ranked_spec(nseq, 4, ch),
            seg_spec(2, ch), whole_spec(width, width),
        ],
        [
            (seg_spec(span, width), (segs, span, width), BF),
            (seg_spec(ch // LANES, span, LANES), (segs, ch // LANES, span, LANES), F32),
            (seg_spec(ch // LANES, span, LANES), (segs, ch // LANES, span, LANES), F32),
            (seg_spec(2, ch), (segs, 2, ch), F32),
            (seg_spec(2, ch), (segs, 2, ch), F32),
        ],
        (pre, trig, chunk, totals, start, perm),
        (rank[None],),
    )
    final_state = lax.dynamic_slice_in_dim(final, rank * mine_ch, mine_ch, axis=2).transpose(0, 2, 1)

    member = ((col[:, None] // (width // GROUPS)) == jnp.arange(GROUPS)[None, :]).astype(F32)

    def group_mean(v):
        sums = lax.dot_general(v, member, (((1,), (0,)), ((), ())), precision=lax.Precision.HIGHEST)
        return sums * (GROUPS / width)

    def spread(s):
        return lax.dot_general(s, member, (((1,), (1,)), ((), ())), precision=lax.Precision.HIGHEST)

    yf = y.reshape(count, width).astype(F32)
    group_inv = spread(lax.rsqrt(group_mean(yf * yf) + epsilon))
    group_unit = yf * group_inv
    normalized = group_unit * norm_group
    og = dot(normed, w_ogate)
    og_sig = jax.nn.sigmoid(og)
    gate_act = og * og_sig
    gated = (normalized * gate_act).astype(BF)
    middle = x + dot(gated, w_out)
    unit_ffn, inv_ffn = rms(middle)
    normed_ffn = (unit_ffn * norm_ffn).astype(BF)
    gate_val = dot(normed_ffn, w_gate)
    up_val = dot(normed_ffn, w_up)
    gate_sig = jax.nn.sigmoid(gate_val)
    gate_silu = gate_val * gate_sig
    hidden = (gate_silu * up_val).astype(BF)
    grad_hidden = dot(cot, w_down, ((1,), (1,)))
    grad_gate = (grad_hidden * up_val * silu_slope(gate_val, gate_sig)).astype(BF)
    grad_up = (grad_hidden * gate_silu).astype(BF)

    rows = width // ndp
    tall = hidden_width // width

    def blocks(a, b):
        out = dot(a, b, ((0,), (0,))).astype(BF)
        return out.reshape(ndp, rows, b.shape[1])

    g_down = dot(hidden, cot, ((0,), (0,))).astype(BF).reshape(ndp, tall, rows, width)
    ffn_buf = jnp.concatenate(
        [blocks(normed_ffn, grad_gate), blocks(normed_ffn, grad_up)] + [g_down[:, i] for i in range(tall)], axis=-1
    )
    ffn_sum = reduce_blocks(ffn_buf, ndp, nseq)

    mixed_out = (middle + dot(hidden, w_down)).astype(BF)
    grad_normed_ffn = dot(grad_gate, w_gate, ((1,), (1,))) + dot(grad_up, w_up, ((1,), (1,)))
    grad_mid_norm, gain_ffn = rms_back(unit_ffn, inv_ffn, norm_ffn, grad_normed_ffn)
    grad_middle = cot.astype(F32) + grad_mid_norm
    grad_branch = grad_middle.astype(BF)
    grad_gated = dot(grad_branch, w_out, ((1,), (1,)))
    grad_normalized = grad_gated * gate_act
    grad_og = (grad_gated * normalized * silu_slope(og, og_sig)).astype(BF)
    through = grad_normalized * norm_group
    grad_y = (group_inv * (through - group_unit * spread(group_mean(through * group_unit)))).astype(BF)
    gain_group = jnp.sum(grad_normalized * group_unit, axis=0)

    dy_split, adj, chain = scan_call(
        adjoint_summary_kernel, segs, span, ch,
        [
            seg_spec(span, 3 * ch), whole_spec(2, ch), seg_spec(span, width), whole_spec(width, width),
            seg_spec(4, CHUNKS, ch),
        ],
        [
            (seg_spec(span, width), (segs, span, width), BF),
            (seg_spec(2, ch), (segs, 2, ch), F32),
            (seg_spec(2, CHUNKS, ch), (segs, 2, CHUNKS, ch), F32),
        ],
        (pre, trig, grad_y.reshape(segs, span, width), perm, chunk),
    )
    adjs = shift_all(adj, "seq", nseq)
    dpre, sums = scan_call(
        adjoint_kernel, segs, span, ch,
        [
            seg_spec(span, 3 * ch), whole_spec(2, ch), seg_spec(span, width), seg_spec(ch // LANES, span, LANES),
            seg_spec(ch // LANES, span, LANES),
            seg_spec(2, ch), seg_spec(4, CHUNKS, ch), seg_spec(2, CHUNKS, ch), ranked_spec(nseq, 4, ch),
            ranked_spec(nseq, 2, ch), whole_spec(width, width),
        ],
        [(seg_spec(span, 3 * ch), (segs, span, 3 * ch), BF), (seg_spec(2, ch), (segs, 2, ch), F32)],
        (pre, trig, dy_split, h_re, h_im, begin, chunk, chain, totals, adjs, perm),
        (rank[None],),
    )
    dpre = dpre.reshape(count, 3 * ch)
    grad_normed = (
        dot(dpre[:, :width], w_in, ((1,), (1,)))
        + dot(dpre[:, width:], w_forget, ((1,), (1,)))
        + dot(grad_og, w_ogate, ((1,), (1,)))
    )
    grad_in_norm, gain_mix = rms_back(unit_mix, inv_mix, norm_mix, grad_normed)
    grad_tokens = (grad_middle + grad_in_norm).astype(BF)

    small = jnp.sum(sums, axis=0).reshape(2 * ch // LANES, LANES)
    gains = jnp.stack([gain_mix, gain_group, gain_ffn]).reshape(3, ndp, rows).transpose(1, 0, 2)
    vec = jnp.concatenate(
        [
            jnp.broadcast_to(small[None], (ndp,) + small.shape),
            jnp.pad(gains, ((0, 0), (0, 0), (0, LANES - rows))),
        ],
        axis=1,
    )
    vec = jnp.pad(vec, ((0, 0), (0, rows - vec.shape[1]), (0, 0))).astype(BF)
    mix_buf = jnp.concatenate(
        [blocks(normed, dpre), blocks(normed, grad_og), blocks(gated, grad_branch), vec], axis=-1
    )
    mix_sum = reduce_blocks(mix_buf, ndp, nseq).astype(F32)

    ffn_sum = ffn_sum.astype(F32)
    part_gate, part_up = ffn_sum[:, :hidden_width], ffn_sum[:, hidden_width : 2 * hidden_width]
    part_down = jnp.concatenate(
        [ffn_sum[:, 2 * hidden_width + i * width : 2 * hidden_width + (i + 1) * width] for i in range(tall)], axis=0
    )
    part_in, part_forget = mix_sum[:, :width], mix_sum[:, width : width + ch]
    part_ogate = mix_sum[:, width + ch : 2 * width + ch]
    part_out = mix_sum[:, 2 * width + ch : 3 * width + ch]
    tail = mix_sum[:, 3 * width + ch :]
    shared = tail[: small.shape[0]].reshape(2, ch)
    shared = lax.dynamic_slice_in_dim(shared, rank * mine_ch, mine_ch, axis=1)
    own_gains = tail[small.shape[0] : small.shape[0] + 3, :rows]
    return (
        mixed_out.reshape(segs, span, width),
        grad_tokens.reshape(segs, span, width),
        final_state,
        own_gains[0], part_in, part_forget, shared[0], shared[1], part_ogate, own_gains[1], part_out, own_gains[2],
        part_gate, part_up, part_down,
    )


def solution(mesh):
    ndp, nseq = mesh.shape["dp"], mesh.shape["seq"]
    tok, vec, col = P("dp", "seq", None), P("dp"), P("dp", None)
    return jax.shard_map(
        functools.partial(local, ndp, nseq),
        mesh=mesh,
        in_specs=(tok, tok, P(), P(), P(), P(), P("seq"), P(), P(), P(), P(), P(), P(), P(), tok),
        out_specs=(tok, tok, tok, vec, col, col, P("seq"), P("seq"), col, vec, col, vec, col, col, col),
        check_vma=False,
    )
```

```python
import functools

import jax
import jax.numpy as jnp
from jax import lax
from jax.experimental import pallas as pl
from jax.experimental.pallas import tpu as pltpu
from jax.sharding import PartitionSpec as P

GROUPS = 8
CHUNKS = 8
LANES = 128
TILE = 16
epsilon = 1e-06
BF = jnp.bfloat16
F32 = jnp.float32
NT = ((1,), (1,))


def dot(a, b, dims=((1,), (0,))):
    return lax.dot_general(a, b, (dims, ((), ())), preferred_element_type=F32)


def silu_slope(values, logistic):
    return logistic * (1.0 + values * (1.0 - logistic))


def cmul(ar, ai, br, bi):
    return ar * br - ai * bi, ar * bi + ai * br


def row_mean(v):
    return jnp.mean(v, axis=-1, keepdims=True)


def split_dot(v, m, dims):
    high = v.astype(BF)
    low = (v - high.astype(F32)).astype(BF)
    return dot(high, m, dims) + dot(low, m, dims)


def group_mean(v, member):
    return split_dot(v, member, ((1,), (0,))) * (GROUPS / v.shape[1])


def group_spread(v, member):
    return split_dot(v, member, NT)


def put_halves(ref, t, col, lo, bit):
    half = ref.shape[0] // 2
    for b in range(t.shape[0] // lo):
        at = jnp.where(bit == b % 2, half, 0) + (b // 2) * lo
        ref[pl.ds(pl.multiple_of(at, TILE), lo), col : col + t.shape[1]] = t[b * lo : (b + 1) * lo, :]


def put(ref, value):
    for g in range(ref.shape[0]):
        ref[g] = value[:, g * LANES : (g + 1) * LANES]


def get(ref):
    return jnp.concatenate([ref[g] for g in range(ref.shape[0])], axis=1)


def lanes(value, parts):
    return [value[:, g * LANES : (g + 1) * LANES] for g in range(parts)]


def decays(pre, trig, lam_re, lam_im):
    ch = lam_re.shape[0] * LANES
    forget = jax.nn.sigmoid(pre[:, 2 * ch :])
    put(lam_re, forget * trig[0:1, :])
    put(lam_im, forget * trig[1:2, :])
    return forget


def drives(pre, trig, lam_re, lam_im, drv_re, drv_im):
    ch = lam_re.shape[0] * LANES
    forget = decays(pre, trig, lam_re, lam_im)
    put(drv_re, (1.0 - forget) * jax.nn.silu(pre[:, :ch]))
    put(drv_im, (1.0 - forget) * jax.nn.silu(pre[:, ch : 2 * ch]))


def project_kernel(bit_ref, x_ref, gain_ref, w_in_ref, w_forget_ref, bias_ref, perm_ref, normed_ref, turned_ref, pre_ref, *, lo):
    width = x_ref.shape[1]
    x = x_ref[...].astype(F32)
    normed = (x * lax.rsqrt(row_mean(x * x) + epsilon) * gain_ref[...][None]).astype(BF)
    normed_ref[...] = normed
    put_halves(turned_ref, normed.T, 0, lo, bit_ref[0])
    mixed = dot(normed, w_in_ref[...]).astype(BF)
    pre_ref[:, :width] = dot(mixed, perm_ref[...]).astype(BF)
    pre_ref[:, width:] = (dot(normed, w_forget_ref[...]) + bias_ref[...][None]).astype(BF)


def summary_kernel(*refs, ranks):
    pre_ref, infos = refs[0], refs[1 : 1 + ranks]
    trig_ref, chunk_ref, total_ref, lam_re, lam_im, drv_re, drv_im = refs[1 + ranks :]
    parts, span, _ = lam_re.shape
    step = span // CHUNKS
    trig = infos[0][...]
    for info in infos[1:]:
        trig = trig + info[...]
    trig_ref[...] = trig
    drives(pre_ref[...].astype(F32), trig, lam_re, lam_im, drv_re, drv_im)
    carried = [None] * parts
    for t in range(step):
        rows = pl.ds(t, CHUNKS, stride=step)
        for g in range(parts):
            lr, li = lam_re[g, rows, :], lam_im[g, rows, :]
            br, bi = drv_re[g, rows, :], drv_im[g, rows, :]
            if t == 0:
                carried[g] = (lr, li, br, bi)
            else:
                pr, pi, hr, hi = carried[g]
                pr, pi = cmul(lr, li, pr, pi)
                hr, hi = cmul(lr, li, hr, hi)
                carried[g] = (pr, pi, hr + br, hi + bi)
    pr, pi, hr, hi = (jnp.concatenate([carried[g][q] for g in range(parts)], axis=1) for q in range(4))
    chunk_ref[0], chunk_ref[1], chunk_ref[2], chunk_ref[3] = pr, pi, hr, hi
    tp_r, tp_i, th_r, th_i = pr[0:1], pi[0:1], hr[0:1], hi[0:1]
    for k in range(1, CHUNKS):
        lr, li = pr[k : k + 1], pi[k : k + 1]
        th_r, th_i = cmul(lr, li, th_r, th_i)
        th_r, th_i = th_r + hr[k : k + 1], th_i + hi[k : k + 1]
        tp_r, tp_i = cmul(lr, li, tp_r, tp_i)
    total_ref[...] = jnp.concatenate([tp_r, tp_i, th_r, th_i], axis=0)


def mixer_kernel(*refs, ranks, lo):
    scalars, refs = refs[0], refs[1:]
    totals, inits, refs = refs[:ranks], refs[ranks : 2 * ranks], refs[2 * ranks :]
    pre_ref, trig_ref, chunk_ref, perm_ref, x_ref, og_ref, gain_ref, member_ref, w_out_ref = refs[:9]
    y_ref, hr_ref, hi_ref, start_ref, final_ref, turned_ref, middle_ref = refs[9:16]
    lam_re, lam_im, drv_re, drv_im = refs[16:]
    parts, span, _ = lam_re.shape
    step = span // CHUNKS
    rank, bit = scalars[0], scalars[1]
    drives(pre_ref[...].astype(F32), trig_ref[...], lam_re, lam_im, drv_re, drv_im)
    init = inits[0][...]
    for info in inits[1:]:
        init = init + info[...]
    cr, ci = init[0:1], init[1:2]

    def after(k, cr, ci, take):
        total = totals[k][...]
        nr, ni = cmul(total[0:1], total[1:2], cr, ci)
        nr, ni = nr + total[2:3], ni + total[3:4]
        return jnp.where(take, nr, cr), jnp.where(take, ni, ci)

    for k in range(ranks - 1, 0, -1):
        cr, ci = after(k, cr, ci, k <= rank)
    start_ref[...] = jnp.concatenate([cr, ci], axis=0)
    er, ei = after(0, cr, ci, rank >= 0)
    for k in range(ranks - 1, 0, -1):
        er, ei = after(k, er, ei, k > rank)
    final_ref[...] = jnp.concatenate([er, ei], axis=0)
    rows_r, rows_i = [cr], [ci]
    for k in range(CHUNKS - 1):
        cr, ci = cmul(chunk_ref[0, k : k + 1, :], chunk_ref[1, k : k + 1, :], cr, ci)
        cr, ci = cr + chunk_ref[2, k : k + 1, :], ci + chunk_ref[3, k : k + 1, :]
        rows_r.append(cr)
        rows_i.append(ci)
    carried = list(
        zip(lanes(jnp.concatenate(rows_r, axis=0), parts), lanes(jnp.concatenate(rows_i, axis=0), parts), strict=True)
    )
    for t in range(step):
        rows = pl.ds(t, CHUNKS, stride=step)
        for g in range(parts):
            hr, hi = cmul(lam_re[g, rows, :], lam_im[g, rows, :], *carried[g])
            hr, hi = hr + drv_re[g, rows, :], hi + drv_im[g, rows, :]
            hr_ref[g, rows, :] = hr
            hi_ref[g, rows, :] = hi
            carried[g] = (hr, hi)
    split = jnp.concatenate([get(hr_ref).astype(BF), get(hi_ref).astype(BF)], axis=1)
    yf = dot(split, perm_ref[...], NT)
    y_ref[...] = yf.astype(BF)
    member = member_ref[...]
    inv = group_spread(lax.rsqrt(group_mean(yf * yf, member) + epsilon), member)
    gated = (yf * inv * gain_ref[...][None] * jax.nn.silu(og_ref[...])).astype(BF)
    put_halves(turned_ref, gated.T, 0, lo, bit)
    middle_ref[...] = x_ref[...].astype(F32) + dot(gated, w_out_ref[...])


def ffn_kernel(
    bit_ref, middle_ref, gain_ref, cot_ref, wg_ref, wu_ref, wd_ref,
    gsend_ref, gkeep_ref, dsend_ref, dkeep_ref, mixed_ref, dn_ref,
    n_ref, nt_ref, acc_ref, hid_ref, dgv_ref, duv_ref, ht_ref,
    *, lo, dlo, rt,
):
    j, last = pl.program_id(0), pl.num_programs(0) - 1
    bit = bit_ref[0]
    count, width = middle_ref.shape
    tile = wg_ref.shape[1]
    spans = [slice(r, r + rt) for r in range(0, count, rt)]

    @pl.when(j == 0)
    def _():
        for rows in spans:
            v = middle_ref[rows, :]
            normed = (v * lax.rsqrt(row_mean(v * v) + epsilon) * gain_ref[...][None]).astype(BF)
            n_ref[rows, :] = normed
            put_halves(nt_ref, normed.T, rows.start, lo, bit)

    for rows in spans:
        g, u = dot(n_ref[rows, :], wg_ref[...]), dot(n_ref[rows, :], wu_ref[...])
        dh = dot(cot_ref[rows, :], wd_ref[...], NT)
        sig = jax.nn.sigmoid(g)
        act = g * sig
        hid_ref[rows, :] = (act * u).astype(BF)
        dgv_ref[rows, :] = (dh * u * silu_slope(g, sig)).astype(BF)
        duv_ref[rows, :] = (dh * act).astype(BF)
    for rows in spans:
        put_halves(ht_ref, hid_ref[rows, :].T, rows.start, dlo, bit)
    for lhs, ref in ((nt_ref[: width // 2, :], gsend_ref), (nt_ref[width // 2 :, :], gkeep_ref)):
        ref[:, :tile] = dot(lhs, dgv_ref[...]).astype(BF)
        ref[:, tile:] = dot(lhs, duv_ref[...]).astype(BF)
    for lhs, ref in ((ht_ref[: tile // 2, :], dsend_ref), (ht_ref[tile // 2 :, :], dkeep_ref)):
        ref[...] = dot(lhs, cot_ref[...]).astype(BF)
    for rows in spans:
        out = dot(hid_ref[rows, :], wd_ref[...])
        dn = dot(dgv_ref[rows, :], wg_ref[...], NT) + dot(duv_ref[rows, :], wu_ref[...], NT)

        @pl.when(j == 0)
        def _():
            acc_ref[rows, :] = middle_ref[rows, :] + out
            dn_ref[rows, :] = dn

        @pl.when(j > 0)
        def _():
            acc_ref[rows, :] += out
            dn_ref[rows, :] += dn

        @pl.when(j == last)
        def _():
            mixed_ref[rows, :] = acc_ref[rows, :].astype(BF)


def turn_kernel(
    dn_ref, middle_ref, cot_ref, ffn_gain_ref, w_out_ref, y_ref, og_ref, gain_ref, member_ref, perm_ref,
    pre_ref, trig_ref, chunk_ref,
    dmiddle_ref, dbranch_ref, dog_ref, split_ref, chain_ref, total_ref, gains_ref,
    lam_re, lam_im, dy_re, dy_im,
):
    parts, span, _ = lam_re.shape
    ch = parts * LANES
    step = span // CHUNKS
    v, up = middle_ref[...], dn_ref[...]
    inv = lax.rsqrt(row_mean(v * v) + epsilon)
    unit = v * inv
    through = up * ffn_gain_ref[...][None]
    dmiddle = cot_ref[...].astype(F32) + inv * (through - unit * row_mean(through * unit))
    gain_ffn = jnp.sum(up * unit, axis=0, keepdims=True)
    dmiddle_ref[...] = dmiddle
    dbranch = dmiddle.astype(BF)
    dbranch_ref[...] = dbranch
    dgated = dot(dbranch, w_out_ref[...], NT)
    og, yf, member, gain = og_ref[...], y_ref[...].astype(F32), member_ref[...], gain_ref[...][None]
    ginv = group_spread(lax.rsqrt(group_mean(yf * yf, member) + epsilon), member)
    gunit = yf * ginv
    sig = jax.nn.sigmoid(og)
    dog_ref[...] = (dgated * gunit * gain * silu_slope(og, sig)).astype(BF)
    dgn = dgated * og * sig
    gains = jnp.concatenate([gain_ffn, jnp.sum(dgn * gunit, axis=0, keepdims=True)], axis=0)

    @pl.when(pl.program_id(0) == 0)
    def _():
        gains_ref[...] = gains

    @pl.when(pl.program_id(0) > 0)
    def _():
        gains_ref[...] += gains

    through = dgn * gain
    dy = (ginv * (through - gunit * group_spread(group_mean(through * gunit, member), member))).astype(BF)
    split = dot(dy, perm_ref[...])
    split_ref[...] = split.astype(BF)
    decays(pre_ref[...].astype(F32), trig_ref[...], lam_re, lam_im)
    put(dy_re, split[:, :ch])
    put(dy_im, split[:, ch:])
    carried = [None] * parts
    for t in range(step - 1, -1, -1):
        rows = pl.ds(t, CHUNKS, stride=step)
        for g in range(parts):
            gr, gi = dy_re[g, rows, :], dy_im[g, rows, :]
            if carried[g] is not None:
                gr, gi = gr + carried[g][0], gi + carried[g][1]
            carried[g] = cmul(lam_re[g, rows, :], -lam_im[g, rows, :], gr, gi)
    ar, ai = (jnp.concatenate([carried[g][q] for g in range(parts)], axis=1) for q in range(2))
    chain_ref[0], chain_ref[1] = ar, ai
    er, ei = ar[CHUNKS - 1 :], ai[CHUNKS - 1 :]
    for k in range(CHUNKS - 2, -1, -1):
        er, ei = cmul(chunk_ref[0, k : k + 1, :], -chunk_ref[1, k : k + 1, :], er, ei)
        er, ei = er + ar[k : k + 1], ei + ai[k : k + 1]
    total_ref[...] = jnp.concatenate([er, ei], axis=0)


def adjoint_kernel(*refs, ranks):
    scalars, refs = refs[0], refs[1:]
    totals, adjs, refs = refs[:ranks], refs[ranks : 2 * ranks], refs[2 * ranks :]
    pre_ref, trig_ref, dy_ref, hr_ref, hi_ref, start_ref, chunk_ref, chain_ref, perm_ref = refs[:9]
    dpre_ref, sums_ref, lam_re, lam_im, dy_re, dy_im = refs[9:]
    parts, span, _ = lam_re.shape
    ch = parts * LANES
    step = span // CHUNKS
    rank = scalars[0]
    pre = pre_ref[...].astype(F32)
    trig = trig_ref[...]
    forget = decays(pre, trig, lam_re, lam_im)
    put(dy_re, dy_ref[:, :ch].astype(F32))
    put(dy_im, dy_ref[:, ch:].astype(F32))
    cr = jnp.zeros((1, ch), F32)
    ci = jnp.zeros((1, ch), F32)
    for k in range(1, ranks):
        total, adj = totals[k][...], adjs[k][...]
        nr, ni = cmul(total[0:1], -total[1:2], cr, ci)
        nr, ni = nr + adj[0:1], ni + adj[1:2]
        cr, ci = jnp.where(k > rank, nr, cr), jnp.where(k > rank, ni, ci)
    rows_r, rows_i = [cr], [ci]
    for k in range(CHUNKS - 1, 0, -1):
        cr, ci = cmul(chunk_ref[0, k : k + 1, :], -chunk_ref[1, k : k + 1, :], cr, ci)
        cr, ci = cr + chain_ref[0, k : k + 1, :], ci + chain_ref[1, k : k + 1, :]
        rows_r.append(cr)
        rows_i.append(ci)
    carried = list(
        zip(
            lanes(jnp.concatenate(rows_r[::-1], axis=0), parts),
            lanes(jnp.concatenate(rows_i[::-1], axis=0), parts),
            strict=True,
        )
    )
    for t in range(step - 1, -1, -1):
        rows = pl.ds(t, CHUNKS, stride=step)
        for g in range(parts):
            gr, gi = dy_re[g, rows, :] + carried[g][0], dy_im[g, rows, :] + carried[g][1]
            dy_re[g, rows, :] = gr
            dy_im[g, rows, :] = gi
            carried[g] = cmul(lam_re[g, rows, :], -lam_im[g, rows, :], gr, gi)
    gr, gi = get(dy_re), get(dy_im)
    first = lax.broadcasted_iota(jnp.int32, (span, ch), 0) == 0
    qr = jnp.where(first, start_ref[0:1, :], pltpu.roll(get(hr_ref), 1, 0))
    qi = jnp.where(first, start_ref[1:2, :], pltpu.roll(get(hi_ref), 1, 0))
    pin_re, pin_im = pre[:, :ch], pre[:, ch : 2 * ch]
    sig_re, sig_im = jax.nn.sigmoid(pin_re), jax.nn.sigmoid(pin_im)
    lr = gr * qr + gi * qi
    li = gi * qr - gr * qi
    turned_re = lr * trig[0:1, :] + li * trig[1:2, :]
    turned_im = li * trig[0:1, :] - lr * trig[1:2, :]
    df = turned_re - (gr * pin_re * sig_re + gi * pin_im * sig_im)
    keep = 1.0 - forget
    dre = (keep * gr * silu_slope(pin_re, sig_re)).astype(BF)
    dim = (keep * gi * silu_slope(pin_im, sig_im)).astype(BF)
    dpz = (forget * keep * df).astype(BF)
    dpre_ref[:, : 2 * ch] = dot(jnp.concatenate([dre, dim], axis=1), perm_ref[...], NT).astype(BF)
    dpre_ref[:, 2 * ch :] = dpz
    sums = jnp.concatenate(
        [
            jnp.sum(dpz.astype(F32), axis=0, keepdims=True),
            jnp.sum(forget * turned_im, axis=0, keepdims=True),
        ],
        axis=0,
    )

    @pl.when(pl.program_id(0) == 0)
    def _():
        sums_ref[...] = sums

    @pl.when(pl.program_id(0) > 0)
    def _():
        sums_ref[...] += sums


def grads_kernel(*refs, pairs):
    ins, (send_ref, keep_ref) = refs[: 2 * pairs], refs[2 * pairs :]
    at = 0
    for p in range(pairs):
        lhs_ref, rhs_ref = ins[2 * p], ins[2 * p + 1]
        half, n = lhs_ref.shape[0] // 2, rhs_ref.shape[1]
        send_ref[:, at : at + n] = dot(lhs_ref[:half, :], rhs_ref[...]).astype(BF)
        keep_ref[:, at : at + n] = dot(lhs_ref[half:, :], rhs_ref[...]).astype(BF)
        at += n


def tokens_kernel(
    dpre_ref, dog_ref, w_in_ref, w_forget_ref, w_ogate_ref, x_ref, gain_ref, dmiddle_ref, out_ref, gains_ref
):
    width = x_ref.shape[1]
    up = (
        dot(dpre_ref[:, :width], w_in_ref[...], NT)
        + dot(dpre_ref[:, width:], w_forget_ref[...], NT)
        + dot(dog_ref[...], w_ogate_ref[...], NT)
    )
    x = x_ref[...].astype(F32)
    inv = lax.rsqrt(row_mean(x * x) + epsilon)
    unit = x * inv
    through = up * gain_ref[...][None]
    out_ref[...] = (dmiddle_ref[...] + inv * (through - unit * row_mean(through * unit))).astype(BF)
    gains = jnp.sum(up * unit, axis=0, keepdims=True)

    @pl.when(pl.program_id(0) == 0)
    def _():
        gains_ref[...] = gains

    @pl.when(pl.program_id(0) > 0)
    def _():
        gains_ref[...] += gains


def seg(*shape):
    zeros = (0,) * len(shape)
    return pl.BlockSpec((None,) + shape, lambda s, *_: (s,) + zeros)


def rows(*shape):
    return pl.BlockSpec(shape, lambda s, *_: (s, 0))


def cols(*shape):
    return pl.BlockSpec(shape, lambda s, *_: (0, s))


def whole(*shape):
    zeros = (0,) * len(shape)
    return pl.BlockSpec(shape, lambda s, *_: zeros)


def call(kernel, steps, ins, outs, scratch, scalars, name, after=()):
    first, extra = len(scalars) + len(ins), len(after)

    def body(*refs):
        kernel(*refs[:first], *refs[first + extra :])

    return pl.pallas_call(
        body,
        grid_spec=pltpu.PrefetchScalarGridSpec(
            num_scalar_prefetch=len(scalars),
            grid=(steps,),
            in_specs=[s for s, _ in ins] + [pl.BlockSpec(memory_space=pl.ANY)] * extra,
            out_specs=[s for s, _, _ in outs],
            scratch_shapes=scratch,
        ),
        out_shape=[jax.ShapeDtypeStruct(s, d) for _, s, d in outs],
        compiler_params=pltpu.CompilerParams(vmem_limit_bytes=56 * 1024 * 1024),
        cost_estimate=pl.CostEstimate(flops=1, bytes_accessed=1, transcendentals=0),
        name=name,
    )(*scalars, *[a for _, a in ins], *after)


def shift_all(payload, axis, n):
    return [payload] + [lax.ppermute(payload, axis, [(i, (i + k) % n) for i in range(n)]) for k in range(1, n)]


def own_bit(axis, bit):
    return (lax.axis_index(axis) // bit) % 2


def swap(v, axis, n, bit):
    return lax.ppermute(v, axis, [(i, i ^ bit) for i in range(n)])


def bits_of(n):
    return [1 << i for i in range((n - 1).bit_length())]


def combine_kernel(bits_ref, *refs, layout):
    n_in = sum(2 * addends for lane in layout for addends, _ in lane)
    ins, outs = list(refs[:n_in]), list(refs[n_in:])
    for lane in layout:
        for out in (outs.pop(0), outs.pop(0)):
            at = 0
            for addends, width in lane:
                acc = ins.pop(0)[...].astype(F32)
                for _ in range(addends - 1):
                    acc = acc + ins.pop(0)[...].astype(F32)
                out[:, at : at + width] = acc.astype(out.dtype)
                at += width


def combine(lanes_in, name, after=()):
    scalars = jnp.stack([bit for _, bit, _ in lanes_in]).astype(jnp.int32)
    ins, outs, layout, steps = [], [], [], None
    for n, (pos, _, sources) in enumerate(lanes_in):
        width = sum(src[4] for src in sources)
        addends, mult = sources[0][0], sources[0][1]
        per = addends[0].shape[1]
        count = addends[0].shape[0] // mult // 2
        assert steps in (None, count)
        steps = count
        for flip in (1, 0):
            for addends, mult, off, col, w in sources:
                def index(i, bits, n=n, pos=pos, flip=flip, mult=mult, off=off, col=col):
                    own = bits[n] if not flip else 1 - bits[n]
                    low = i % (1 << pos)
                    return (((i - low) * 2 + own * (1 << pos) + low) * mult + off, 0, col)

                ins += [(pl.BlockSpec((None, per, w), index), a) for a in addends]
        layout.append([(len(src[0]), src[4]) for src in sources])
        outs += [(pl.BlockSpec((None, per, width), lambda i, *_: (i, 0, 0)), (count, per, width), BF)] * 2
    got = call(
        functools.partial(combine_kernel, layout=layout), steps, ins, outs, [], [scalars], name, after
    )
    return [(got[2 * n], got[2 * n + 1]) for n in range(len(lanes_in))]


def add_kernel(*refs):
    n = len(refs) // 3
    for i in range(n):
        refs[2 * n + i][...] = (refs[2 * i][...].astype(F32) + refs[2 * i + 1][...].astype(F32)).astype(BF)


def add_pairs(pairs, name, after=()):
    ins = [(whole(*a.shape), a) for pair in pairs for a in pair]
    outs = [(whole(*p[0].shape), p[0].shape, BF) for p in pairs]
    return call(add_kernel, 1, ins, outs, [], [], name, after)


def finish_kernel(bits_ref, *refs, moves, lanes_n):
    halves, outs = refs[: 2 * lanes_n], refs[2 * lanes_n :]
    for lane, col, width, out, row, at in moves:
        own, other = halves[2 * lane], halves[2 * lane + 1]
        half = own.shape[0]
        for h in range(2):
            pick = bits_ref[lane] == h
            value = jnp.where(pick, own[:, col : col + width].astype(F32), other[:, col : col + width].astype(F32))
            outs[out][row + h * half : row + (h + 1) * half, at : at + width] = value


def finish(halves, bits, moves, shapes, name, after=()):
    ins = [(whole(*a.shape), a) for pair in halves for a in pair]
    outs = [(whole(*s), s, F32) for s in shapes]
    return call(
        functools.partial(finish_kernel, moves=moves, lanes_n=len(halves)), 1, ins, outs, [],
        [jnp.stack(bits).astype(jnp.int32)], name, after,
    )


def total(parts):
    out = parts[0].astype(F32)
    for p in parts[1:]:
        out = out + p.astype(F32)
    return out.astype(BF)


def halve(parts, dim, axis, n, bit):
    mine = own_bit(axis, bit)
    got = swap(total([lax.dynamic_index_in_dim(p, 1 - mine, dim, keepdims=False) for p in parts]), axis, n, bit)
    return [lax.dynamic_index_in_dim(p, mine, dim, keepdims=False) for p in parts] + [got]


def plain_reduce(parts, bits, ndp, nseq):
    left = sorted(bits, reverse=True)
    for b in bits:
        parts = halve(parts, left.index(b), "dp", ndp, b)
        left.remove(b)
    out = total(parts)
    for b in bits_of(nseq):
        out = total([out, swap(out, "seq", nseq, b)])
    return out.astype(F32)


def local(
    ndp, nseq,
    tokens, init_state, norm_mix, w_in, w_forget, forget_bias, phase, w_ogate,
    norm_group, w_out, norm_ffn, w_gate, w_up, w_down, cotangent,
):
    segs, span, width = tokens.shape
    ch = w_forget.shape[1]
    hidden = w_gate.shape[1]
    count = segs * span
    mine = ch // nseq
    per = width // ndp
    tall = hidden // width
    rank = lax.axis_index("seq").astype(jnp.int32)
    bits = bits_of(ndp)
    first = next(b for b in bits if (per * b) % TILE == 0)
    rest = [b for b in bits if b != first]
    bit = own_bit("dp", first).astype(jnp.int32)
    lo = per * first
    scan_scratch = [pltpu.VMEM((ch // LANES, span, LANES), F32)] * 4

    own = jnp.concatenate(
        [jnp.stack([jnp.cos(phase), jnp.sin(phase)])[None], init_state.transpose(0, 2, 1)], axis=0
    )
    place = (jnp.arange(ch) // mine) == rank
    infos = shift_all(jnp.where(place, jnp.concatenate([own] * nseq, axis=2), 0.0), "seq", nseq)

    col = jnp.arange(width)
    perm = (col[:, None] == 2 * (col % ch)[None, :] + (col // ch)[None, :]).astype(BF)
    member = ((col[:, None] // (width // GROUPS)) == jnp.arange(LANES)[None, :]).astype(BF)

    x = tokens.reshape(count, width)
    cot = cotangent.reshape(count, width)
    normed, normed_t, pre = call(
        functools.partial(project_kernel, lo=lo), segs,
        [
            (rows(span, width), x), (whole(width), norm_mix), (whole(width, width), w_in),
            (whole(width, ch), w_forget), (whole(ch), forget_bias), (whole(width, width), perm),
        ],
        [
            (rows(span, width), (count, width), BF),
            (cols(width, span), (width, count), BF),
            (seg(span, 3 * ch), (segs, span, 3 * ch), BF),
        ],
        [], [bit[None]], "project",
    )
    trig, chunk, totals = call(
        functools.partial(summary_kernel, ranks=nseq), segs,
        [(seg(span, 3 * ch), pre)] + [(pl.BlockSpec((None, 2, ch), lambda s, *_: (0, 0, 0)), i) for i in infos],
        [
            (whole(2, ch), (2, ch), F32),
            (seg(4, CHUNKS, ch), (segs, 4, CHUNKS, ch), F32),
            (seg(4, ch), (segs, 4, ch), F32),
        ],
        scan_scratch, [], "summary",
    )
    totals = shift_all(totals, "seq", nseq)
    og = dot(normed, w_ogate)
    y, h_re, h_im, start, final, gated_t, middle = call(
        functools.partial(mixer_kernel, ranks=nseq, lo=lo), segs,
        [(seg(4, ch), t) for t in totals]
        + [(pl.BlockSpec((None, 2, ch), lambda s, *_: (1 + s, 0, 0)), i) for i in infos]
        + [
            (seg(span, 3 * ch), pre), (whole(2, ch), trig), (seg(4, CHUNKS, ch), chunk), (whole(width, width), perm),
            (rows(span, width), x), (rows(span, width), og), (whole(width), norm_group),
            (whole(width, LANES), member), (whole(width, width), w_out),
        ],
        [
            (rows(span, width), (count, width), BF),
            (seg(ch // LANES, span, LANES), (segs, ch // LANES, span, LANES), F32),
            (seg(ch // LANES, span, LANES), (segs, ch // LANES, span, LANES), F32),
            (seg(2, ch), (segs, 2, ch), F32),
            (seg(2, ch), (segs, 2, ch), F32),
            (cols(width, span), (width, count), BF),
            (rows(span, width), (count, width), F32),
        ],
        scan_scratch, [jnp.stack([rank, bit])], "mixer",
    )
    final_state = lax.dynamic_slice_in_dim(final, rank * mine, mine, axis=2).transpose(0, 2, 1)

    tile = width
    gsend, gkeep, dsend, dkeep, mixed_out, dn = call(
        functools.partial(ffn_kernel, lo=lo, dlo=lo * tall, rt=span), hidden // tile,
        [
            (whole(count, width), middle), (whole(width), norm_ffn), (whole(count, width), cot),
            (cols(width, tile), w_gate), (cols(width, tile), w_up), (rows(tile, width), w_down),
        ],
        [
            (cols(width // 2, 2 * tile), (width // 2, 2 * hidden), BF),
            (cols(width // 2, 2 * tile), (width // 2, 2 * hidden), BF),
            (rows(tile // 2, width), (hidden // 2, width), BF),
            (rows(tile // 2, width), (hidden // 2, width), BF),
            (whole(count, width), (count, width), BF),
            (whole(count, width), (count, width), F32),
        ],
        [
            pltpu.VMEM((count, width), BF), pltpu.VMEM((width, count), BF), pltpu.VMEM((count, width), F32),
            pltpu.VMEM((count, tile), BF), pltpu.VMEM((count, tile), BF), pltpu.VMEM((count, tile), BF),
            pltpu.VMEM((tile, count), BF),
        ],
        [bit[None]], "ffn",
    )

    ggot, dgot = swap(gsend, "dp", ndp, first), swap(dsend, "dp", ndp, first)

    dmiddle, dbranch, dog, dy_split, chain, adj, gains = call(
        turn_kernel, segs,
        [
            (rows(span, width), dn), (rows(span, width), middle), (rows(span, width), cot), (whole(width), norm_ffn),
            (whole(width, width), w_out), (rows(span, width), y), (rows(span, width), og), (whole(width), norm_group),
            (whole(width, LANES), member), (whole(width, width), perm), (seg(span, 3 * ch), pre), (whole(2, ch), trig),
            (seg(4, CHUNKS, ch), chunk),
        ],
        [
            (rows(span, width), (count, width), F32),
            (rows(span, width), (count, width), BF),
            (rows(span, width), (count, width), BF),
            (rows(span, width), (count, width), BF),
            (seg(2, CHUNKS, ch), (segs, 2, CHUNKS, ch), F32),
            (seg(2, ch), (segs, 2, ch), F32),
            (whole(2, width), (2, width), F32),
        ],
        scan_scratch, [], "turn",
    )
    adjs = shift_all(adj, "seq", nseq)

    ntile = width // 3
    osend, okeep = call(
        functools.partial(grads_kernel, pairs=2), width // ntile,
        [
            (whole(width, count), normed_t), (cols(count, ntile), dog),
            (whole(width, count), gated_t), (cols(count, ntile), dbranch),
        ],
        [
            (cols(width // 2, 2 * ntile), (width // 2, 2 * width), BF),
            (cols(width // 2, 2 * ntile), (width // 2, 2 * width), BF),
        ],
        [], [], "mixer_grads",
    )
    ogot = swap(osend, "dp", ndp, first)
    nblk = ndp // 2
    fast = ndp == 8 and nseq == 4 and per % (2 * TILE) == 0
    x_bit, y_bit = (own_bit("dp", b) for b in rest[:2]) if fast else (None, None)
    z_bits = [own_bit("seq", b) for b in bits_of(nseq)]

    def blocks(a, cols_n, tall_n=1):
        return a.reshape(nblk * tall_n, per, cols_n)

    order = ()
    if fast:
        g = [blocks(a, 2 * hidden) for a in (gkeep, ggot)]
        d = [blocks(a, width, tall) for a in (dkeep, dgot)]
        fa = [(g, 1, 0, 0, 3 * width)]
        fb = [(g, 1, 0, 3, width)] + [(d, tall, i, 0, width) for i in range(tall)]
        (fa_send, fa_keep), (fb_send, fb_keep) = combine([(0, x_bit, fa), (1, y_bit, fb)], "ffn_sum1", (osend,))
        fa_got, fb_got = swap(fa_send, "dp", ndp, rest[0]), swap(fb_send, "dp", ndp, rest[1])
        order = (fa_keep,)

    dpre, sums = call(
        functools.partial(adjoint_kernel, ranks=nseq), segs,
        [(seg(4, ch), t) for t in totals] + [(seg(2, ch), a) for a in adjs]
        + [
            (seg(span, 3 * ch), pre), (whole(2, ch), trig), (rows(span, width), dy_split),
            (seg(ch // LANES, span, LANES), h_re), (seg(ch // LANES, span, LANES), h_im), (seg(2, ch), start),
            (seg(4, CHUNKS, ch), chunk), (seg(2, CHUNKS, ch), chain), (whole(width, width), perm),
        ],
        [(rows(span, 3 * ch), (count, 3 * ch), BF), (whole(2, ch), (2, ch), F32)],
        scan_scratch, [rank[None]], "adjoint", order,
    )
    isend, ikeep = call(
        functools.partial(grads_kernel, pairs=1), 3,
        [(whole(width, count), normed_t), (cols(count, ch), dpre)],
        [
            (cols(width // 2, ch), (width // 2, 3 * ch), BF),
            (cols(width // 2, ch), (width // 2, 3 * ch), BF),
        ],
        [], [], "input_grads",
    )
    igot = swap(isend, "dp", ndp, first)
    order = ()
    if fast:
        def one(keep, got):
            return [([keep, got], 1, 0, 0, keep.shape[2])]

        def rows_of(keep, got):
            return one(*(a.reshape(2, per // 2, a.shape[2]) for a in (keep, got)))

        (fa_send, fa_keep), (fb_send, fb_keep) = combine(
            [(0, y_bit, one(fa_keep, fa_got)), (0, x_bit, one(fb_keep, fb_got))], "ffn_sum2", (isend,)
        )
        fa_got, fb_got = swap(fa_send, "dp", ndp, rest[1]), swap(fb_send, "dp", ndp, rest[0])
        o = [blocks(a, 2 * width) for a in (okeep, ogot)]
        i = [blocks(a, 3 * ch) for a in (ikeep, igot)]
        (ra_send, ra_keep), (rb_send, rb_keep) = combine(
            [(0, x_bit, [(o, 1, 0, 0, 2 * width)]), (1, y_bit, [(i, 1, 0, 0, 3 * ch)])], "mixer_sum1", (fa_keep,)
        )
        ra_got, rb_got = swap(ra_send, "dp", ndp, rest[0]), swap(rb_send, "dp", ndp, rest[1])
        order = (ra_keep,)

    grad_tokens, gain_mix = call(
        tokens_kernel, segs,
        [
            (rows(span, 3 * ch), dpre), (rows(span, width), dog), (whole(width, width), w_in),
            (whole(width, ch), w_forget), (whole(width, width), w_ogate), (rows(span, width), x),
            (whole(width), norm_mix), (rows(span, width), dmiddle),
        ],
        [(rows(span, width), (count, width), BF), (whole(1, width), (1, width), F32)],
        [], [], "tokens", order,
    )

    vec = jnp.concatenate([gains.reshape(-1), gain_mix.reshape(-1), sums.reshape(-1)]).reshape(-1, LANES)
    for axis, n in (("dp", ndp), ("seq", nseq)):
        for b in bits_of(n):
            vec = vec + swap(vec, axis, n, b)
    vec = vec.reshape(-1)
    place = lax.axis_index("dp") * per

    def own_gain(i):
        return lax.dynamic_slice_in_dim(vec, i * width + place, per)

    def own_sum(i):
        return lax.dynamic_slice_in_dim(vec, 3 * width + i * ch + rank * mine, mine)

    shapes_f = [(per, hidden), (per, hidden), (tall * per, width)]
    shapes_r = [(per, width), (per, width), (per, width), (per, ch)]
    if fast:
        lead, other = bits_of(nseq)

        def over(send, axis_n, bit):
            return swap(send, "seq", axis_n, bit)

        (fa_send, fa_keep), (fb_send, fb_keep) = combine(
            [(0, z_bits[0], rows_of(fa_keep, fa_got)), (0, z_bits[1], rows_of(fb_keep, fb_got))],
            "ffn_sum3", (grad_tokens,),
        )
        fa_got, fb_got = over(fa_send, nseq, lead), over(fb_send, nseq, other)
        (ra_send, ra_keep), (rb_send, rb_keep) = combine(
            [(0, y_bit, one(ra_keep, ra_got)), (0, x_bit, one(rb_keep, rb_got))], "mixer_sum2", (fa_keep,)
        )
        ra_got, rb_got = swap(ra_send, "dp", ndp, rest[1]), swap(rb_send, "dp", ndp, rest[0])
        fa, fb = add_pairs([(fa_keep, fa_got), (fb_keep, fb_got)], "ffn_sum4", (ra_keep,))
        fa_got, fb_got = over(fa, nseq, other), over(fb, nseq, lead)
        (ra_send, ra_keep), (rb_send, rb_keep) = combine(
            [(0, z_bits[0], rows_of(ra_keep, ra_got)), (0, z_bits[1], rows_of(rb_keep, rb_got))], "mixer_sum3", (fa,)
        )
        ra_got, rb_got = over(ra_send, nseq, lead), over(rb_send, nseq, other)
        fa, fb = add_pairs([(fa, fa_got), (fb, fb_got)], "ffn_sum5", (ra_keep,))
        fa_got, fb_got = over(fa, nseq, lead), over(fb, nseq, other)
        ra, rb = add_pairs([(ra_keep, ra_got), (rb_keep, rb_got)], "mixer_sum4", (fa,))
        ra_got, rb_got = over(ra, nseq, other), over(rb, nseq, lead)

        def flat(*pairs):
            return [tuple(a.reshape(per // 2, a.shape[2]) for a in pair) for pair in pairs]

        guv = [(0, c * width) for c in range(3)] + [(1, 0)]
        moves = [
            (lane, col, width, n % 2, 0, (n // 2) * width) for n, (lane, col) in enumerate(guv)
        ] + [(1, (1 + t) * width, width, 2, t * per, 0) for t in range(tall)]
        part_gate, part_up, part_down = finish(
            flat((fa, fa_got), (fb, fb_got)), z_bits, moves, shapes_f, "ffn_out", (ra,)
        )
        ra, rb = add_pairs([(ra, ra_got), (rb, rb_got)], "mixer_sum5", (part_gate,))
        ra_got, rb_got = over(ra, nseq, lead), over(rb, nseq, other)
        moves = [(0, n * ntile, ntile, n % 2, 0, (n // 2) * ntile) for n in range(2 * width // ntile)]
        moves += [(1, 0, width, 2, 0, 0), (1, width, ch, 3, 0, 0)]
        part_ogate, part_out, part_in, part_forget = finish(
            flat((ra, ra_got), (rb, rb_got)), z_bits, moves, shapes_r, "mixer_out"
        )
    else:
        def plain(keep, got, cols_n, tall_n=1):
            shape = [2] * len(rest) + [tall_n * per, cols_n]
            return plain_reduce([keep.reshape(shape), got.reshape(shape)], rest, ndp, nseq)

        guv = plain(gkeep, ggot, 2 * hidden)
        guv = [guv[:, n * tile : (n + 1) * tile] for n in range(2 * hidden // tile)]
        part_gate, part_up = jnp.concatenate(guv[0::2], axis=1), jnp.concatenate(guv[1::2], axis=1)
        part_down = plain(dkeep, dgot, width, tall)
        mix = plain(okeep, ogot, 2 * width)
        mix = [mix[:, n * ntile : (n + 1) * ntile] for n in range(2 * width // ntile)]
        part_ogate, part_out = jnp.concatenate(mix[0::2], axis=1), jnp.concatenate(mix[1::2], axis=1)
        into = plain(ikeep, igot, 3 * ch)
        part_in, part_forget = into[:, :width], into[:, width:]
    return (
        mixed_out.reshape(segs, span, width),
        grad_tokens.reshape(segs, span, width),
        final_state,
        own_gain(2), part_in, part_forget, own_sum(0), own_sum(1), part_ogate, own_gain(1), part_out, own_gain(0),
        part_gate, part_up, part_down,
    )


def solution(mesh):
    ndp, nseq = mesh.shape["dp"], mesh.shape["seq"]
    tok, vec, col = P("dp", "seq", None), P("dp"), P("dp", None)
    return jax.shard_map(
        functools.partial(local, ndp, nseq),
        mesh=mesh,
        in_specs=(tok, tok, P(), P(), P(), P(), P("seq"), P(), P(), P(), P(), P(), P(), P(), tok),
        out_specs=(tok, tok, tok, vec, col, col, P("seq"), P("seq"), col, vec, col, vec, col, col, col),
        check_vma=False,
    )
```

```python
import functools

import jax
import jax.numpy as jnp
from jax import lax
from jax.experimental import pallas as pl
from jax.experimental.pallas import tpu as pltpu
from jax.sharding import PartitionSpec as P

GROUPS = 8
CHUNKS = 8
LANES = 128
RANK, PLACE, FIRST, OTHERS = 0, 1, 2, 3
MICROSECONDS = dict(
    project=3.6, summary=4.8, mixer=10.9, ffn=22.0, turn=12.3, mixer_grads=3.4, adjoint=8.7, input_grads=2.4, tokens=4.5, out=3.5,
    ffn_sum1=3.6, mixer_sum1=3.4,
)
COST = 1.15e9
TILE = 16
epsilon = 1e-06
BF = jnp.bfloat16
F32 = jnp.float32
NT = ((1,), (1,))


def dot(a, b, dims=((1,), (0,))):
    return lax.dot_general(a, b, (dims, ((), ())), preferred_element_type=F32)


def silu_slope(values, logistic):
    return logistic * (1.0 + values * (1.0 - logistic))


def cmul(ar, ai, br, bi):
    return ar * br - ai * bi, ar * bi + ai * br


def row_mean(v):
    return jnp.mean(v, axis=-1, keepdims=True)


def split_dot(v, m, dims):
    high = v.astype(BF)
    low = (v - high.astype(F32)).astype(BF)
    return dot(high, m, dims) + dot(low, m, dims)


def group_mean(v, member):
    return split_dot(v, member, ((1,), (0,))) * (GROUPS / v.shape[1])


def group_spread(v, member):
    return split_dot(v, member, NT)


def put_halves(ref, t, col, lo, bit):
    half = ref.shape[0] // 2
    for b in range(t.shape[0] // lo):
        at = jnp.where(bit == b % 2, half, 0) + (b // 2) * lo
        ref[pl.ds(pl.multiple_of(at, TILE), lo), col : col + t.shape[1]] = t[b * lo : (b + 1) * lo, :]


def put(ref, value):
    for g in range(ref.shape[0]):
        ref[g] = value[:, g * LANES : (g + 1) * LANES]


def get(ref):
    return jnp.concatenate([ref[g] for g in range(ref.shape[0])], axis=1)


def lanes(value, parts):
    return [value[:, g * LANES : (g + 1) * LANES] for g in range(parts)]


def decays(pre, trig, lam_re, lam_im):
    ch = lam_re.shape[0] * LANES
    forget = jax.nn.sigmoid(pre[:, 2 * ch :])
    put(lam_re, forget * trig[0:1, :])
    put(lam_im, forget * trig[1:2, :])
    return forget


def drives(pre, trig, lam_re, lam_im, drv_re, drv_im):
    ch = lam_re.shape[0] * LANES
    forget = decays(pre, trig, lam_re, lam_im)
    put(drv_re, (1.0 - forget) * jax.nn.silu(pre[:, :ch]))
    put(drv_im, (1.0 - forget) * jax.nn.silu(pre[:, ch : 2 * ch]))


def project_kernel(here_ref, x_ref, gain_ref, w_in_ref, w_forget_ref, bias_ref, perm_ref, normed_ref, turned_ref, pre_ref, *, lo):
    width = x_ref.shape[1]
    x = x_ref[...].astype(F32)
    normed = (x * lax.rsqrt(row_mean(x * x) + epsilon) * gain_ref[...][None]).astype(BF)
    normed_ref[...] = normed
    put_halves(turned_ref, normed.T, 0, lo, here_ref[FIRST])
    mixed = dot(normed, w_in_ref[...]).astype(BF)
    pre_ref[:, :width] = dot(mixed, perm_ref[...]).astype(BF)
    pre_ref[:, width:] = (dot(normed, w_forget_ref[...]) + bias_ref[...][None]).astype(BF)


def summary_kernel(*refs, ranks):
    pre_ref, infos = refs[0], refs[1 : 1 + ranks]
    trig_ref, chunk_ref, total_ref, lam_re, lam_im, drv_re, drv_im = refs[1 + ranks :]
    parts, span, _ = lam_re.shape
    step = span // CHUNKS
    trig = infos[0][...]
    for info in infos[1:]:
        trig = trig + info[...]
    trig_ref[...] = trig
    drives(pre_ref[...].astype(F32), trig, lam_re, lam_im, drv_re, drv_im)
    carried = [None] * parts
    for t in range(step):
        rows = pl.ds(t, CHUNKS, stride=step)
        for g in range(parts):
            lr, li = lam_re[g, rows, :], lam_im[g, rows, :]
            br, bi = drv_re[g, rows, :], drv_im[g, rows, :]
            if t == 0:
                carried[g] = (lr, li, br, bi)
            else:
                pr, pi, hr, hi = carried[g]
                pr, pi = cmul(lr, li, pr, pi)
                hr, hi = cmul(lr, li, hr, hi)
                carried[g] = (pr, pi, hr + br, hi + bi)
    pr, pi, hr, hi = (jnp.concatenate([carried[g][q] for g in range(parts)], axis=1) for q in range(4))
    chunk_ref[0], chunk_ref[1], chunk_ref[2], chunk_ref[3] = pr, pi, hr, hi
    tp_r, tp_i, th_r, th_i = pr[0:1], pi[0:1], hr[0:1], hi[0:1]
    for k in range(1, CHUNKS):
        lr, li = pr[k : k + 1], pi[k : k + 1]
        th_r, th_i = cmul(lr, li, th_r, th_i)
        th_r, th_i = th_r + hr[k : k + 1], th_i + hi[k : k + 1]
        tp_r, tp_i = cmul(lr, li, tp_r, tp_i)
    total_ref[...] = jnp.concatenate([tp_r, tp_i, th_r, th_i], axis=0)


def mixer_kernel(*refs, ranks, lo):
    scalars, refs = refs[0], refs[1:]
    totals, inits, refs = refs[:ranks], refs[ranks : 2 * ranks], refs[2 * ranks :]
    pre_ref, trig_ref, chunk_ref, perm_ref, x_ref, og_ref, gain_ref, member_ref, w_out_ref = refs[:9]
    y_ref, split_ref, start_ref, final_ref, turned_ref, middle_ref = refs[9:15]
    lam_re, lam_im, drv_re, drv_im = refs[15:]
    parts, span, _ = lam_re.shape
    ch = parts * LANES
    step = span // CHUNKS
    rank, bit = scalars[RANK], scalars[FIRST]
    drives(pre_ref[...].astype(F32), trig_ref[...], lam_re, lam_im, drv_re, drv_im)
    init = inits[0][...]
    for info in inits[1:]:
        init = init + info[...]
    cr, ci = init[0:1], init[1:2]

    def after(k, cr, ci, take):
        total = totals[k][...]
        nr, ni = cmul(total[0:1], total[1:2], cr, ci)
        nr, ni = nr + total[2:3], ni + total[3:4]
        return jnp.where(take, nr, cr), jnp.where(take, ni, ci)

    for k in range(ranks - 1, 0, -1):
        cr, ci = after(k, cr, ci, k <= rank)
    start_ref[...] = jnp.concatenate([cr, ci], axis=0)
    er, ei = after(0, cr, ci, rank >= 0)
    for k in range(ranks - 1, 0, -1):
        er, ei = after(k, er, ei, k > rank)
    own = ch // ranks
    final_ref[...] = pltpu.roll(jnp.concatenate([er, ei] * 4, axis=0), (ch - own * rank) % ch, 1)[:2, :own]
    rows_r, rows_i = [cr], [ci]
    for k in range(CHUNKS - 1):
        cr, ci = cmul(chunk_ref[0, k : k + 1, :], chunk_ref[1, k : k + 1, :], cr, ci)
        cr, ci = cr + chunk_ref[2, k : k + 1, :], ci + chunk_ref[3, k : k + 1, :]
        rows_r.append(cr)
        rows_i.append(ci)
    carried = list(
        zip(lanes(jnp.concatenate(rows_r, axis=0), parts), lanes(jnp.concatenate(rows_i, axis=0), parts), strict=True)
    )
    for t in range(step):
        rows = pl.ds(t, CHUNKS, stride=step)
        for g in range(parts):
            hr, hi = cmul(lam_re[g, rows, :], lam_im[g, rows, :], *carried[g])
            hr, hi = hr + drv_re[g, rows, :], hi + drv_im[g, rows, :]
            drv_re[g, rows, :] = hr
            drv_im[g, rows, :] = hi
            carried[g] = (hr, hi)
    split = jnp.concatenate([get(drv_re).astype(BF), get(drv_im).astype(BF)], axis=1)
    split_ref[...] = split
    yf = dot(split, perm_ref[...], NT)
    y_ref[...] = yf.astype(BF)
    member = member_ref[...]
    inv = group_spread(lax.rsqrt(group_mean(yf * yf, member) + epsilon), member)
    gated = (yf * inv * gain_ref[...][None] * jax.nn.silu(og_ref[...].astype(F32))).astype(BF)
    put_halves(turned_ref, gated.T, 0, lo, bit)
    middle_ref[...] = x_ref[...].astype(F32) + dot(gated, w_out_ref[...])


def ffn_kernel(
    here_ref, middle_ref, gain_ref, cot_ref, wg_ref, wu_ref, wd_ref,
    gsend_ref, gkeep_ref, dsend_ref, dkeep_ref, hid_ref, dn_ref,
    n_ref, nt_ref, dgv_ref, duv_ref, ht_ref,
    *, lo, dlo, rt,
):
    j = pl.program_id(0)
    bit = here_ref[FIRST]
    count, width = middle_ref.shape
    tile = wg_ref.shape[1]
    spans = [slice(r, r + rt) for r in range(0, count, rt)]

    @pl.when(j == 0)
    def _():
        for rows in spans:
            v = middle_ref[rows, :]
            normed = (v * lax.rsqrt(row_mean(v * v) + epsilon) * gain_ref[...][None]).astype(BF)
            n_ref[rows, :] = normed
            put_halves(nt_ref, normed.T, rows.start, lo, bit)

    for rows in spans:
        g, u = dot(n_ref[rows, :], wg_ref[...]), dot(n_ref[rows, :], wu_ref[...])
        dh = dot(cot_ref[rows, :], wd_ref[...], NT)
        sig = jax.nn.sigmoid(g)
        act = g * sig
        hid_ref[rows, :] = (act * u).astype(BF)
        dgv_ref[rows, :] = (dh * u * silu_slope(g, sig)).astype(BF)
        duv_ref[rows, :] = (dh * act).astype(BF)
    for rows in spans:
        put_halves(ht_ref, hid_ref[rows, :].T, rows.start, dlo, bit)
    for lhs, ref in ((nt_ref[: width // 2, :], gsend_ref), (nt_ref[width // 2 :, :], gkeep_ref)):
        ref[:, :tile] = dot(lhs, dgv_ref[...]).astype(BF)
        ref[:, tile:] = dot(lhs, duv_ref[...]).astype(BF)
    for lhs, ref in ((ht_ref[: tile // 2, :], dsend_ref), (ht_ref[tile // 2 :, :], dkeep_ref)):
        ref[...] = dot(lhs, cot_ref[...]).astype(BF)
    for rows in spans:
        dn = dot(dgv_ref[rows, :], wg_ref[...], NT) + dot(duv_ref[rows, :], wu_ref[...], NT)

        @pl.when(j == 0)
        def _():
            dn_ref[rows, :] = dn

        @pl.when(j > 0)
        def _():
            dn_ref[rows, :] += dn


def turn_kernel(
    dn_ref, middle_ref, cot_ref, ffn_gain_ref, w_out_ref, y_ref, og_ref, gain_ref, member_ref, perm_ref,
    pre_ref, trig_ref, chunk_ref,
    dmiddle_ref, dbranch_ref, dog_ref, split_ref, chain_ref, total_ref, gains_ref,
    lam_re, lam_im, dy_re, dy_im,
):
    parts, span, _ = lam_re.shape
    ch = parts * LANES
    step = span // CHUNKS
    v, up = middle_ref[...], dn_ref[...]
    inv = lax.rsqrt(row_mean(v * v) + epsilon)
    unit = v * inv
    through = up * ffn_gain_ref[...][None]
    dmiddle = cot_ref[...].astype(F32) + inv * (through - unit * row_mean(through * unit))
    gain_ffn = jnp.sum(up * unit, axis=0, keepdims=True)
    dmiddle_ref[...] = dmiddle
    dbranch = dmiddle.astype(BF)
    dbranch_ref[...] = dbranch
    dgated = dot(dbranch, w_out_ref[...], NT)
    og, yf, member, gain = og_ref[...].astype(F32), y_ref[...].astype(F32), member_ref[...], gain_ref[...][None]
    ginv = group_spread(lax.rsqrt(group_mean(yf * yf, member) + epsilon), member)
    gunit = yf * ginv
    sig = jax.nn.sigmoid(og)
    dog_ref[...] = (dgated * gunit * gain * silu_slope(og, sig)).astype(BF)
    dgn = dgated * og * sig
    gains = jnp.concatenate([gain_ffn, jnp.sum(dgn * gunit, axis=0, keepdims=True)], axis=0)

    @pl.when(pl.program_id(0) == 0)
    def _():
        gains_ref[...] = gains

    @pl.when(pl.program_id(0) > 0)
    def _():
        gains_ref[...] += gains

    through = dgn * gain
    dy = (ginv * (through - gunit * group_spread(group_mean(through * gunit, member), member))).astype(BF)
    split = dot(dy, perm_ref[...])
    split_ref[...] = split.astype(BF)
    decays(pre_ref[...].astype(F32), trig_ref[...], lam_re, lam_im)
    put(dy_re, split[:, :ch])
    put(dy_im, split[:, ch:])
    carried = [None] * parts
    for t in range(step - 1, -1, -1):
        rows = pl.ds(t, CHUNKS, stride=step)
        for g in range(parts):
            gr, gi = dy_re[g, rows, :], dy_im[g, rows, :]
            if carried[g] is not None:
                gr, gi = gr + carried[g][0], gi + carried[g][1]
            carried[g] = cmul(lam_re[g, rows, :], -lam_im[g, rows, :], gr, gi)
    ar, ai = (jnp.concatenate([carried[g][q] for g in range(parts)], axis=1) for q in range(2))
    chain_ref[0], chain_ref[1] = ar, ai
    er, ei = ar[CHUNKS - 1 :], ai[CHUNKS - 1 :]
    for k in range(CHUNKS - 2, -1, -1):
        er, ei = cmul(chunk_ref[0, k : k + 1, :], -chunk_ref[1, k : k + 1, :], er, ei)
        er, ei = er + ar[k : k + 1], ei + ai[k : k + 1]
    total_ref[...] = jnp.concatenate([er, ei], axis=0)


def adjoint_kernel(*refs, ranks):
    scalars, refs = refs[0], refs[1:]
    totals, adjs, refs = refs[:ranks], refs[ranks : 2 * ranks], refs[2 * ranks :]
    pre_ref, trig_ref, dy_ref, split_ref, start_ref, chunk_ref, chain_ref, perm_ref = refs[:8]
    dpre_ref, sums_ref, lam_re, lam_im, dy_re, dy_im = refs[8:]
    parts, span, _ = lam_re.shape
    ch = parts * LANES
    step = span // CHUNKS
    rank = scalars[RANK]
    pre = pre_ref[...].astype(F32)
    trig = trig_ref[...]
    forget = decays(pre, trig, lam_re, lam_im)
    put(dy_re, dy_ref[:, :ch].astype(F32))
    put(dy_im, dy_ref[:, ch:].astype(F32))
    cr = jnp.zeros((1, ch), F32)
    ci = jnp.zeros((1, ch), F32)
    for k in range(1, ranks):
        total, adj = totals[k][...], adjs[k][...]
        nr, ni = cmul(total[0:1], -total[1:2], cr, ci)
        nr, ni = nr + adj[0:1], ni + adj[1:2]
        cr, ci = jnp.where(k > rank, nr, cr), jnp.where(k > rank, ni, ci)
    rows_r, rows_i = [cr], [ci]
    for k in range(CHUNKS - 1, 0, -1):
        cr, ci = cmul(chunk_ref[0, k : k + 1, :], -chunk_ref[1, k : k + 1, :], cr, ci)
        cr, ci = cr + chain_ref[0, k : k + 1, :], ci + chain_ref[1, k : k + 1, :]
        rows_r.append(cr)
        rows_i.append(ci)
    carried = list(
        zip(
            lanes(jnp.concatenate(rows_r[::-1], axis=0), parts),
            lanes(jnp.concatenate(rows_i[::-1], axis=0), parts),
            strict=True,
        )
    )
    for t in range(step - 1, -1, -1):
        rows = pl.ds(t, CHUNKS, stride=step)
        for g in range(parts):
            gr, gi = dy_re[g, rows, :] + carried[g][0], dy_im[g, rows, :] + carried[g][1]
            dy_re[g, rows, :] = gr
            dy_im[g, rows, :] = gi
            carried[g] = cmul(lam_re[g, rows, :], -lam_im[g, rows, :], gr, gi)
    gr, gi = get(dy_re), get(dy_im)
    first = lax.broadcasted_iota(jnp.int32, (span, ch), 0) == 0
    qr = jnp.where(first, start_ref[0:1, :], pltpu.roll(split_ref[:, :ch].astype(F32), 1, 0))
    qi = jnp.where(first, start_ref[1:2, :], pltpu.roll(split_ref[:, ch:].astype(F32), 1, 0))
    pin_re, pin_im = pre[:, :ch], pre[:, ch : 2 * ch]
    sig_re, sig_im = jax.nn.sigmoid(pin_re), jax.nn.sigmoid(pin_im)
    lr = gr * qr + gi * qi
    li = gi * qr - gr * qi
    turned_re = lr * trig[0:1, :] + li * trig[1:2, :]
    turned_im = li * trig[0:1, :] - lr * trig[1:2, :]
    df = turned_re - (gr * pin_re * sig_re + gi * pin_im * sig_im)
    keep = 1.0 - forget
    dre = (keep * gr * silu_slope(pin_re, sig_re)).astype(BF)
    dim = (keep * gi * silu_slope(pin_im, sig_im)).astype(BF)
    dpz = (forget * keep * df).astype(BF)
    dpre_ref[:, : 2 * ch] = dot(jnp.concatenate([dre, dim], axis=1), perm_ref[...], NT).astype(BF)
    dpre_ref[:, 2 * ch :] = dpz
    sums = jnp.concatenate(
        [
            jnp.sum(dpz.astype(F32), axis=0, keepdims=True),
            jnp.sum(forget * turned_im, axis=0, keepdims=True),
        ],
        axis=0,
    )

    @pl.when(pl.program_id(0) == 0)
    def _():
        sums_ref[...] = sums

    @pl.when(pl.program_id(0) > 0)
    def _():
        sums_ref[...] += sums


def grads_kernel(*refs, pairs):
    ins, (send_ref, keep_ref) = refs[: 2 * pairs], refs[2 * pairs :]
    at = 0
    for p in range(pairs):
        lhs_ref, rhs_ref = ins[2 * p], ins[2 * p + 1]
        half, n = lhs_ref.shape[0] // 2, rhs_ref.shape[1]
        send_ref[:, at : at + n] = dot(lhs_ref[:half, :], rhs_ref[...]).astype(BF)
        keep_ref[:, at : at + n] = dot(lhs_ref[half:, :], rhs_ref[...]).astype(BF)
        at += n


def out_kernel(middle_ref, hid_ref, w_down_ref, out_ref):
    out_ref[...] = (middle_ref[...] + dot(hid_ref[...], w_down_ref[...])).astype(BF)


def tokens_kernel(
    dpre_ref, dog_ref, w_in_ref, w_forget_ref, w_ogate_ref, x_ref, gain_ref, dmiddle_ref, others_ref, sums_ref,
    out_ref, vectors_ref,
):
    width = x_ref.shape[1]
    up = (
        dot(dpre_ref[:, :width], w_in_ref[...], NT)
        + dot(dpre_ref[:, width:], w_forget_ref[...], NT)
        + dot(dog_ref[...], w_ogate_ref[...], NT)
    )
    x = x_ref[...].astype(F32)
    inv = lax.rsqrt(row_mean(x * x) + epsilon)
    unit = x * inv
    through = up * gain_ref[...][None]
    out_ref[...] = (dmiddle_ref[...] + inv * (through - unit * row_mean(through * unit))).astype(BF)
    gains = jnp.sum(up * unit, axis=0, keepdims=True)

    @pl.when(pl.program_id(0) == 0)
    def _():
        vectors_ref[0:1, :] = gains
        vectors_ref[1:3, :] = others_ref[...]
        vectors_ref[3:4, :] = jnp.concatenate([sums_ref[0:1, :], sums_ref[1:2, :]], axis=1)

    @pl.when(pl.program_id(0) > 0)
    def _():
        vectors_ref[0:1, :] += gains


def vectors_kernel(here_ref, vectors_ref, mix_ref, ffn_ref, group_ref, bias_ref, phase_ref):
    width, ch = vectors_ref.shape[1], vectors_ref.shape[1] // 2
    rows = jnp.concatenate([vectors_ref[...]] * 2, axis=0)
    per, own = mix_ref.shape[1], bias_ref.shape[1]
    gains = pltpu.roll(rows, (width - per * here_ref[PLACE]) % width, 1)
    mix_ref[...], ffn_ref[...], group_ref[...] = gains[0:1, :per], gains[1:2, :per], gains[2:3, :per]
    bias_ref[...] = pltpu.roll(rows[:, :ch], (ch - own * here_ref[RANK]) % ch, 1)[3:4, :own]
    phase_ref[...] = pltpu.roll(rows[:, ch:], (ch - own * here_ref[RANK]) % ch, 1)[3:4, :own]


def rows(*shape):
    return ("rows", shape)


def cols(*shape):
    return ("cols", shape)


def seg(*shape, shift=0, fixed=False):
    return ("seg", shape, shift, fixed)


def whole(*shape):
    return ("whole", shape)


def moved(*shape, dim):
    return ("moved", shape, dim)


def spec_of(kind):
    if kind[0] != "moved":
        return pl.BlockSpec(memory_space=pltpu.VMEM)
    _, shape, dim = kind
    return pl.BlockSpec(shape, lambda s, *_: tuple(s if d == dim else 0 for d in range(len(shape))))


def view_of(kind, ref):
    step = pl.program_id(0)
    if kind[0] == "rows":
        n = kind[1][0]
        return ref.at[pl.ds(pl.multiple_of(step * n, n), n)]
    if kind[0] == "cols":
        n = kind[1][1]
        return ref.at[:, pl.ds(pl.multiple_of(step * n, n), n)]
    if kind[0] == "seg":
        return ref.at[kind[2] if kind[3] else step + kind[2]]
    return ref


def size_of(shape, dtype):
    return functools.reduce(lambda p, q: p * q, shape) * jnp.dtype(dtype).itemsize


def call(kernel, steps, ins, outs, scratch, scalars, name, after=(), room=6):
    cost = int(COST * MICROSECONDS.get(name, 2.0))
    lead, extra = len(scalars), len(after)
    kinds_in, kinds_out = [k for k, _ in ins], [k for k, _, _ in outs]

    def body(*refs):
        given, refs = refs[: lead + len(ins)], refs[lead + len(ins) + extra :]
        kernel(
            *given[:lead],
            *[view_of(k, r) for k, r in zip(kinds_in, given[lead:], strict=True)],
            *[view_of(k, r) for k, r in zip(kinds_out, refs[: len(outs)], strict=True)],
            *refs[len(outs) :],
        )

    limit = room << 20
    limit += sum(2 * size_of(k[1], a.dtype) for k, a in ins if k[0] == "moved")
    limit += sum(2 * size_of(k[1], d) for k, _, d in outs if k[0] == "moved")
    limit += sum(size_of(m.shape, m.dtype) for m in scratch)
    return pl.pallas_call(
        body,
        grid_spec=pltpu.PrefetchScalarGridSpec(
            num_scalar_prefetch=lead,
            grid=(steps,),
            in_specs=[spec_of(k) for k in kinds_in] + [pl.BlockSpec(memory_space=pl.ANY)] * extra,
            out_specs=[spec_of(k) for k in kinds_out],
            scratch_shapes=scratch,
        ),
        out_shape=[jax.ShapeDtypeStruct(s, d) for _, s, d in outs],
        compiler_params=pltpu.CompilerParams(vmem_limit_bytes=limit),
        cost_estimate=pl.CostEstimate(flops=cost, bytes_accessed=1, transcendentals=0),
        name=name,
    )(*scalars, *[a for _, a in ins], *after)


def shift_all(payload, axis, n):
    return [payload] + [lax.ppermute(payload, axis, [(i, (i + k) % n) for i in range(n)]) for k in range(1, n)]


def own_bit(axis, bit):
    return lax.shift_right_logical(lax.axis_index(axis).astype(jnp.int32), jnp.int32(bit.bit_length() - 1)) & 1


def swap(v, axis, n, bit):
    return lax.ppermute(v, axis, [(i, i ^ bit) for i in range(n)])


def bits_of(n):
    return [1 << i for i in range((n - 1).bit_length())]


def combine_kernel(here_ref, *refs, plan, n_in):
    ins, outs = refs[:n_in], refs[n_in:]
    for n, (pos, bit, count, sources) in enumerate(plan):
        for flip in (1, 0):
            own = 1 - here_ref[bit] if flip else here_ref[bit]
            for i in range(count):
                low = i % (1 << pos)
                q = (i - low) * 2 + own * (1 << pos) + low
                at = 0
                for addends, mult, off, col, width in sources:
                    cut = slice(col * width, (col + 1) * width)
                    acc = ins[addends[0]][q * mult + off, :, cut].astype(F32)
                    for k in addends[1:]:
                        acc = acc + ins[k][q * mult + off, :, cut].astype(F32)
                    outs[2 * n + 1 - flip][i, :, at : at + width] = acc.astype(BF)
                    at += width


def combine(here, lanes_in, name, after=()):
    arrays, outs, plan = [], [], []

    def operand(a):
        for k, b in enumerate(arrays):
            if a is b:
                return k
        arrays.append(a)
        return len(arrays) - 1

    for pos, bit, sources in lanes_in:
        addends, mult = sources[0][0], sources[0][1]
        per, count = addends[0].shape[1], addends[0].shape[0] // mult // 2
        plan.append((pos, bit, count, [([operand(a) for a in src[0]], *src[1:]) for src in sources]))
        shape = (count, per, sum(src[4] for src in sources))
        outs += [(whole(*shape), shape, BF)] * 2
    got = call(
        functools.partial(combine_kernel, plan=plan, n_in=len(arrays)), 1, [(whole(), a) for a in arrays], outs, [],
        [here], name, after, 4,
    )
    return [(got[2 * n], got[2 * n + 1]) for n in range(len(lanes_in))]


def add_kernel(*refs):
    n = len(refs) // 3
    for i in range(n):
        refs[2 * n + i][...] = (refs[2 * i][...].astype(F32) + refs[2 * i + 1][...].astype(F32)).astype(BF)


def add_pairs(pairs, name, after=()):
    ins = [(whole(*a.shape), a) for pair in pairs for a in pair]
    outs = [(whole(*p[0].shape), p[0].shape, BF) for p in pairs]
    return call(add_kernel, 1, ins, outs, [], [], name, after)


def finish_kernel(here_ref, *refs, moves, lanes_n, bits):
    halves, outs = refs[: 2 * lanes_n], refs[2 * lanes_n :]
    for lane, col, width, out, row, at in moves:
        own, other = halves[2 * lane], halves[2 * lane + 1]
        half = own.shape[0]
        for h in range(2):
            pick = here_ref[bits[lane]] == h
            value = jnp.where(pick, own[:, col : col + width].astype(F32), other[:, col : col + width].astype(F32))
            outs[out][row + h * half : row + (h + 1) * half, at : at + width] = value


def finish(here, halves, bits, moves, shapes, name, after=()):
    ins = [(whole(*a.shape), a) for pair in halves for a in pair]
    outs = [(whole(*s), s, F32) for s in shapes]
    return call(
        functools.partial(finish_kernel, moves=moves, lanes_n=len(halves), bits=bits), 1, ins, outs, [], [here], name,
        after,
    )


def total(parts):
    out = parts[0].astype(F32)
    for p in parts[1:]:
        out = out + p.astype(F32)
    return out.astype(BF)


def halve(parts, dim, axis, n, bit):
    mine = own_bit(axis, bit)
    got = swap(total([lax.dynamic_index_in_dim(p, 1 - mine, dim, keepdims=False) for p in parts]), axis, n, bit)
    return [lax.dynamic_index_in_dim(p, mine, dim, keepdims=False) for p in parts] + [got]


def plain_reduce(parts, bits, ndp, nseq):
    left = sorted(bits, reverse=True)
    for b in bits:
        parts = halve(parts, left.index(b), "dp", ndp, b)
        left.remove(b)
    out = total(parts)
    for b in bits_of(nseq):
        out = total([out, swap(out, "seq", nseq, b)])
    return out.astype(F32)


def local(
    ndp, nseq,
    tokens, init_state, norm_mix, w_in, w_forget, forget_bias, phase, w_ogate,
    norm_group, w_out, norm_ffn, w_gate, w_up, w_down, cotangent,
):
    segs, span, width = tokens.shape
    ch = w_forget.shape[1]
    hidden = w_gate.shape[1]
    count = segs * span
    mine = ch // nseq
    per = width // ndp
    tall = hidden // width
    rank = lax.axis_index("seq").astype(jnp.int32)
    bits = bits_of(ndp)
    first = next(b for b in bits if (per * b) % TILE == 0)
    rest = [b for b in bits if b != first]
    lo = per * first
    here = [rank, lax.axis_index("dp"), own_bit("dp", first)]
    here += [own_bit("dp", b) for b in rest] + [own_bit("seq", b) for b in bits_of(nseq)]
    here = jnp.stack([h.astype(jnp.int32) for h in here])
    scan_scratch = [pltpu.VMEM((ch // LANES, span, LANES), F32)] * 4

    own = jnp.concatenate(
        [jnp.stack([jnp.cos(phase), jnp.sin(phase)])[None], init_state.transpose(0, 2, 1)], axis=0
    )
    place = (jnp.arange(ch) // mine) == rank
    infos = shift_all(jnp.where(place, jnp.concatenate([own] * nseq, axis=2), 0.0), "seq", nseq)

    col = jnp.arange(width)
    perm = (col[:, None] == 2 * (col % ch)[None, :] + (col // ch)[None, :]).astype(BF)
    member = ((col[:, None] // (width // GROUPS)) == jnp.arange(LANES)[None, :]).astype(BF)

    x = tokens.reshape(count, width)
    cot = cotangent.reshape(count, width)
    normed, normed_t, pre = call(
        functools.partial(project_kernel, lo=lo), segs,
        [
            (rows(span, width), x), (whole(width), norm_mix), (whole(width, width), w_in),
            (whole(width, ch), w_forget), (whole(ch), forget_bias), (whole(width, width), perm),
        ],
        [
            (rows(span, width), (count, width), BF),
            (cols(width, span), (width, count), BF),
            (seg(span, 3 * ch), (segs, span, 3 * ch), BF),
        ],
        [], [here], "project",
    )
    trig, chunk, totals = call(
        functools.partial(summary_kernel, ranks=nseq), segs,
        [(seg(span, 3 * ch), pre)] + [(seg(2, ch, fixed=True), i) for i in infos],
        [
            (whole(2, ch), (2, ch), F32),
            (seg(4, CHUNKS, ch), (segs, 4, CHUNKS, ch), F32),
            (seg(4, ch), (segs, 4, ch), F32),
        ],
        scan_scratch, [], "summary",
    )
    totals = shift_all(totals, "seq", nseq)
    og = dot(normed, w_ogate).astype(BF)
    y, y_split, start, final, gated_t, middle = call(
        functools.partial(mixer_kernel, ranks=nseq, lo=lo), segs,
        [(seg(4, ch), t) for t in totals]
        + [(seg(2, ch, shift=1), i) for i in infos]
        + [
            (seg(span, 3 * ch), pre), (whole(2, ch), trig), (seg(4, CHUNKS, ch), chunk), (whole(width, width), perm),
            (rows(span, width), x), (rows(span, width), og), (whole(width), norm_group),
            (whole(width, LANES), member), (whole(width, width), w_out),
        ],
        [
            (rows(span, width), (count, width), BF),
            (rows(span, width), (count, width), BF),
            (seg(2, ch), (segs, 2, ch), F32),
            (seg(2, mine), (segs, 2, mine), F32),
            (cols(width, span), (width, count), BF),
            (rows(span, width), (count, width), F32),
        ],
        scan_scratch, [here], "mixer",
    )
    final_state = final.transpose(0, 2, 1)

    tile = width
    gsend, gkeep, dsend, dkeep, hid, dn = call(
        functools.partial(ffn_kernel, lo=lo, dlo=lo * tall, rt=span), hidden // tile,
        [
            (whole(count, width), middle), (whole(width), norm_ffn), (whole(count, width), cot),
            (cols(width, tile), w_gate), (cols(width, tile), w_up), (rows(tile, width), w_down),
        ],
        [
            (cols(width // 2, 2 * tile), (width // 2, 2 * hidden), BF),
            (cols(width // 2, 2 * tile), (width // 2, 2 * hidden), BF),
            (rows(tile // 2, width), (hidden // 2, width), BF),
            (rows(tile // 2, width), (hidden // 2, width), BF),
            (cols(count, tile), (count, hidden), BF),
            (whole(count, width), (count, width), F32),
        ],
        [
            pltpu.VMEM((count, width), BF), pltpu.VMEM((width, count), BF),
            pltpu.VMEM((count, tile), BF), pltpu.VMEM((count, tile), BF),
            pltpu.VMEM((tile, count), BF),
        ],
        [here], "ffn",
    )

    ggot, dgot = swap(gsend, "dp", ndp, first), swap(dsend, "dp", ndp, first)

    dmiddle, dbranch, dog, dy_split, chain, adj, gains = call(
        turn_kernel, segs,
        [
            (rows(span, width), dn), (rows(span, width), middle), (rows(span, width), cot), (whole(width), norm_ffn),
            (whole(width, width), w_out), (rows(span, width), y), (rows(span, width), og), (whole(width), norm_group),
            (whole(width, LANES), member), (whole(width, width), perm), (seg(span, 3 * ch), pre), (whole(2, ch), trig),
            (seg(4, CHUNKS, ch), chunk),
        ],
        [
            (rows(span, width), (count, width), F32),
            (rows(span, width), (count, width), BF),
            (rows(span, width), (count, width), BF),
            (rows(span, width), (count, width), BF),
            (seg(2, CHUNKS, ch), (segs, 2, CHUNKS, ch), F32),
            (seg(2, ch), (segs, 2, ch), F32),
            (whole(2, width), (2, width), F32),
        ],
        scan_scratch, [], "turn",
    )
    adjs = shift_all(adj, "seq", nseq)

    ntile = width // 3
    osend, okeep = call(
        functools.partial(grads_kernel, pairs=2), width // ntile,
        [
            (whole(width, count), normed_t), (cols(count, ntile), dog),
            (whole(width, count), gated_t), (cols(count, ntile), dbranch),
        ],
        [
            (cols(width // 2, 2 * ntile), (width // 2, 2 * width), BF),
            (cols(width // 2, 2 * ntile), (width // 2, 2 * width), BF),
        ],
        [], [], "mixer_grads",
    )
    ogot = swap(osend, "dp", ndp, first)
    nblk = ndp // 2
    fast = ndp == 8 and nseq == 4 and per % (2 * TILE) == 0
    x_bit, y_bit = OTHERS, OTHERS + 1
    z_bits = [OTHERS + len(rest) + i for i in range(len(bits_of(nseq)))]

    def blocks(a, cols_n, tall_n=1):
        return a.reshape(nblk * tall_n, per, cols_n)

    order = ()
    if fast:
        g = [blocks(a, 2 * hidden) for a in (gkeep, ggot)]
        d = [blocks(a, width, tall) for a in (dkeep, dgot)]
        fa = [(g, 1, 0, 0, 3 * width)]
        fb = [(g, 1, 0, 3, width)] + [(d, tall, i, 0, width) for i in range(tall)]
        (fa_send, fa_keep), (fb_send, fb_keep) = combine(here, [(0, x_bit, fa), (1, y_bit, fb)], "ffn_sum1", (osend,))
        fa_got, fb_got = swap(fa_send, "dp", ndp, rest[0]), swap(fb_send, "dp", ndp, rest[1])
        order = (fa_keep,)

    dpre, sums = call(
        functools.partial(adjoint_kernel, ranks=nseq), segs,
        [(seg(4, ch), t) for t in totals] + [(seg(2, ch), a) for a in adjs]
        + [
            (seg(span, 3 * ch), pre), (whole(2, ch), trig), (rows(span, width), dy_split),
            (rows(span, width), y_split), (seg(2, ch), start),
            (seg(4, CHUNKS, ch), chunk), (seg(2, CHUNKS, ch), chain), (whole(width, width), perm),
        ],
        [(rows(span, 3 * ch), (count, 3 * ch), BF), (whole(2, ch), (2, ch), F32)],
        scan_scratch, [here], "adjoint", order,
    )
    isend, ikeep = call(
        functools.partial(grads_kernel, pairs=1), 3,
        [(whole(width, count), normed_t), (cols(count, ch), dpre)],
        [
            (cols(width // 2, ch), (width // 2, 3 * ch), BF),
            (cols(width // 2, ch), (width // 2, 3 * ch), BF),
        ],
        [], [], "input_grads",
    )
    igot = swap(isend, "dp", ndp, first)
    order = ()
    if fast:
        def one(keep, got):
            return [([keep, got], 1, 0, 0, keep.shape[2])]

        def rows_of(keep, got):
            return one(*(a.reshape(2, per // 2, a.shape[2]) for a in (keep, got)))

        (fa_send, fa_keep), (fb_send, fb_keep) = combine(
            here, [(0, y_bit, one(fa_keep, fa_got)), (0, x_bit, one(fb_keep, fb_got))], "ffn_sum2", (isend,)
        )
        fa_got, fb_got = swap(fa_send, "dp", ndp, rest[1]), swap(fb_send, "dp", ndp, rest[0])
        o = [blocks(a, 2 * width) for a in (okeep, ogot)]
        i = [blocks(a, 3 * ch) for a in (ikeep, igot)]
        (ra_send, ra_keep), (rb_send, rb_keep) = combine(
            here, [(0, x_bit, [(o, 1, 0, 0, 2 * width)]), (1, y_bit, [(i, 1, 0, 0, 3 * ch)])], "mixer_sum1", (fa_keep,)
        )
        ra_got, rb_got = swap(ra_send, "dp", ndp, rest[0]), swap(rb_send, "dp", ndp, rest[1])
        order = (ra_keep,)

    grad_tokens, vectors = call(
        tokens_kernel, segs,
        [
            (rows(span, 3 * ch), dpre), (rows(span, width), dog), (whole(width, width), w_in),
            (whole(width, ch), w_forget), (whole(width, width), w_ogate), (rows(span, width), x),
            (whole(width), norm_mix), (rows(span, width), dmiddle), (whole(2, width), gains), (whole(2, ch), sums),
        ],
        [(moved(span, width, dim=0), (count, width), BF), (whole(4, width), (4, width), F32)],
        [], [], "tokens", order,
    )

    (mixed_out,) = call(
        out_kernel, segs, [(rows(span, width), middle), (rows(span, hidden), hid), (whole(hidden, width), w_down)],
        [(moved(span, width, dim=0), (count, width), BF)], [], [], "out", (grad_tokens,),
    )

    for axis, n in (("dp", ndp), ("seq", nseq)):
        for b in bits_of(n):
            vectors = vectors + swap(vectors, axis, n, b)
    part_mix, part_ffn, part_group, part_bias, part_phase = call(
        vectors_kernel, 1, [(whole(4, width), vectors)],
        [(whole(1, per), (1, per), F32)] * 3 + [(whole(1, mine), (1, mine), F32)] * 2, [], [here], "vectors",
    )

    shapes_f = [(per, hidden), (per, hidden), (tall * per, width)]
    shapes_r = [(per, width), (per, width), (per, width), (per, ch)]
    if fast:
        lead, other = bits_of(nseq)

        def over(send, axis_n, bit):
            return swap(send, "seq", axis_n, bit)

        (fa_send, fa_keep), (fb_send, fb_keep) = combine(
            here, [(0, z_bits[0], rows_of(fa_keep, fa_got)), (0, z_bits[1], rows_of(fb_keep, fb_got))],
            "ffn_sum3", (mixed_out,),
        )
        fa_got, fb_got = over(fa_send, nseq, lead), over(fb_send, nseq, other)
        (ra_send, ra_keep), (rb_send, rb_keep) = combine(
            here, [(0, y_bit, one(ra_keep, ra_got)), (0, x_bit, one(rb_keep, rb_got))], "mixer_sum2", (fa_keep,)
        )
        ra_got, rb_got = swap(ra_send, "dp", ndp, rest[1]), swap(rb_send, "dp", ndp, rest[0])
        fa, fb = add_pairs([(fa_keep, fa_got), (fb_keep, fb_got)], "ffn_sum4", (ra_keep,))
        fa_got, fb_got = over(fa, nseq, other), over(fb, nseq, lead)
        (ra_send, ra_keep), (rb_send, rb_keep) = combine(
            here, [(0, z_bits[0], rows_of(ra_keep, ra_got)), (0, z_bits[1], rows_of(rb_keep, rb_got))], "mixer_sum3", (fa,)
        )
        ra_got, rb_got = over(ra_send, nseq, lead), over(rb_send, nseq, other)
        fa, fb = add_pairs([(fa, fa_got), (fb, fb_got)], "ffn_sum5", (ra_keep,))
        fa_got, fb_got = over(fa, nseq, lead), over(fb, nseq, other)
        ra, rb = add_pairs([(ra_keep, ra_got), (rb_keep, rb_got)], "mixer_sum4", (fa,))
        ra_got, rb_got = over(ra, nseq, other), over(rb, nseq, lead)

        def flat(*pairs):
            return [tuple(a.reshape(per // 2, a.shape[2]) for a in pair) for pair in pairs]

        guv = [(0, c * width) for c in range(3)] + [(1, 0)]
        moves = [
            (lane, col, width, n % 2, 0, (n // 2) * width) for n, (lane, col) in enumerate(guv)
        ] + [(1, (1 + t) * width, width, 2, t * per, 0) for t in range(tall)]
        part_gate, part_up, part_down = finish(
            here, flat((fa, fa_got), (fb, fb_got)), z_bits, moves, shapes_f, "ffn_out", (ra,)
        )
        ra, rb = add_pairs([(ra, ra_got), (rb, rb_got)], "mixer_sum5", (part_gate,))
        ra_got, rb_got = over(ra, nseq, lead), over(rb, nseq, other)
        moves = [(0, n * ntile, ntile, n % 2, 0, (n // 2) * ntile) for n in range(2 * width // ntile)]
        moves += [(1, 0, width, 2, 0, 0), (1, width, ch, 3, 0, 0)]
        part_ogate, part_out, part_in, part_forget = finish(
            here, flat((ra, ra_got), (rb, rb_got)), z_bits, moves, shapes_r, "mixer_out"
        )
    else:
        def plain(keep, got, cols_n, tall_n=1):
            shape = [2] * len(rest) + [tall_n * per, cols_n]
            return plain_reduce([keep.reshape(shape), got.reshape(shape)], rest, ndp, nseq)

        guv = plain(gkeep, ggot, 2 * hidden)
        guv = [guv[:, n * tile : (n + 1) * tile] for n in range(2 * hidden // tile)]
        part_gate, part_up = jnp.concatenate(guv[0::2], axis=1), jnp.concatenate(guv[1::2], axis=1)
        part_down = plain(dkeep, dgot, width, tall)
        mix = plain(okeep, ogot, 2 * width)
        mix = [mix[:, n * ntile : (n + 1) * ntile] for n in range(2 * width // ntile)]
        part_ogate, part_out = jnp.concatenate(mix[0::2], axis=1), jnp.concatenate(mix[1::2], axis=1)
        into = plain(ikeep, igot, 3 * ch)
        part_in, part_forget = into[:, :width], into[:, width:]
    return (
        mixed_out.reshape(segs, span, width),
        grad_tokens.reshape(segs, span, width),
        final_state,
        part_mix[0], part_in, part_forget, part_bias[0], part_phase[0], part_ogate, part_group[0], part_out, part_ffn[0],
        part_gate, part_up, part_down,
    )


def solution(mesh):
    ndp, nseq = mesh.shape["dp"], mesh.shape["seq"]
    tok, vec, col = P("dp", "seq", None), P("dp"), P("dp", None)
    return jax.shard_map(
        functools.partial(local, ndp, nseq),
        mesh=mesh,
        in_specs=(tok, tok, P(), P(), P(), P(), P("seq"), P(), P(), P(), P(), P(), P(), P(), tok),
        out_specs=(tok, tok, tok, vec, col, col, P("seq"), P("seq"), col, vec, col, vec, col, col, col),
        check_vma=False,
    )
```

```python
import functools

import jax
import jax.numpy as jnp
from jax import lax
from jax.experimental import pallas as pl
from jax.experimental.pallas import tpu as pltpu
from jax.sharding import PartitionSpec as P

GROUPS = 8
CHUNKS = 8
LANES = 128
RANK, PLACE = 0, 1
MICROSECONDS = dict(
    project=4, summary=4, hidden_grad=2.5, mixer=8, ffn=18, turn=7, chains=3.5, mixer_grads=1, adjoint=1, input_grads=1, tokens=4.5, out=3.5,
    ffn_sum1=1.3, mixer_sum1=1.0, ffn_sum2=5,
)
COST = 1.15e9
TILE = 16
epsilon = 1e-06
BF = jnp.bfloat16
F32 = jnp.float32
NT = ((1,), (1,))


def dot(a, b, dims=((1,), (0,))):
    return lax.dot_general(a, b, (dims, ((), ())), preferred_element_type=F32)


def silu_slope(values, logistic):
    return logistic * (1.0 + values * (1.0 - logistic))


def cmul(ar, ai, br, bi):
    return ar * br - ai * bi, ar * bi + ai * br


def row_mean(v):
    return jnp.mean(v, axis=-1, keepdims=True)


def split_dot(v, m, dims):
    high = v.astype(BF)
    low = (v - high.astype(F32)).astype(BF)
    return dot(high, m, dims) + dot(low, m, dims)


def group_mean(v, member):
    return split_dot(v, member, ((1,), (0,))) * (GROUPS / v.shape[1])


def group_spread(v, member):
    return split_dot(v, member, NT)


def bit_of(here_ref, which, bit):
    return lax.shift_right_logical(here_ref[which], bit.bit_length() - 1) & 1


def put_halves(ref, t, col, lo, bit):
    half = ref.shape[0] // 2
    for b in range(t.shape[0] // lo):
        at = jnp.where(bit == b % 2, half, 0) + (b // 2) * lo
        ref[pl.ds(pl.multiple_of(at, TILE), lo), col : col + t.shape[1]] = t[b * lo : (b + 1) * lo, :]


def put(ref, value):
    for g in range(ref.shape[0]):
        ref[g] = value[:, g * LANES : (g + 1) * LANES]


def get(ref):
    return jnp.concatenate([ref[g] for g in range(ref.shape[0])], axis=1)


def lanes(value, parts):
    return [value[:, g * LANES : (g + 1) * LANES] for g in range(parts)]


def project_kernel(
    here_ref, x_ref, gain_ref, w_in_ref, w_forget_ref, bias_ref, perm_ref, normed_ref, turned_ref, pre_ref, *, lo, first
):
    width = x_ref.shape[1]
    x = x_ref[...].astype(F32)
    normed = (x * lax.rsqrt(row_mean(x * x) + epsilon) * gain_ref[...][None]).astype(BF)
    normed_ref[...] = normed
    put_halves(turned_ref, normed.T, 0, lo, bit_of(here_ref, PLACE, first))
    mixed = dot(normed, w_in_ref[...]).astype(BF)
    pre_ref[:, :width] = dot(mixed, perm_ref[...]).astype(BF)
    pre_ref[:, width:] = (dot(normed, w_forget_ref[...]) + bias_ref[...][None]).astype(BF)


def summary_kernel(*refs, ranks):
    pre_ref, infos = refs[0], refs[1 : 1 + ranks]
    trig_ref, chunk_ref, total_ref, lam_re, lam_im, drv_re, drv_im = refs[1 + ranks :]
    parts, span, _ = lam_re.shape
    step = span // CHUNKS
    trig = infos[0][...]
    for info in infos[1:]:
        trig = trig + info[...]
    trig_ref[...] = trig
    ch = parts * LANES
    pre = pre_ref[...].astype(F32)
    forget = jax.nn.sigmoid(pre[:, 2 * ch :])
    put(lam_re, forget * trig[0:1, :])
    put(lam_im, forget * trig[1:2, :])
    put(drv_re, (1.0 - forget) * jax.nn.silu(pre[:, :ch]))
    put(drv_im, (1.0 - forget) * jax.nn.silu(pre[:, ch : 2 * ch]))
    carried = [None] * parts
    for t in range(step):
        rows = pl.ds(t, CHUNKS, stride=step)
        for g in range(parts):
            lr, li = lam_re[g, rows, :], lam_im[g, rows, :]
            br, bi = drv_re[g, rows, :], drv_im[g, rows, :]
            if t == 0:
                carried[g] = (lr, li, br, bi)
            else:
                pr, pi, hr, hi = carried[g]
                pr, pi = cmul(lr, li, pr, pi)
                hr, hi = cmul(lr, li, hr, hi)
                carried[g] = (pr, pi, hr + br, hi + bi)
    pr, pi, hr, hi = (jnp.concatenate([carried[g][q] for g in range(parts)], axis=1) for q in range(4))
    chunk_ref[0], chunk_ref[1], chunk_ref[2], chunk_ref[3] = pr, pi, hr, hi
    tp_r, tp_i, th_r, th_i = pr[0:1], pi[0:1], hr[0:1], hi[0:1]
    for k in range(1, CHUNKS):
        lr, li = pr[k : k + 1], pi[k : k + 1]
        th_r, th_i = cmul(lr, li, th_r, th_i)
        th_r, th_i = th_r + hr[k : k + 1], th_i + hi[k : k + 1]
        tp_r, tp_i = cmul(lr, li, tp_r, tp_i)
    total_ref[...] = jnp.concatenate([tp_r, tp_i, th_r, th_i], axis=0)


def mixer_kernel(*refs, ranks, lo, first):
    scalars, refs = refs[0], refs[1:]
    totals, inits, refs = refs[:ranks], refs[ranks : 2 * ranks], refs[2 * ranks :]
    lam_re, lam_im, drv_re, drv_im, chunk_ref, perm_ref, x_ref, og_ref, gain_ref, member_ref, w_out_ref = refs[:11]
    y_ref, split_ref, start_ref, final_ref, turned_ref, middle_ref, st_re, st_im = refs[11:]
    parts, span, _ = lam_re.shape
    ch = parts * LANES
    step = span // CHUNKS
    rank, bit = scalars[RANK], bit_of(scalars, PLACE, first)
    init = inits[0][...]
    for info in inits[1:]:
        init = init + info[...]
    cr, ci = init[0:1], init[1:2]

    def after(k, cr, ci, take):
        total = totals[k][...]
        nr, ni = cmul(total[0:1], total[1:2], cr, ci)
        nr, ni = nr + total[2:3], ni + total[3:4]
        return jnp.where(take, nr, cr), jnp.where(take, ni, ci)

    for k in range(ranks - 1, 0, -1):
        cr, ci = after(k, cr, ci, k <= rank)
    start_ref[...] = jnp.concatenate([cr, ci], axis=0)
    er, ei = after(0, cr, ci, rank >= 0)
    for k in range(ranks - 1, 0, -1):
        er, ei = after(k, er, ei, k > rank)
    own = ch // ranks
    final_ref[...] = pltpu.roll(jnp.concatenate([er, ei] * 4, axis=0), (ch - own * rank) % ch, 1)[:2, :own]
    rows_r, rows_i = [cr], [ci]
    for k in range(CHUNKS - 1):
        cr, ci = cmul(chunk_ref[0, k : k + 1, :], chunk_ref[1, k : k + 1, :], cr, ci)
        cr, ci = cr + chunk_ref[2, k : k + 1, :], ci + chunk_ref[3, k : k + 1, :]
        rows_r.append(cr)
        rows_i.append(ci)
    carried = list(
        zip(lanes(jnp.concatenate(rows_r, axis=0), parts), lanes(jnp.concatenate(rows_i, axis=0), parts), strict=True)
    )
    for t in range(step):
        rows = pl.ds(t, CHUNKS, stride=step)
        for g in range(parts):
            hr, hi = cmul(lam_re[g, rows, :], lam_im[g, rows, :], *carried[g])
            hr, hi = hr + drv_re[g, rows, :], hi + drv_im[g, rows, :]
            st_re[g, rows, :] = hr
            st_im[g, rows, :] = hi
            carried[g] = (hr, hi)
    split = jnp.concatenate([get(st_re).astype(BF), get(st_im).astype(BF)], axis=1)
    split_ref[...] = split
    yf = dot(split, perm_ref[...], NT)
    y_ref[...] = yf.astype(BF)
    member = member_ref[...]
    inv = group_spread(lax.rsqrt(group_mean(yf * yf, member) + epsilon), member)
    gated = (yf * inv * gain_ref[...][None] * jax.nn.silu(og_ref[...].astype(F32))).astype(BF)
    put_halves(turned_ref, gated.T, 0, lo, bit)
    middle_ref[...] = x_ref[...].astype(F32) + dot(gated, w_out_ref[...])


def ffn_kernel(
    here_ref, middle_ref, gain_ref, cot_ref, wg_ref, wu_ref, dh_ref,
    gsend_ref, gkeep_ref, dsend_ref, dkeep_ref, hid_ref, dn_ref,
    n_ref, nt_ref, dgv_ref, duv_ref, ht_ref,
    *, lo, dlo, rt, first,
):
    j = pl.program_id(0)
    bit = bit_of(here_ref, PLACE, first)
    count, width = middle_ref.shape
    tile = wg_ref.shape[1]
    spans = [slice(r, r + rt) for r in range(0, count, rt)]

    @pl.when(j == 0)
    def _():
        for rows in spans:
            v = middle_ref[rows, :]
            normed = (v * lax.rsqrt(row_mean(v * v) + epsilon) * gain_ref[...][None]).astype(BF)
            n_ref[rows, :] = normed
            put_halves(nt_ref, normed.T, rows.start, lo, bit)

    for rows in spans:
        g, u = dot(n_ref[rows, :], wg_ref[...]), dot(n_ref[rows, :], wu_ref[...])
        dh = dh_ref[rows, :].astype(F32)
        sig = jax.nn.sigmoid(g)
        act = g * sig
        hid_ref[rows, :] = (act * u).astype(BF)
        dgv_ref[rows, :] = (dh * u * silu_slope(g, sig)).astype(BF)
        duv_ref[rows, :] = (dh * act).astype(BF)
    for rows in spans:
        put_halves(ht_ref, hid_ref[rows, :].T, rows.start, dlo, bit)
    for lhs, ref in ((nt_ref[: width // 2, :], gsend_ref), (nt_ref[width // 2 :, :], gkeep_ref)):
        ref[:, :tile] = dot(lhs, dgv_ref[...]).astype(BF)
        ref[:, tile:] = dot(lhs, duv_ref[...]).astype(BF)
    for lhs, ref in ((ht_ref[: tile // 2, :], dsend_ref), (ht_ref[tile // 2 :, :], dkeep_ref)):
        ref[...] = dot(lhs, cot_ref[...]).astype(BF)
    for rows in spans:
        dn = dot(dgv_ref[rows, :], wg_ref[...], NT) + dot(duv_ref[rows, :], wu_ref[...], NT)

        @pl.when(j == 0)
        def _():
            dn_ref[rows, :] = dn

        @pl.when(j > 0)
        def _():
            dn_ref[rows, :] += dn


def gate_kernel(normed_ref, w_ref, og_ref):
    og_ref[...] = dot(normed_ref[...], w_ref[...]).astype(BF)


def hidden_grad_kernel(cot_ref, wd_ref, dh_ref):
    dh_ref[...] = dot(cot_ref[...], wd_ref[...], NT).astype(BF)


def turn_kernel(
    dn_ref, middle_ref, cot_ref, ffn_gain_ref, w_out_ref, y_ref, og_ref, gain_ref, member_ref, perm_ref,
    dmiddle_ref, dbranch_ref, dog_ref, split_ref,
):
    v, up = middle_ref[...], dn_ref[...]
    inv = lax.rsqrt(row_mean(v * v) + epsilon)
    unit = v * inv
    through = up * ffn_gain_ref[...][None]
    dmiddle = cot_ref[...].astype(F32) + inv * (through - unit * row_mean(through * unit))
    dmiddle_ref[...] = dmiddle
    dbranch = dmiddle.astype(BF)
    dbranch_ref[...] = dbranch
    dgated = dot(dbranch, w_out_ref[...], NT)
    og, yf, member, gain = og_ref[...].astype(F32), y_ref[...].astype(F32), member_ref[...], gain_ref[...][None]
    ginv = group_spread(lax.rsqrt(group_mean(yf * yf, member) + epsilon), member)
    gunit = yf * ginv
    sig = jax.nn.sigmoid(og)
    dog_ref[...] = (dgated * gunit * gain * silu_slope(og, sig)).astype(BF)
    through = dgated * og * sig * gain
    dy = (ginv * (through - gunit * group_spread(group_mean(through * gunit, member), member))).astype(BF)
    split_ref[...] = dot(dy, perm_ref[...]).astype(BF)


def chains_kernel(split_ref, lam_re, lam_im, chunk_ref, chain_ref, total_ref, dy_re, dy_im):
    parts, span, _ = lam_re.shape
    ch = parts * LANES
    step = span // CHUNKS
    put(dy_re, split_ref[:, :ch].astype(F32))
    put(dy_im, split_ref[:, ch:].astype(F32))
    carried = [None] * parts
    for t in range(step - 1, -1, -1):
        rows = pl.ds(t, CHUNKS, stride=step)
        for g in range(parts):
            gr, gi = dy_re[g, rows, :], dy_im[g, rows, :]
            if carried[g] is not None:
                gr, gi = gr + carried[g][0], gi + carried[g][1]
            carried[g] = cmul(lam_re[g, rows, :], -lam_im[g, rows, :], gr, gi)
    ar, ai = (jnp.concatenate([carried[g][q] for g in range(parts)], axis=1) for q in range(2))
    chain_ref[0], chain_ref[1] = ar, ai
    er, ei = ar[CHUNKS - 1 :], ai[CHUNKS - 1 :]
    for k in range(CHUNKS - 2, -1, -1):
        er, ei = cmul(chunk_ref[0, k : k + 1, :], -chunk_ref[1, k : k + 1, :], er, ei)
        er, ei = er + ar[k : k + 1], ei + ai[k : k + 1]
    total_ref[...] = jnp.concatenate([er, ei], axis=0)


def adjoint_kernel(*refs, ranks):
    scalars, refs = refs[0], refs[1:]
    totals, adjs, refs = refs[:ranks], refs[ranks : 2 * ranks], refs[2 * ranks :]
    pre_ref, trig_ref, lam_re, lam_im, dy_ref, split_ref, start_ref, chunk_ref, chain_ref, perm_ref = refs[:10]
    dpre_ref, sums_ref, dy_re, dy_im = refs[10:]
    parts, span, _ = lam_re.shape
    ch = parts * LANES
    step = span // CHUNKS
    rank = scalars[RANK]
    pre = pre_ref[...].astype(F32)
    trig = trig_ref[...]
    forget = jax.nn.sigmoid(pre[:, 2 * ch :])
    put(dy_re, dy_ref[:, :ch].astype(F32))
    put(dy_im, dy_ref[:, ch:].astype(F32))
    cr = jnp.zeros((1, ch), F32)
    ci = jnp.zeros((1, ch), F32)
    for k in range(1, ranks):
        total, adj = totals[k][...], adjs[k][...]
        nr, ni = cmul(total[0:1], -total[1:2], cr, ci)
        nr, ni = nr + adj[0:1], ni + adj[1:2]
        cr, ci = jnp.where(k > rank, nr, cr), jnp.where(k > rank, ni, ci)
    rows_r, rows_i = [cr], [ci]
    for k in range(CHUNKS - 1, 0, -1):
        cr, ci = cmul(chunk_ref[0, k : k + 1, :], -chunk_ref[1, k : k + 1, :], cr, ci)
        cr, ci = cr + chain_ref[0, k : k + 1, :], ci + chain_ref[1, k : k + 1, :]
        rows_r.append(cr)
        rows_i.append(ci)
    carried = list(
        zip(
            lanes(jnp.concatenate(rows_r[::-1], axis=0), parts),
            lanes(jnp.concatenate(rows_i[::-1], axis=0), parts),
            strict=True,
        )
    )
    for t in range(step - 1, -1, -1):
        rows = pl.ds(t, CHUNKS, stride=step)
        for g in range(parts):
            gr, gi = dy_re[g, rows, :] + carried[g][0], dy_im[g, rows, :] + carried[g][1]
            dy_re[g, rows, :] = gr
            dy_im[g, rows, :] = gi
            carried[g] = cmul(lam_re[g, rows, :], -lam_im[g, rows, :], gr, gi)
    gr, gi = get(dy_re), get(dy_im)
    first = lax.broadcasted_iota(jnp.int32, (span, ch), 0) == 0
    qr = jnp.where(first, start_ref[0:1, :], pltpu.roll(split_ref[:, :ch].astype(F32), 1, 0))
    qi = jnp.where(first, start_ref[1:2, :], pltpu.roll(split_ref[:, ch:].astype(F32), 1, 0))
    pin_re, pin_im = pre[:, :ch], pre[:, ch : 2 * ch]
    sig_re, sig_im = jax.nn.sigmoid(pin_re), jax.nn.sigmoid(pin_im)
    lr = gr * qr + gi * qi
    li = gi * qr - gr * qi
    turned_re = lr * trig[0:1, :] + li * trig[1:2, :]
    turned_im = li * trig[0:1, :] - lr * trig[1:2, :]
    df = turned_re - (gr * pin_re * sig_re + gi * pin_im * sig_im)
    keep = 1.0 - forget
    dre = (keep * gr * silu_slope(pin_re, sig_re)).astype(BF)
    dim = (keep * gi * silu_slope(pin_im, sig_im)).astype(BF)
    dpz = (forget * keep * df).astype(BF)
    dpre_ref[:, : 2 * ch] = dot(jnp.concatenate([dre, dim], axis=1), perm_ref[...], NT).astype(BF)
    dpre_ref[:, 2 * ch :] = dpz
    sums = jnp.concatenate(
        [
            jnp.sum(dpz.astype(F32), axis=0, keepdims=True),
            jnp.sum(forget * turned_im, axis=0, keepdims=True),
        ],
        axis=0,
    )

    @pl.when(pl.program_id(0) == 0)
    def _():
        sums_ref[...] = sums

    @pl.when(pl.program_id(0) > 0)
    def _():
        sums_ref[...] += sums


def grads_kernel(*refs, pairs):
    ins, (send_ref, keep_ref) = refs[: 2 * pairs], refs[2 * pairs :]
    at = 0
    for p in range(pairs):
        lhs_ref, rhs_ref = ins[2 * p], ins[2 * p + 1]
        half, n = lhs_ref.shape[0] // 2, rhs_ref.shape[1]
        send_ref[:, at : at + n] = dot(lhs_ref[:half, :], rhs_ref[...]).astype(BF)
        keep_ref[:, at : at + n] = dot(lhs_ref[half:, :], rhs_ref[...]).astype(BF)
        at += n


def out_kernel(middle_ref, hid_ref, w_down_ref, out_ref):
    out_ref[...] = (middle_ref[...] + dot(hid_ref[...], w_down_ref[...])).astype(BF)


def input_grads_kernel(lhs_ref, dpre_ref, sums_ref, send_ref, keep_ref, *, per):
    half, n = lhs_ref.shape[0] // 2, dpre_ref.shape[1]
    send_ref[:, :n] = dot(lhs_ref[:half, :], dpre_ref[...]).astype(BF)
    keep_ref[:, :n] = dot(lhs_ref[half:, :], dpre_ref[...]).astype(BF)
    parts = n // 3 // LANES
    flat = [sums_ref[k : k + 1, g * LANES : (g + 1) * LANES] for k in range(2) for g in range(parts)]
    flat.append(jnp.zeros((-2 * parts % 8, LANES), F32))
    flat = jnp.concatenate(flat, axis=0).astype(BF)
    shape = (half, flat.shape[0])
    row, k = lax.broadcasted_iota(jnp.int32, shape, 0), lax.broadcasted_iota(jnp.int32, shape, 1)
    beside = dot((row % per == k).astype(F32).astype(BF), flat).astype(BF)
    send_ref[:, n:] = beside
    keep_ref[:, n:] = beside


def tokens_kernel(dpre_ref, dog_ref, w_in_ref, w_forget_ref, w_ogate_ref, x_ref, gain_ref, dmiddle_ref, out_ref):
    width = x_ref.shape[1]
    up = (
        dot(dpre_ref[:, :width], w_in_ref[...], NT)
        + dot(dpre_ref[:, width:], w_forget_ref[...], NT)
        + dot(dog_ref[...], w_ogate_ref[...], NT)
    )
    x = x_ref[...].astype(F32)
    inv = lax.rsqrt(row_mean(x * x) + epsilon)
    unit = x * inv
    through = up * gain_ref[...][None]
    out_ref[...] = (dmiddle_ref[...] + inv * (through - unit * row_mean(through * unit))).astype(BF)


def rows(*shape):
    return ("rows", shape)


def cols(*shape):
    return ("cols", shape)


def seg(*shape, shift=0, fixed=False):
    return ("seg", shape, shift, fixed)


def whole(*shape):
    return ("whole", shape)


def moved(*shape, dim):
    return ("moved", shape, dim)


def ours(*shape):
    return ("own", shape)


def full(*shape):
    return ("full", shape)


def spec_of(kind):
    if kind[0] == "full":
        return pl.BlockSpec(kind[1], lambda s, *_: (0,) * len(kind[1]))
    if kind[0] == "own":
        return pl.BlockSpec(kind[1], lambda s, here: (here[PLACE], 0))
    if kind[0] not in ("moved",):
        return pl.BlockSpec(memory_space=pltpu.VMEM)
    _, shape, dim = kind
    return pl.BlockSpec(shape, lambda s, *_: tuple(s if d == dim else 0 for d in range(len(shape))))


def view_of(kind, ref):
    step = pl.program_id(0)
    if kind[0] == "rows":
        n = kind[1][0]
        return ref.at[pl.ds(pl.multiple_of(step * n, n), n)]
    if kind[0] == "cols":
        n = kind[1][1]
        return ref.at[:, pl.ds(pl.multiple_of(step * n, n), n)]
    if kind[0] == "seg":
        return ref.at[kind[2] if kind[3] else step + kind[2]]
    return ref


def size_of(shape, dtype):
    return functools.reduce(lambda p, q: p * q, shape) * jnp.dtype(dtype).itemsize


def call(kernel, steps, ins, outs, scratch, scalars, name, after=(), room=5):
    cost = int(COST * MICROSECONDS.get(name, 0.8))
    lead, extra = len(scalars), len(after)
    kinds_in, kinds_out = [k for k, _ in ins], [k for k, _, _ in outs]

    def body(*refs):
        given, refs = refs[: lead + len(ins)], refs[lead + len(ins) + extra :]
        kernel(
            *given[:lead],
            *[view_of(k, r) for k, r in zip(kinds_in, given[lead:], strict=True)],
            *[view_of(k, r) for k, r in zip(kinds_out, refs[: len(outs)], strict=True)],
            *refs[len(outs) :],
        )

    limit = room << 20
    limit += sum(2 * size_of(k[1], a.dtype) for k, a in ins if k[0] in ("moved", "own"))
    limit += sum(2 * size_of(k[1], d) for k, _, d in outs if k[0] in ("moved", "full"))
    limit += sum(size_of(m.shape, m.dtype) for m in scratch)
    return pl.pallas_call(
        body,
        grid_spec=pltpu.PrefetchScalarGridSpec(
            num_scalar_prefetch=lead,
            grid=(steps,),
            in_specs=[spec_of(k) for k in kinds_in] + [pl.BlockSpec(memory_space=pl.ANY)] * extra,
            out_specs=[spec_of(k) for k in kinds_out],
            scratch_shapes=scratch,
        ),
        out_shape=[jax.ShapeDtypeStruct(s, d) for _, s, d in outs],
        compiler_params=pltpu.CompilerParams(vmem_limit_bytes=limit),
        cost_estimate=pl.CostEstimate(flops=cost, bytes_accessed=1, transcendentals=0),
        name=name,
    )(*scalars, *[a for _, a in ins], *after)


def shift_all(payload, axis, n):
    return [payload] + [lax.ppermute(payload, axis, [(i, (i + k) % n) for i in range(n)]) for k in range(1, n)]


def own_bit(axis, bit):
    return lax.shift_right_logical(lax.axis_index(axis).astype(jnp.int32), jnp.int32(bit.bit_length() - 1)) & 1


def swap(v, axis, n, bit):
    return lax.ppermute(v, axis, [(i, i ^ bit) for i in range(n)])


def bits_of(n):
    return [1 << i for i in range((n - 1).bit_length())]


def combine_kernel(here_ref, *refs, plan, n_in):
    ins, outs = refs[:n_in], refs[n_in:]
    for n, (pos, bit, count, sources) in enumerate(plan):
        for flip in (1, 0):
            own = 1 - bit_of(here_ref, *bit) if flip else bit_of(here_ref, *bit)
            for i in range(count):
                low = i % (1 << pos)
                q = (i - low) * 2 + own * (1 << pos) + low
                at = 0
                for addends, mult, off, col, width in sources:
                    cut = slice(col * width, (col + 1) * width)
                    acc = ins[addends[0]][q * mult + off, :, cut].astype(F32)
                    for k in addends[1:]:
                        acc = acc + ins[k][q * mult + off, :, cut].astype(F32)
                    outs[2 * n + 1 - flip][i, :, at : at + width] = acc.astype(BF)
                    at += width


def combine(here, lanes_in, name, after=()):
    arrays, outs, plan = [], [], []

    def operand(a):
        for k, b in enumerate(arrays):
            if a is b:
                return k
        arrays.append(a)
        return len(arrays) - 1

    for pos, bit, sources in lanes_in:
        addends, mult = sources[0][0], sources[0][1]
        per, count = addends[0].shape[1], addends[0].shape[0] // mult // 2
        plan.append((pos, bit, count, [([operand(a) for a in src[0]], *src[1:]) for src in sources]))
        shape = (count, per, sum(src[4] for src in sources))
        outs += [(whole(*shape), shape, BF)] * 2
    got = call(
        functools.partial(combine_kernel, plan=plan, n_in=len(arrays)), 1, [(whole(), a) for a in arrays], outs, [],
        [here], name, after, 4,
    )
    return [(got[2 * n], got[2 * n + 1]) for n in range(len(lanes_in))]


def add_kernel(*refs):
    n = len(refs) // 3
    for i in range(n):
        refs[2 * n + i][...] = (refs[2 * i][...].astype(F32) + refs[2 * i + 1][...].astype(F32)).astype(BF)


def add_pairs(pairs, name, after=()):
    ins = [(whole(*a.shape), a) for pair in pairs for a in pair]
    outs = [(whole(*p[0].shape), p[0].shape, BF) for p in pairs]
    return call(add_kernel, 1, ins, outs, [], [], name, after)


def own_part(row, at, n):
    width = row.shape[1]
    return pltpu.roll(jnp.concatenate([row] * 8, axis=0), (width - at) % width, 1)[0:1, :n]


def finish_kernel(here_ref, *refs, moves, bits, gains, n_out, vectors, ranks):
    lanes_n = len(bits)
    halves, refs = refs[: 2 * lanes_n], refs[2 * lanes_n :]
    ins, outs = refs[: len(refs) - n_out], refs[len(refs) - n_out :]
    half = halves[0].shape[0]

    def at(lane, h, cut):
        pick = bit_of(here_ref, *bits[lane]) == h
        return jnp.where(pick, halves[2 * lane][:, cut].astype(F32), halves[2 * lane + 1][:, cut].astype(F32))

    for lane, col, width, out, row, to in moves:
        for h in range(2):
            outs[out][row + h * half : row + (h + 1) * half, to : to + width] = at(lane, h, slice(col, col + width))
    for out, norm, terms in gains:
        acc = 0.0
        for weight, grad in terms:
            product = ins[weight][...].astype(F32) * outs[grad][...]
            ones = jnp.ones((8, product.shape[1]), BF)
            high = product.astype(BF)
            acc = acc + dot(ones, high, NT) + dot(ones, (product - high.astype(F32)).astype(BF), NT)
        per = acc.shape[1]
        outs[out][...] = (acc[0:1] / own_part(ins[norm][...][None], per * here_ref[PLACE], per))[0]
    if vectors:
        lane, col, first_out = vectors
        block = at(lane, 0, slice(col, col + LANES))
        n = outs[first_out].shape[0]
        parts = n * ranks // LANES
        for k in range(2):
            row = jnp.concatenate([block[k * parts + g : k * parts + g + 1] for g in range(parts)], axis=1)
            outs[first_out + k][...] = own_part(row, n * here_ref[RANK], n)[0]


def finish(here, halves, bits, moves, extra, outs, gains, vectors, ranks, name, after=()):
    ins = [(whole(*a.shape), a) for pair in halves for a in pair] + extra
    return call(
        functools.partial(
            finish_kernel, moves=moves, bits=bits, gains=gains, n_out=len(outs), vectors=vectors, ranks=ranks
        ),
        1, ins, [(k(*shape), shape, F32) for k, shape in outs], [], [here], name, after,
    )


def total(parts):
    out = parts[0].astype(F32)
    for p in parts[1:]:
        out = out + p.astype(F32)
    return out.astype(BF)


def halve(parts, dim, axis, n, bit):
    mine = own_bit(axis, bit)
    got = swap(total([lax.dynamic_index_in_dim(p, 1 - mine, dim, keepdims=False) for p in parts]), axis, n, bit)
    return [lax.dynamic_index_in_dim(p, mine, dim, keepdims=False) for p in parts] + [got]


def plain_reduce(parts, bits, ndp, nseq):
    left = sorted(bits, reverse=True)
    for b in bits:
        parts = halve(parts, left.index(b), "dp", ndp, b)
        left.remove(b)
    out = total(parts)
    for b in bits_of(nseq):
        out = total([out, swap(out, "seq", nseq, b)])
    return out.astype(F32)


def local(
    ndp, nseq,
    tokens, init_state, norm_mix, w_in, w_forget, forget_bias, phase, w_ogate,
    norm_group, w_out, norm_ffn, w_gate, w_up, w_down, cotangent,
):
    segs, span, width = tokens.shape
    ch = w_forget.shape[1]
    hidden = w_gate.shape[1]
    count = segs * span
    mine = ch // nseq
    per = width // ndp
    tall = hidden // width
    rank = lax.axis_index("seq").astype(jnp.int32)
    bits = bits_of(ndp)
    first = next(b for b in bits if (per * b) % TILE == 0)
    rest = [b for b in bits if b != first]
    lo = per * first
    here = jnp.stack([rank, lax.axis_index("dp").astype(jnp.int32)])
    scan = seg(ch // LANES, span, LANES)
    scanned = (scan, (segs, ch // LANES, span, LANES), F32)
    scan_scratch = [pltpu.VMEM((ch // LANES, span, LANES), F32)] * 2

    own = jnp.concatenate(
        [jnp.stack([jnp.cos(phase), jnp.sin(phase)])[None], init_state.transpose(0, 2, 1)], axis=0
    )
    place = (jnp.arange(ch) // mine) == rank
    infos = shift_all(jnp.where(place, jnp.concatenate([own] * nseq, axis=2), 0.0), "seq", nseq)

    col = jnp.arange(width)
    perm = (col[:, None] == 2 * (col % ch)[None, :] + (col // ch)[None, :]).astype(BF)
    member = ((col[:, None] // (width // GROUPS)) == jnp.arange(LANES)[None, :]).astype(BF)

    x = tokens.reshape(count, width)
    cot = cotangent.reshape(count, width)
    normed, normed_t, pre = call(
        functools.partial(project_kernel, lo=lo, first=first), segs,
        [
            (rows(span, width), x), (whole(width), norm_mix), (whole(width, width), w_in),
            (whole(width, ch), w_forget), (whole(ch), forget_bias), (whole(width, width), perm),
        ],
        [
            (rows(span, width), (count, width), BF),
            (cols(width, span), (width, count), BF),
            (seg(span, 3 * ch), (segs, span, 3 * ch), BF),
        ],
        [], [here], "project",
    )
    trig, chunk, totals, lam_re, lam_im, drv_re, drv_im = call(
        functools.partial(summary_kernel, ranks=nseq), segs,
        [(seg(span, 3 * ch), pre)] + [(seg(2, ch, fixed=True), i) for i in infos],
        [
            (whole(2, ch), (2, ch), F32),
            (seg(4, CHUNKS, ch), (segs, 4, CHUNKS, ch), F32),
            (seg(4, ch), (segs, 4, ch), F32),
            scanned, scanned, scanned, scanned,
        ],
        [], [], "summary",
    )
    totals = shift_all(totals, "seq", nseq)
    (og,) = call(
        gate_kernel, 1, [(whole(count, width), normed), (whole(width, width), w_ogate)],
        [(whole(count, width), (count, width), BF)], [], [], "gate", (lam_re,),
    )
    (dh,) = call(
        hidden_grad_kernel, tall, [(whole(count, width), cot), (rows(width, width), w_down)],
        [(cols(count, width), (count, hidden), BF)], [], [], "hidden_grad", (lam_re,),
    )
    y, y_split, start, final, gated_t, middle = call(
        functools.partial(mixer_kernel, ranks=nseq, lo=lo, first=first), segs,
        [(seg(4, ch), t) for t in totals]
        + [(seg(2, ch, shift=1), i) for i in infos]
        + [
            (scan, lam_re), (scan, lam_im), (scan, drv_re), (scan, drv_im), (seg(4, CHUNKS, ch), chunk),
            (whole(width, width), perm), (rows(span, width), x), (rows(span, width), og), (whole(width), norm_group),
            (whole(width, LANES), member), (whole(width, width), w_out),
        ],
        [
            (rows(span, width), (count, width), BF),
            (rows(span, width), (count, width), BF),
            (seg(2, ch), (segs, 2, ch), F32),
            (seg(2, mine), (segs, 2, mine), F32),
            (cols(width, span), (width, count), BF),
            (rows(span, width), (count, width), F32),
        ],
        scan_scratch, [here], "mixer",
    )
    final_state = final.transpose(0, 2, 1)

    tile = width
    gsend, gkeep, dsend, dkeep, hid, dn = call(
        functools.partial(ffn_kernel, lo=lo, dlo=lo * tall, rt=span, first=first), hidden // tile,
        [
            (whole(count, width), middle), (whole(width), norm_ffn), (whole(count, width), cot),
            (cols(width, tile), w_gate), (cols(width, tile), w_up), (cols(count, tile), dh),
        ],
        [
            (cols(width // 2, 2 * tile), (width // 2, 2 * hidden), BF),
            (cols(width // 2, 2 * tile), (width // 2, 2 * hidden), BF),
            (rows(tile // 2, width), (hidden // 2, width), BF),
            (rows(tile // 2, width), (hidden // 2, width), BF),
            (cols(count, tile), (count, hidden), BF),
            (whole(count, width), (count, width), F32),
        ],
        [
            pltpu.VMEM((count, width), BF), pltpu.VMEM((width, count), BF),
            pltpu.VMEM((count, tile), BF), pltpu.VMEM((count, tile), BF),
            pltpu.VMEM((tile, count), BF),
        ],
        [here], "ffn", (), 7,
    )

    ggot, dgot = swap(gsend, "dp", ndp, first), swap(dsend, "dp", ndp, first)

    dmiddle, dbranch, dog, dy_split = call(
        turn_kernel, segs,
        [
            (rows(span, width), dn), (rows(span, width), middle), (rows(span, width), cot), (whole(width), norm_ffn),
            (whole(width, width), w_out), (rows(span, width), y), (rows(span, width), og), (whole(width), norm_group),
            (whole(width, LANES), member), (whole(width, width), perm),
        ],
        [
            (rows(span, width), (count, width), F32),
            (rows(span, width), (count, width), BF),
            (rows(span, width), (count, width), BF),
            (rows(span, width), (count, width), BF),
        ],
        [], [], "turn",
    )
    nblk = ndp // 2
    fast = ndp == 8 and nseq == 4 and per % (2 * TILE) == 0
    x_bit, y_bit = (PLACE, rest[0]), (PLACE, rest[1])
    z_bits = [(RANK, b) for b in bits_of(nseq)]

    def blocks(a, cols_n, tall_n=1):
        return a.reshape(nblk * tall_n, per, cols_n)

    order = ()
    if fast:
        g = [blocks(a, 2 * hidden) for a in (gkeep, ggot)]
        d = [blocks(a, width, tall) for a in (dkeep, dgot)]
        fa = [(g, 1, 0, 0, 3 * width)]
        fb = [(g, 1, 0, 3, width)] + [(d, tall, i, 0, width) for i in range(tall)]
        (fa_send, fa_keep), (fb_send, fb_keep) = combine(here, [(0, x_bit, fa), (1, y_bit, fb)], "ffn_sum1", (dog,))
        fa_got, fb_got = swap(fa_send, "dp", ndp, rest[0]), swap(fb_send, "dp", ndp, rest[1])
        order = (fa_keep,)

    chain, adj = call(
        chains_kernel, segs,
        [(rows(span, width), dy_split), (scan, lam_re), (scan, lam_im), (seg(4, CHUNKS, ch), chunk)],
        [(seg(2, CHUNKS, ch), (segs, 2, CHUNKS, ch), F32), (seg(2, ch), (segs, 2, ch), F32)],
        scan_scratch, [], "chains", order,
    )
    adjs = shift_all(adj, "seq", nseq)

    ntile = width // 3
    osend, okeep = call(
        functools.partial(grads_kernel, pairs=2), width // ntile,
        [
            (whole(width, count), normed_t), (cols(count, ntile), dog),
            (whole(width, count), gated_t), (cols(count, ntile), dbranch),
        ],
        [
            (cols(width // 2, 2 * ntile), (width // 2, 2 * width), BF),
            (cols(width // 2, 2 * ntile), (width // 2, 2 * width), BF),
        ],
        [], [], "mixer_grads", (chain,),
    )
    late, *adjs = lax.optimization_barrier((osend, *adjs))
    ogot = swap(late, "dp", ndp, first)
    dpre, sums = call(
        functools.partial(adjoint_kernel, ranks=nseq), segs,
        [(seg(4, ch), t) for t in totals] + [(seg(2, ch), a) for a in adjs]
        + [
            (seg(span, 3 * ch), pre), (whole(2, ch), trig), (scan, lam_re), (scan, lam_im),
            (rows(span, width), dy_split),
            (rows(span, width), y_split), (seg(2, ch), start),
            (seg(4, CHUNKS, ch), chunk), (seg(2, CHUNKS, ch), chain), (whole(width, width), perm),
        ],
        [(rows(span, 3 * ch), (count, 3 * ch), BF), (whole(2, ch), (2, ch), F32)],
        scan_scratch, [here], "adjoint", (osend,),
    )
    into = 3 * ch + LANES
    isend, ikeep = call(
        functools.partial(input_grads_kernel, per=per), 1,
        [(whole(width, count), normed_t), (whole(count, 3 * ch), dpre), (whole(2, ch), sums)],
        [(whole(width // 2, into), (width // 2, into), BF)] * 2, [], [], "input_grads",
    )
    igot = swap(isend, "dp", ndp, first)
    order = ()
    if fast:
        def one(keep, got):
            return [([keep, got], 1, 0, 0, keep.shape[2])]

        def rows_of(keep, got):
            return one(*(a.reshape(2, per // 2, a.shape[2]) for a in (keep, got)))

        (fa_send, fa_keep), (fb_send, fb_keep) = combine(
            here, [(0, y_bit, one(fa_keep, fa_got)), (0, x_bit, one(fb_keep, fb_got))], "ffn_sum2", (isend,)
        )
        fa_got, fb_got = swap(fa_send, "dp", ndp, rest[1]), swap(fb_send, "dp", ndp, rest[0])
        order = (fa_keep,)

    (grad_tokens,) = call(
        tokens_kernel, segs,
        [
            (rows(span, 3 * ch), dpre), (rows(span, width), dog), (whole(width, width), w_in),
            (whole(width, ch), w_forget), (whole(width, width), w_ogate), (rows(span, width), x),
            (whole(width), norm_mix), (rows(span, width), dmiddle),
        ],
        [(moved(span, width, dim=0), (count, width), BF)],
        [], [], "tokens", order,
    )

    def output(*after):
        return call(
            out_kernel, segs, [(rows(span, width), middle), (rows(span, hidden), hid), (whole(hidden, width), w_down)],
            [(moved(span, width, dim=0), (count, width), BF)], [], [], "out", after,
        )[0]

    if fast:
        lead, other = bits_of(nseq)

        o = [blocks(a, 2 * width) for a in (okeep, ogot)]
        i = [blocks(a, into) for a in (ikeep, igot)]
        (ra_send, ra_keep), (rb_send, rb_keep) = combine(
            here, [(0, x_bit, [(o, 1, 0, 0, 2 * width)]), (1, y_bit, [(i, 1, 0, 0, into)])], "mixer_sum1", (grad_tokens,)
        )
        ra_got, rb_got = swap(ra_send, "dp", ndp, rest[0]), swap(rb_send, "dp", ndp, rest[1])

        def over(send, axis_n, bit):
            return swap(send, "seq", axis_n, bit)

        (fa_send, fa_keep), (fb_send, fb_keep) = combine(
            here, [(0, z_bits[0], rows_of(fa_keep, fa_got)), (0, z_bits[1], rows_of(fb_keep, fb_got))],
            "ffn_sum3", (ra_keep,),
        )
        fa_got, fb_got = over(fa_send, nseq, lead), over(fb_send, nseq, other)
        mixed_out = output(fa_keep)
        fa, fb = add_pairs([(fa_keep, fa_got), (fb_keep, fb_got)], "ffn_sum4", (mixed_out,))
        fa_got, fb_got = over(fa, nseq, other), over(fb, nseq, lead)
        (ra_send, ra_keep), (rb_send, rb_keep) = combine(
            here, [(0, y_bit, one(ra_keep, ra_got)), (0, x_bit, one(rb_keep, rb_got))], "mixer_sum2", (fa,)
        )
        ra_got, rb_got = swap(ra_send, "dp", ndp, rest[1]), swap(rb_send, "dp", ndp, rest[0])
        (ra_send, ra_keep), (rb_send, rb_keep) = combine(
            here, [(0, z_bits[0], rows_of(ra_keep, ra_got)), (0, z_bits[1], rows_of(rb_keep, rb_got))], "mixer_sum3", (fa,)
        )
        ra_got, rb_got = over(ra_send, nseq, lead), over(rb_send, nseq, other)
        fa, fb = add_pairs([(fa, fa_got), (fb, fb_got)], "ffn_sum5", (ra_keep,))
        fa_got, fb_got = over(fa, nseq, lead), over(fb, nseq, other)
        ra, rb = add_pairs([(ra_keep, ra_got), (rb_keep, rb_got)], "mixer_sum4", (fa,))
        ra_got, rb_got = over(ra, nseq, other), over(rb, nseq, lead)

        def flat(*pairs):
            return [tuple(a.reshape(per // 2, a.shape[2]) for a in pair) for pair in pairs]

        guv = [(0, c * width) for c in range(3)] + [(1, 0)]
        moves = [
            (lane, col, width, n % 2, 0, (n // 2) * width) for n, (lane, col) in enumerate(guv)
        ] + [(1, (1 + t) * width, width, 2, t * per, 0) for t in range(tall)]
        part_gate, part_up, part_down, part_ffn = finish(
            here, flat((fa, fa_got), (fb, fb_got)), z_bits, moves,
            [(ours(per, hidden), w_gate), (ours(per, hidden), w_up), (whole(width), norm_ffn)],
            [(full, (per, hidden)), (full, (per, hidden)), (full, (tall * per, width)), (full, (per,))],
            [(3, 2, [(0, 0), (1, 1)])], None, nseq, "ffn_out", (ra,),
        )
        ra, rb = add_pairs([(ra, ra_got), (rb, rb_got)], "mixer_sum5", (part_gate,))
        ra_got, rb_got = over(ra, nseq, lead), over(rb, nseq, other)
        moves = [(0, n * ntile, ntile, n % 2, 0, (n // 2) * ntile) for n in range(2 * width // ntile)]
        moves += [(1, 0, width, 2, 0, 0), (1, width, ch, 3, 0, 0)]
        part_ogate, part_out, part_in, part_forget, part_mix, part_group, part_bias, part_phase = finish(
            here, flat((ra, ra_got), (rb, rb_got)), z_bits, moves,
            [
                (ours(per, width), w_ogate), (ours(per, width), w_out), (ours(per, width), w_in), (ours(per, ch), w_forget),
                (whole(width), norm_mix), (whole(width), norm_group),
            ],
            [(full, (per, n)) for n in (width, width, width, ch)] + [(full, (n,)) for n in (per, per, mine, mine)],
            [(4, 4, [(0, 0), (2, 2), (3, 3)]), (5, 5, [(1, 1)])], (1, 3 * ch, 6), nseq, "mixer_out",
        )
    else:
        mixed_out = output()

        def plain(keep, got, cols_n, tall_n=1):
            shape = [2] * len(rest) + [tall_n * per, cols_n]
            return plain_reduce([keep.reshape(shape), got.reshape(shape)], rest, ndp, nseq)

        guv = plain(gkeep, ggot, 2 * hidden)
        guv = [guv[:, n * tile : (n + 1) * tile] for n in range(2 * hidden // tile)]
        part_gate, part_up = jnp.concatenate(guv[0::2], axis=1), jnp.concatenate(guv[1::2], axis=1)
        part_down = plain(dkeep, dgot, width, tall)
        mix = plain(okeep, ogot, 2 * width)
        mix = [mix[:, n * ntile : (n + 1) * ntile] for n in range(2 * width // ntile)]
        part_ogate, part_out = jnp.concatenate(mix[0::2], axis=1), jnp.concatenate(mix[1::2], axis=1)
        both = plain(ikeep, igot, into)
        part_in, part_forget = both[:, :width], both[:, width : 3 * ch]
        shared = both[: 2 * ch // LANES, 3 * ch :].reshape(2, ch)
        part_bias, part_phase = lax.dynamic_slice_in_dim(shared, rank * mine, mine, axis=1)

        def own_rows(a):
            return lax.dynamic_slice_in_dim(a, lax.axis_index("dp") * per, per, axis=0).astype(F32)

        def gain_of(norm, *pairs):
            return sum(jnp.sum(own_rows(w) * gw, axis=1) for w, gw in pairs) / own_rows(norm)

        part_ffn = gain_of(norm_ffn, (w_gate, part_gate), (w_up, part_up))
        part_mix = gain_of(norm_mix, (w_in, part_in), (w_forget, part_forget), (w_ogate, part_ogate))
        part_group = gain_of(norm_group, (w_out, part_out))
    return (
        mixed_out.reshape(segs, span, width),
        grad_tokens.reshape(segs, span, width),
        final_state,
        part_mix, part_in, part_forget, part_bias, part_phase, part_ogate, part_group, part_out, part_ffn,
        part_gate, part_up, part_down,
    )


def solution(mesh):
    ndp, nseq = mesh.shape["dp"], mesh.shape["seq"]
    tok, vec, col = P("dp", "seq", None), P("dp"), P("dp", None)
    return jax.shard_map(
        functools.partial(local, ndp, nseq),
        mesh=mesh,
        in_specs=(tok, tok, P(), P(), P(), P(), P("seq"), P(), P(), P(), P(), P(), P(), P(), tok),
        out_specs=(tok, tok, tok, vec, col, col, P("seq"), P("seq"), col, vec, col, vec, col, col, col),
        check_vma=False,
    )
```

```python
import functools

import jax
import jax.numpy as jnp
from jax import lax
from jax.experimental import pallas as pl
from jax.experimental.pallas import tpu as pltpu
from jax.sharding import PartitionSpec as P

GROUPS = 8
CHUNKS = 8
LANES = 128
RANK, PLACE = 0, 1
MICROSECONDS = dict(
    project=4, summary=4, hidden_grad=2.5, mixer=8, ffn_first=6, ffn_rest=12, turn=7, chains=0.3, mixer_grads=0.3, adjoint=0.3, input_grads=0.3, tokens=0.3, ffn_sum4=8, out=3.5,
    ffn_sum1=1.3, mixer_sum1=1.0, ffn_sum2=3, ffn_sum3=20,
)
COST = 1.15e9
TILE = 16
epsilon = 1e-06
BF = jnp.bfloat16
F32 = jnp.float32
NT = ((1,), (1,))


def dot(a, b, dims=((1,), (0,))):
    return lax.dot_general(a, b, (dims, ((), ())), preferred_element_type=F32)


def silu_slope(values, logistic):
    return logistic * (1.0 + values * (1.0 - logistic))


def cmul(ar, ai, br, bi):
    return ar * br - ai * bi, ar * bi + ai * br


def row_mean(v):
    return jnp.mean(v, axis=-1, keepdims=True)


def split_dot(v, m, dims):
    high = v.astype(BF)
    low = (v - high.astype(F32)).astype(BF)
    return dot(high, m, dims) + dot(low, m, dims)


def group_mean(v, member):
    return split_dot(v, member, ((1,), (0,))) * (GROUPS / v.shape[1])


def group_spread(v, member):
    return split_dot(v, member, NT)


def bit_of(here_ref, which, bit):
    return lax.shift_right_logical(here_ref[which], bit.bit_length() - 1) & 1


def put_halves(ref, t, col, lo, bit):
    half = ref.shape[0] // 2
    for b in range(t.shape[0] // lo):
        at = jnp.where(bit == b % 2, half, 0) + (b // 2) * lo
        ref[pl.ds(pl.multiple_of(at, TILE), lo), col : col + t.shape[1]] = t[b * lo : (b + 1) * lo, :]


def at_step(t):
    return slice(CHUNKS * t, CHUNKS * (t + 1))


def reorder(order_ref, v, back=False):
    return dot(order_ref[...], v, ((0,), (0,)) if back else ((1,), (0,))).astype(BF)


def own_kernel(phase_ref, init_ref, infos_ref, here_ref, line_ref):
    own = phase_ref.shape[0]
    rank, place = lax.axis_index("seq"), lax.axis_index("dp")
    here_ref[RANK], here_ref[PLACE] = rank, place
    theta = phase_ref[...][None]
    line_ref[...] = jnp.zeros_like(line_ref)
    line_ref[0:1, :own] = jnp.cos(theta)
    line_ref[1:2, :own] = jnp.sin(theta)
    for n in range(init_ref.shape[0]):
        line_ref[2 + 2 * n : 4 + 2 * n, :own] = init_ref[n]
    placed = pltpu.roll(line_ref[...], own * rank, 1)
    for n in range(infos_ref.shape[0]):
        infos_ref[n] = placed[2 * n : 2 * n + 2, :]


def project_kernel(
    here_ref, x_ref, gain_ref, w_in_ref, w_forget_ref, bias_ref, perm_ref, order_ref, xs_ref, normed_ref, turned_ref,
    pre_ref, *, lo, first
):
    width = x_ref.shape[1]
    xs = reorder(order_ref, x_ref[...])
    xs_ref[...] = xs
    x = xs.astype(F32)
    normed = (x * lax.rsqrt(row_mean(x * x) + epsilon) * gain_ref[...][None]).astype(BF)
    normed_ref[...] = normed
    put_halves(turned_ref, normed.T, 0, lo, bit_of(here_ref, PLACE, first))
    mixed = dot(normed, w_in_ref[...]).astype(BF)
    pre_ref[:, :width] = dot(mixed, perm_ref[...]).astype(BF)
    pre_ref[:, width:] = (dot(normed, w_forget_ref[...]) + bias_ref[...][None]).astype(BF)


def summary_kernel(*refs, ranks):
    pre_ref, infos = refs[0], refs[1 : 1 + ranks]
    trig_ref, chunk_ref, total_ref, lam_re, lam_im, drv_re, drv_im = refs[1 + ranks :]
    span, ch = lam_re.shape
    trig = infos[0][...]
    for info in infos[1:]:
        trig = trig + info[...]
    trig_ref[...] = trig
    pre = pre_ref[...].astype(F32)
    forget = jax.nn.sigmoid(pre[:, 2 * ch :])
    lam_re[...] = forget * trig[0:1, :]
    lam_im[...] = forget * trig[1:2, :]
    drv_re[...] = (1.0 - forget) * jax.nn.silu(pre[:, :ch])
    drv_im[...] = (1.0 - forget) * jax.nn.silu(pre[:, ch : 2 * ch])
    first = at_step(0)
    pr, pi, hr, hi = lam_re[first, :], lam_im[first, :], drv_re[first, :], drv_im[first, :]
    for t in range(1, span // CHUNKS):
        lr, li = lam_re[at_step(t), :], lam_im[at_step(t), :]
        pr, pi = cmul(lr, li, pr, pi)
        hr, hi = cmul(lr, li, hr, hi)
        hr, hi = hr + drv_re[at_step(t), :], hi + drv_im[at_step(t), :]
    chunk_ref[0], chunk_ref[1], chunk_ref[2], chunk_ref[3] = pr, pi, hr, hi
    tp_r, tp_i, th_r, th_i = pr[0:1], pi[0:1], hr[0:1], hi[0:1]
    for k in range(1, CHUNKS):
        lr, li = pr[k : k + 1], pi[k : k + 1]
        th_r, th_i = cmul(lr, li, th_r, th_i)
        th_r, th_i = th_r + hr[k : k + 1], th_i + hi[k : k + 1]
        tp_r, tp_i = cmul(lr, li, tp_r, tp_i)
    total_ref[...] = jnp.concatenate([tp_r, tp_i, th_r, th_i], axis=0)


def mixer_kernel(*refs, ranks, lo, first):
    scalars, refs = refs[0], refs[1:]
    totals, inits, refs = refs[:ranks], refs[ranks : 2 * ranks], refs[2 * ranks :]
    lam_re, lam_im, drv_re, drv_im, chunk_ref, perm_ref, x_ref, og_ref, gain_ref, member_ref, w_out_ref = refs[:11]
    y_ref, split_ref, start_ref, final_ref, turned_ref, middle_ref, st_re, st_im = refs[11:]
    span, ch = lam_re.shape
    rank, bit = scalars[RANK], bit_of(scalars, PLACE, first)
    init = inits[0][...]
    for info in inits[1:]:
        init = init + info[...]
    cr, ci = init[0:1], init[1:2]

    def after(k, cr, ci, take):
        total = totals[k][...]
        nr, ni = cmul(total[0:1], total[1:2], cr, ci)
        nr, ni = nr + total[2:3], ni + total[3:4]
        return jnp.where(take, nr, cr), jnp.where(take, ni, ci)

    for k in range(ranks - 1, 0, -1):
        cr, ci = after(k, cr, ci, k <= rank)
    start_ref[...] = jnp.concatenate([cr, ci], axis=0)
    er, ei = after(0, cr, ci, rank >= 0)
    for k in range(ranks - 1, 0, -1):
        er, ei = after(k, er, ei, k > rank)
    own = ch // ranks
    final_ref[...] = pltpu.roll(jnp.concatenate([er, ei] * 4, axis=0), (ch - own * rank) % ch, 1)[:2, :own]
    rows_r, rows_i = [cr], [ci]
    for k in range(CHUNKS - 1):
        cr, ci = cmul(chunk_ref[0, k : k + 1, :], chunk_ref[1, k : k + 1, :], cr, ci)
        cr, ci = cr + chunk_ref[2, k : k + 1, :], ci + chunk_ref[3, k : k + 1, :]
        rows_r.append(cr)
        rows_i.append(ci)
    hr, hi = jnp.concatenate(rows_r, axis=0), jnp.concatenate(rows_i, axis=0)
    for t in range(span // CHUNKS):
        hr, hi = cmul(lam_re[at_step(t), :], lam_im[at_step(t), :], hr, hi)
        hr, hi = hr + drv_re[at_step(t), :], hi + drv_im[at_step(t), :]
        st_re[at_step(t), :] = hr
        st_im[at_step(t), :] = hi
    split = jnp.concatenate([st_re[...].astype(BF), st_im[...].astype(BF)], axis=1)
    split_ref[...] = split
    yf = dot(split, perm_ref[...], NT)
    y_ref[...] = yf.astype(BF)
    member = member_ref[...]
    inv = group_spread(lax.rsqrt(group_mean(yf * yf, member) + epsilon), member)
    gated = (yf * inv * gain_ref[...][None] * jax.nn.silu(og_ref[...].astype(F32))).astype(BF)
    put_halves(turned_ref, gated.T, 0, lo, bit)
    middle_ref[...] = x_ref[...].astype(F32) + dot(gated, w_out_ref[...])


def hidden_tile(n_ref, rows, cut, wg_ref, wu_ref, dh_ref, hid_ref, dgv_ref, duv_ref, to):
    g, u = dot(n_ref[rows, :], wg_ref[:, cut]), dot(n_ref[rows, :], wu_ref[:, cut])
    dh = dh_ref[rows, cut].astype(F32)
    sig = jax.nn.sigmoid(g)
    act = g * sig
    hid_ref[rows, to] = (act * u).astype(BF)
    dgv_ref[rows, to] = (dh * u * silu_slope(g, sig)).astype(BF)
    duv_ref[rows, to] = (dh * act).astype(BF)


def two_halves(lhs_ref, rhs, send_ref, keep_ref, to):
    half = lhs_ref.shape[0] // 2
    send_ref[:, to] = dot(lhs_ref[:half, :], rhs).astype(BF)
    keep_ref[:, to] = dot(lhs_ref[half:, :], rhs).astype(BF)


def ffn_first_kernel(
    here_ref, middle_ref, gain_ref, wg_ref, wu_ref, dh_ref,
    gsend_ref, gkeep_ref, n_ref, nt_ref, hid_ref, dgv_ref, duv_ref,
    *, lo, rt, first,
):
    bit = bit_of(here_ref, PLACE, first)
    count, width = middle_ref.shape
    cut = slice(0, width)
    for r in range(0, count, rt):
        rows = slice(r, r + rt)
        v = middle_ref[rows, :]
        normed = (v * lax.rsqrt(row_mean(v * v) + epsilon) * gain_ref[...][None]).astype(BF)
        n_ref[rows, :] = normed
        put_halves(nt_ref, normed.T, r, lo, bit)
        hidden_tile(n_ref, rows, cut, wg_ref, wu_ref, dh_ref, hid_ref, dgv_ref, duv_ref, cut)
    two_halves(nt_ref, dgv_ref[...], gsend_ref, gkeep_ref, cut)
    two_halves(nt_ref, duv_ref[...], gsend_ref, gkeep_ref, slice(width, 2 * width))


def ffn_rest_kernel(
    here_ref, n_ref, nt_ref, cot_ref, wg_ref, wu_ref, dh_ref, hid0_ref, dgv0_ref, duv0_ref,
    gsend_ref, gkeep_ref, dsend_ref, dkeep_ref, hid_ref, dn_ref,
    dgv_ref, duv_ref, ht_ref,
    *, lo, rt, first,
):
    bit = bit_of(here_ref, PLACE, first)
    count, width = n_ref.shape
    spans = [slice(r, r + rt) for r in range(0, count, rt)]
    cut, own = slice(width, 2 * width), slice(0, width)
    for rows in spans:
        hidden_tile(n_ref, rows, cut, wg_ref, wu_ref, dh_ref, hid_ref, dgv_ref, duv_ref, own)
    two_halves(nt_ref, dgv_ref[...], gsend_ref, gkeep_ref, own)
    two_halves(nt_ref, duv_ref[...], gsend_ref, gkeep_ref, cut)
    half = width // 2
    for j, ref in enumerate((hid0_ref, hid_ref)):
        for rows in spans:
            put_halves(ht_ref.at[j], ref[rows, :].T, rows.start, lo, bit)
    for j in range(2):
        out = slice(j * half, (j + 1) * half)
        dsend_ref[out, :] = dot(ht_ref[j, :half, :], cot_ref[...]).astype(BF)
        dkeep_ref[out, :] = dot(ht_ref[j, half:, :], cot_ref[...]).astype(BF)
    for rows in spans:
        dn_ref[rows, :] = (
            dot(dgv0_ref[rows, :], wg_ref[:, own], NT)
            + dot(duv0_ref[rows, :], wu_ref[:, own], NT)
            + dot(dgv_ref[rows, :], wg_ref[:, cut], NT)
            + dot(duv_ref[rows, :], wu_ref[:, cut], NT)
        )


def gate_kernel(normed_ref, w_ref, og_ref):
    og_ref[...] = dot(normed_ref[...], w_ref[...]).astype(BF)


def hidden_grad_kernel(cot_ref, wd_ref, order_ref, cots_ref, dh_ref):
    cots = reorder(order_ref, cot_ref[...])
    cots_ref[...] = cots
    dh_ref[...] = dot(cots, wd_ref[...], NT).astype(BF)


def turn_kernel(
    dn_ref, middle_ref, cot_ref, ffn_gain_ref, w_out_ref, y_ref, og_ref, gain_ref, member_ref, perm_ref,
    dmiddle_ref, dbranch_ref, dog_ref, split_ref,
):
    v, up = middle_ref[...], dn_ref[...]
    inv = lax.rsqrt(row_mean(v * v) + epsilon)
    unit = v * inv
    through = up * ffn_gain_ref[...][None]
    dmiddle = cot_ref[...].astype(F32) + inv * (through - unit * row_mean(through * unit))
    dmiddle_ref[...] = dmiddle
    dbranch = dmiddle.astype(BF)
    dbranch_ref[...] = dbranch
    dgated = dot(dbranch, w_out_ref[...], NT)
    og, yf, member, gain = og_ref[...].astype(F32), y_ref[...].astype(F32), member_ref[...], gain_ref[...][None]
    ginv = group_spread(lax.rsqrt(group_mean(yf * yf, member) + epsilon), member)
    gunit = yf * ginv
    sig = jax.nn.sigmoid(og)
    dog_ref[...] = (dgated * gunit * gain * silu_slope(og, sig)).astype(BF)
    through = dgated * og * sig * gain
    dy = (ginv * (through - gunit * group_spread(group_mean(through * gunit, member), member))).astype(BF)
    split_ref[...] = dot(dy, perm_ref[...]).astype(BF)


def chains_kernel(split_ref, lam_re, lam_im, chunk_ref, chain_ref, total_ref, dy_re, dy_im):
    span, ch = lam_re.shape
    dy_re[...] = split_ref[:, :ch].astype(F32)
    dy_im[...] = split_ref[:, ch:].astype(F32)
    last = span // CHUNKS - 1
    gr, gi = dy_re[at_step(last), :], dy_im[at_step(last), :]
    ar, ai = cmul(lam_re[at_step(last), :], -lam_im[at_step(last), :], gr, gi)
    for t in range(last - 1, -1, -1):
        gr, gi = dy_re[at_step(t), :] + ar, dy_im[at_step(t), :] + ai
        ar, ai = cmul(lam_re[at_step(t), :], -lam_im[at_step(t), :], gr, gi)
    chain_ref[0], chain_ref[1] = ar, ai
    er, ei = ar[CHUNKS - 1 :], ai[CHUNKS - 1 :]
    for k in range(CHUNKS - 2, -1, -1):
        er, ei = cmul(chunk_ref[0, k : k + 1, :], -chunk_ref[1, k : k + 1, :], er, ei)
        er, ei = er + ar[k : k + 1], ei + ai[k : k + 1]
    total_ref[...] = jnp.concatenate([er, ei], axis=0)


def adjoint_kernel(*refs, ranks):
    scalars, refs = refs[0], refs[1:]
    totals, adjs, refs = refs[:ranks], refs[ranks : 2 * ranks], refs[2 * ranks :]
    pre_ref, trig_ref, lam_re, lam_im, dy_ref, split_ref, start_ref, chunk_ref, chain_ref, perm_ref = refs[:10]
    dpre_ref, sums_ref, dy_re, dy_im = refs[10:]
    span, ch = lam_re.shape
    rank = scalars[RANK]
    pre = pre_ref[...].astype(F32)
    trig = trig_ref[...]
    forget = jax.nn.sigmoid(pre[:, 2 * ch :])
    dy_re[...] = dy_ref[:, :ch].astype(F32)
    dy_im[...] = dy_ref[:, ch:].astype(F32)
    cr = jnp.zeros((1, ch), F32)
    ci = jnp.zeros((1, ch), F32)
    for k in range(1, ranks):
        total, adj = totals[k][...], adjs[k][...]
        nr, ni = cmul(total[0:1], -total[1:2], cr, ci)
        nr, ni = nr + adj[0:1], ni + adj[1:2]
        cr, ci = jnp.where(k > rank, nr, cr), jnp.where(k > rank, ni, ci)
    rows_r, rows_i = [cr], [ci]
    for k in range(CHUNKS - 1, 0, -1):
        cr, ci = cmul(chunk_ref[0, k : k + 1, :], -chunk_ref[1, k : k + 1, :], cr, ci)
        cr, ci = cr + chain_ref[0, k : k + 1, :], ci + chain_ref[1, k : k + 1, :]
        rows_r.append(cr)
        rows_i.append(ci)
    ar, ai = jnp.concatenate(rows_r[::-1], axis=0), jnp.concatenate(rows_i[::-1], axis=0)
    for t in range(span // CHUNKS - 1, -1, -1):
        gr, gi = dy_re[at_step(t), :] + ar, dy_im[at_step(t), :] + ai
        dy_re[at_step(t), :] = gr
        dy_im[at_step(t), :] = gi
        ar, ai = cmul(lam_re[at_step(t), :], -lam_im[at_step(t), :], gr, gi)
    gr, gi = dy_re[...], dy_im[...]

    def before(states, start):
        ends = pltpu.roll(states[span - CHUNKS :, :], 1, 0)
        ends = jnp.where(lax.broadcasted_iota(jnp.int32, ends.shape, 0) == 0, start, ends)
        return jnp.concatenate([ends, states[: span - CHUNKS, :]], axis=0)

    qr = before(split_ref[:, :ch].astype(F32), start_ref[0:1, :])
    qi = before(split_ref[:, ch:].astype(F32), start_ref[1:2, :])
    pin_re, pin_im = pre[:, :ch], pre[:, ch : 2 * ch]
    sig_re, sig_im = jax.nn.sigmoid(pin_re), jax.nn.sigmoid(pin_im)
    lr = gr * qr + gi * qi
    li = gi * qr - gr * qi
    turned_re = lr * trig[0:1, :] + li * trig[1:2, :]
    turned_im = li * trig[0:1, :] - lr * trig[1:2, :]
    df = turned_re - (gr * pin_re * sig_re + gi * pin_im * sig_im)
    keep = 1.0 - forget
    dre = (keep * gr * silu_slope(pin_re, sig_re)).astype(BF)
    dim = (keep * gi * silu_slope(pin_im, sig_im)).astype(BF)
    dpz = (forget * keep * df).astype(BF)
    dpre_ref[:, : 2 * ch] = dot(jnp.concatenate([dre, dim], axis=1), perm_ref[...], NT).astype(BF)
    dpre_ref[:, 2 * ch :] = dpz
    sums = jnp.concatenate(
        [
            jnp.sum(dpz.astype(F32), axis=0, keepdims=True),
            jnp.sum(forget * turned_im, axis=0, keepdims=True),
        ],
        axis=0,
    )

    @pl.when(pl.program_id(0) == 0)
    def _():
        sums_ref[...] = sums

    @pl.when(pl.program_id(0) > 0)
    def _():
        sums_ref[...] += sums


def grads_kernel(*refs, pairs):
    ins, (send_ref, keep_ref) = refs[: 2 * pairs], refs[2 * pairs :]
    at = 0
    for p in range(pairs):
        lhs_ref, rhs_ref = ins[2 * p], ins[2 * p + 1]
        half, n = lhs_ref.shape[0] // 2, rhs_ref.shape[1]
        send_ref[:, at : at + n] = dot(lhs_ref[:half, :], rhs_ref[...]).astype(BF)
        keep_ref[:, at : at + n] = dot(lhs_ref[half:, :], rhs_ref[...]).astype(BF)
        at += n


def out_kernel(middle_ref, hid0_ref, hid_ref, w_down_ref, order_ref, out_ref, done_ref):
    width = middle_ref.shape[1]
    branch = dot(hid0_ref[...], w_down_ref[:width, :]) + dot(hid_ref[...], w_down_ref[width:, :])
    out = (middle_ref[...] + branch).astype(BF)
    out_ref[...] = reorder(order_ref, out, True)
    done_ref[...] = jnp.zeros_like(done_ref)


def input_grads_kernel(lhs_ref, dpre_ref, sums_ref, send_ref, keep_ref, *, per):
    half, n = lhs_ref.shape[0] // 2, dpre_ref.shape[1]
    send_ref[:, :n] = dot(lhs_ref[:half, :], dpre_ref[...]).astype(BF)
    keep_ref[:, :n] = dot(lhs_ref[half:, :], dpre_ref[...]).astype(BF)
    parts = n // 3 // LANES
    flat = [sums_ref[k : k + 1, g * LANES : (g + 1) * LANES] for k in range(2) for g in range(parts)]
    flat.append(jnp.zeros((-2 * parts % 8, LANES), F32))
    flat = jnp.concatenate(flat, axis=0).astype(BF)
    shape = (half, flat.shape[0])
    row, k = lax.broadcasted_iota(jnp.int32, shape, 0), lax.broadcasted_iota(jnp.int32, shape, 1)
    beside = dot((row % per == k).astype(F32).astype(BF), flat).astype(BF)
    send_ref[:, n:] = beside
    keep_ref[:, n:] = beside


def tokens_kernel(
    dpre_ref, dog_ref, w_in_ref, w_forget_ref, w_ogate_ref, x_ref, gain_ref, dmiddle_ref, order_ref, out_ref, done_ref
):
    width = x_ref.shape[1]
    up = (
        dot(dpre_ref[:, :width], w_in_ref[...], NT)
        + dot(dpre_ref[:, width:], w_forget_ref[...], NT)
        + dot(dog_ref[...], w_ogate_ref[...], NT)
    )
    x = x_ref[...].astype(F32)
    inv = lax.rsqrt(row_mean(x * x) + epsilon)
    unit = x * inv
    through = up * gain_ref[...][None]
    out = (dmiddle_ref[...] + inv * (through - unit * row_mean(through * unit))).astype(BF)
    out_ref[...] = reorder(order_ref, out, True)
    done_ref[...] = jnp.zeros_like(done_ref)


def rows(*shape):
    return ("rows", shape)


def cols(*shape):
    return ("cols", shape)


def seg(*shape, shift=0, fixed=False):
    return ("seg", shape, shift, fixed)


def whole(*shape):
    return ("whole", shape)


def moved(*shape, dim):
    return ("moved", shape, dim)


def ours(*shape):
    return ("own", shape)


def full(*shape):
    return ("full", shape)


def spec_of(kind):
    if kind[0] == "smem":
        return pl.BlockSpec(memory_space=pltpu.SMEM)
    if kind[0] == "full":
        return pl.BlockSpec(kind[1], lambda s, *_: (0,) * len(kind[1]))
    if kind[0] == "own":
        return pl.BlockSpec(kind[1], lambda s, here: (here[PLACE], 0))
    if kind[0] not in ("moved",):
        return pl.BlockSpec(memory_space=pltpu.VMEM)
    _, shape, dim = kind
    return pl.BlockSpec(shape, lambda s, *_: tuple(s if d == dim else 0 for d in range(len(shape))))


def view_of(kind, ref):
    step = pl.program_id(0)
    if kind[0] == "rows":
        n = kind[1][0]
        return ref.at[pl.ds(pl.multiple_of(step * n, n), n)]
    if kind[0] == "cols":
        n = kind[1][1]
        return ref.at[:, pl.ds(pl.multiple_of(step * n, n), n)]
    if kind[0] == "seg":
        return ref.at[kind[2] if kind[3] else step + kind[2]]
    return ref


def size_of(shape, dtype):
    return functools.reduce(lambda p, q: p * q, shape) * jnp.dtype(dtype).itemsize


def call(kernel, steps, ins, outs, scratch, scalars, name, after=(), room=5):
    cost = int(COST * MICROSECONDS.get(name, 0.8))
    lead, extra = len(scalars), len(after)
    kinds_in, kinds_out = [k for k, _ in ins], [k for k, _, _ in outs]

    def body(*refs):
        given, refs = refs[: lead + len(ins)], refs[lead + len(ins) + extra :]
        kernel(
            *given[:lead],
            *[view_of(k, r) for k, r in zip(kinds_in, given[lead:], strict=True)],
            *[view_of(k, r) for k, r in zip(kinds_out, refs[: len(outs)], strict=True)],
            *refs[len(outs) :],
        )

    limit = room << 20
    limit += sum(2 * size_of(k[1], a.dtype) for k, a in ins if k[0] in ("moved", "own"))
    limit += sum(2 * size_of(k[1], d) for k, _, d in outs if k[0] in ("moved", "full"))
    limit += sum(size_of(m.shape, m.dtype) for m in scratch)
    return pl.pallas_call(
        body,
        grid_spec=pltpu.PrefetchScalarGridSpec(
            num_scalar_prefetch=lead,
            grid=(steps,),
            in_specs=[spec_of(k) for k in kinds_in] + [pl.BlockSpec(memory_space=pl.ANY)] * extra,
            out_specs=[spec_of(k) for k in kinds_out],
            scratch_shapes=scratch,
        ),
        out_shape=[jax.ShapeDtypeStruct(s, d) for _, s, d in outs],
        compiler_params=pltpu.CompilerParams(vmem_limit_bytes=limit),
        cost_estimate=pl.CostEstimate(flops=cost, bytes_accessed=1, transcendentals=0),
        name=name,
    )(*scalars, *[a for _, a in ins], *after)


def shift_all(payload, axis, n):
    return [payload] + [lax.ppermute(payload, axis, [(i, (i + k) % n) for i in range(n)]) for k in range(1, n)]


def own_bit(axis, bit):
    return lax.shift_right_logical(lax.axis_index(axis).astype(jnp.int32), jnp.int32(bit.bit_length() - 1)) & 1


def swap(v, axis, n, bit):
    return lax.ppermute(v, axis, [(i, i ^ bit) for i in range(n)])


def bits_of(n):
    return [1 << i for i in range((n - 1).bit_length())]


def combine_kernel(here_ref, *refs, plan, n_in, sums):
    ins, outs = refs[:n_in], refs[n_in:]
    for n, (a, b) in enumerate(sums):
        outs[2 * len(plan) + n][...] = (ins[a][...].astype(F32) + ins[b][...].astype(F32)).astype(BF)
    for n, (pos, bit, count, sources) in enumerate(plan):
        for flip in (1, 0):
            own = 1 - bit_of(here_ref, *bit) if flip else bit_of(here_ref, *bit)
            for i in range(count):
                low = i % (1 << pos)
                q = (i - low) * 2 + own * (1 << pos) + low
                at = 0
                for addends, mult, off, col, width in sources:
                    cut = slice(col * width, (col + 1) * width)
                    acc = ins[addends[0]][q * mult + off, :, cut].astype(F32)
                    for k in addends[1:]:
                        acc = acc + ins[k][q * mult + off, :, cut].astype(F32)
                    outs[2 * n + 1 - flip][i, :, at : at + width] = acc.astype(BF)
                    at += width


def combine(here, lanes_in, name, after=(), sums=()):
    arrays, outs, plan = [], [], []

    def operand(a):
        for k, b in enumerate(arrays):
            if a is b:
                return k
        arrays.append(a)
        return len(arrays) - 1

    for pos, bit, sources in lanes_in:
        addends, mult = sources[0][0], sources[0][1]
        per, count = addends[0].shape[1], addends[0].shape[0] // mult // 2
        plan.append((pos, bit, count, [([operand(a) for a in src[0]], *src[1:]) for src in sources]))
        shape = (count, per, sum(src[4] for src in sources))
        outs += [(whole(*shape), shape, BF)] * 2
    pairs = [tuple(operand(a) for a in pair) for pair in sums]
    outs += [(whole(*pair[0].shape), pair[0].shape, BF) for pair in sums]
    got = call(
        functools.partial(combine_kernel, plan=plan, n_in=len(arrays), sums=pairs), 1, [(whole(), a) for a in arrays], outs, [],
        [here], name, after, 4,
    )
    return [(got[2 * n], got[2 * n + 1]) for n in range(len(lanes_in))] + list(got[2 * len(lanes_in) :])


def add_kernel(*refs):
    n = len(refs) // 3
    for i in range(n):
        refs[2 * n + i][...] = (refs[2 * i][...].astype(F32) + refs[2 * i + 1][...].astype(F32)).astype(BF)


def add_pairs(pairs, name, after=()):
    ins = [(whole(*a.shape), a) for pair in pairs for a in pair]
    outs = [(whole(*p[0].shape), p[0].shape, BF) for p in pairs]
    return call(add_kernel, 1, ins, outs, [], [], name, after)


def own_part(row, at, n):
    width = row.shape[1]
    return pltpu.roll(jnp.concatenate([row] * 8, axis=0), (width - at) % width, 1)[0:1, :n]


def finish_kernel(here_ref, *refs, moves, bits, gains, n_out, vectors, ranks):
    lanes_n = len(bits)
    halves, done_ref, refs = refs[: 2 * lanes_n], refs[-1], refs[2 * lanes_n : -1]
    done_ref[...] = jnp.zeros_like(done_ref)
    ins, outs = refs[: len(refs) - n_out], refs[len(refs) - n_out :]
    half = halves[0].shape[0]

    def at(lane, h, cut):
        pick = bit_of(here_ref, *bits[lane]) == h
        return jnp.where(pick, halves[2 * lane][:, cut].astype(F32), halves[2 * lane + 1][:, cut].astype(F32))

    for lane, col, width, out, row, to in moves:
        for h in range(2):
            outs[out][row + h * half : row + (h + 1) * half, to : to + width] = at(lane, h, slice(col, col + width))
    for out, norm, terms in gains:
        acc = 0.0
        for weight, grad in terms:
            product = ins[weight][...].astype(F32) * outs[grad][...]
            ones = jnp.ones((8, product.shape[1]), BF)
            high = product.astype(BF)
            acc = acc + dot(ones, high, NT) + dot(ones, (product - high.astype(F32)).astype(BF), NT)
        per = acc.shape[1]
        outs[out][...] = (acc[0:1] / own_part(ins[norm][...][None], per * here_ref[PLACE], per))[0]
    if vectors:
        lane, col, first_out = vectors
        block = at(lane, 0, slice(col, col + LANES))
        n = outs[first_out].shape[0]
        parts = n * ranks // LANES
        for k in range(2):
            row = jnp.concatenate([block[k * parts + g : k * parts + g + 1] for g in range(parts)], axis=1)
            outs[first_out + k][...] = own_part(row, n * here_ref[RANK], n)[0]


def finish(here, halves, bits, moves, extra, outs, gains, vectors, ranks, name, after=()):
    ins = [(whole(*a.shape), a) for pair in halves for a in pair] + extra
    return call(
        functools.partial(
            finish_kernel, moves=moves, bits=bits, gains=gains, n_out=len(outs), vectors=vectors, ranks=ranks
        ),
        1, ins, [(k(*shape), shape, F32) for k, shape in outs] + [(whole(), (8, LANES), F32)], [], [here], name, after,
    )


def total(parts):
    out = parts[0].astype(F32)
    for p in parts[1:]:
        out = out + p.astype(F32)
    return out.astype(BF)


def halve(parts, dim, axis, n, bit):
    mine = own_bit(axis, bit)
    got = swap(total([lax.dynamic_index_in_dim(p, 1 - mine, dim, keepdims=False) for p in parts]), axis, n, bit)
    return [lax.dynamic_index_in_dim(p, mine, dim, keepdims=False) for p in parts] + [got]


def plain_reduce(parts, bits, ndp, nseq):
    left = sorted(bits, reverse=True)
    for b in bits:
        parts = halve(parts, left.index(b), "dp", ndp, b)
        left.remove(b)
    out = total(parts)
    for b in bits_of(nseq):
        out = total([out, swap(out, "seq", nseq, b)])
    return out.astype(F32)


def local(
    ndp, nseq,
    tokens, init_state, norm_mix, w_in, w_forget, forget_bias, phase, w_ogate,
    norm_group, w_out, norm_ffn, w_gate, w_up, w_down, cotangent,
):
    segs, span, width = tokens.shape
    ch = w_forget.shape[1]
    hidden = w_gate.shape[1]
    count = segs * span
    mine = ch // nseq
    per = width // ndp
    tall = hidden // width
    rank = lax.axis_index("seq").astype(jnp.int32)
    bits = bits_of(ndp)
    first = next(b for b in bits if (per * b) % TILE == 0)
    rest = [b for b in bits if b != first]
    lo = per * first
    scan = rows(span, ch)
    scanned = (scan, (count, ch), F32)
    scan_scratch = [pltpu.VMEM((span, ch), F32)] * 2

    infos, here = call(
        own_kernel, 1, [(whole(), phase), (whole(), init_state.transpose(0, 2, 1))],
        [(whole(), (1 + segs, 2, ch), F32), (("smem",), (2,), jnp.int32)],
        [pltpu.VMEM((-(-(2 + 2 * segs) // 8) * 8, ch), F32)], [], "own",
    )
    infos = shift_all(infos, "seq", nseq)

    col = jnp.arange(width)
    perm = (col[:, None] == 2 * (col % ch)[None, :] + (col // ch)[None, :]).astype(BF)
    member = ((col[:, None] // (width // GROUPS)) == jnp.arange(LANES)[None, :]).astype(BF)

    place_of = jnp.arange(span)
    step_order = ((place_of % CHUNKS) * (span // CHUNKS) + place_of // CHUNKS)[:, None] == place_of[None, :]
    step_order = (whole(span, span), step_order.astype(BF))

    x, normed, normed_t, pre = call(
        functools.partial(project_kernel, lo=lo, first=first), segs,
        [
            (rows(span, width), tokens.reshape(count, width)), (whole(width), norm_mix), (whole(width, width), w_in),
            (whole(width, ch), w_forget), (whole(ch), forget_bias), (whole(width, width), perm), step_order,
        ],
        [
            (rows(span, width), (count, width), BF),
            (rows(span, width), (count, width), BF),
            (cols(width, span), (width, count), BF),
            (seg(span, 3 * ch), (segs, span, 3 * ch), BF),
        ],
        [], [here], "project",
    )
    trig, chunk, totals, lam_re, lam_im, drv_re, drv_im = call(
        functools.partial(summary_kernel, ranks=nseq), segs,
        [(seg(span, 3 * ch), pre)] + [(seg(2, ch, fixed=True), i) for i in infos],
        [
            (whole(2, ch), (2, ch), F32),
            (seg(4, CHUNKS, ch), (segs, 4, CHUNKS, ch), F32),
            (seg(4, ch), (segs, 4, ch), F32),
            scanned, scanned, scanned, scanned,
        ],
        [], [], "summary",
    )
    totals = shift_all(totals, "seq", nseq)
    (og,) = call(
        gate_kernel, 1, [(whole(count, width), normed), (whole(width, width), w_ogate)],
        [(whole(count, width), (count, width), BF)], [], [], "gate", (lam_re,),
    )
    cot, dh = call(
        hidden_grad_kernel, segs,
        [(rows(span, width), cotangent.reshape(count, width)), (whole(hidden, width), w_down), step_order],
        [(rows(span, width), (count, width), BF), (rows(span, hidden), (count, hidden), BF)], [], [], "hidden_grad",
        (lam_re,),
    )
    y, y_split, start, final, gated_t, middle = call(
        functools.partial(mixer_kernel, ranks=nseq, lo=lo, first=first), segs,
        [(seg(4, ch), t) for t in totals]
        + [(seg(2, ch, shift=1), i) for i in infos]
        + [
            (scan, lam_re), (scan, lam_im), (scan, drv_re), (scan, drv_im), (seg(4, CHUNKS, ch), chunk),
            (whole(width, width), perm), (rows(span, width), x), (rows(span, width), og), (whole(width), norm_group),
            (whole(width, LANES), member), (whole(width, width), w_out),
        ],
        [
            (rows(span, width), (count, width), BF),
            (rows(span, width), (count, width), BF),
            (seg(2, ch), (segs, 2, ch), F32),
            (seg(2, mine), (segs, 2, mine), F32),
            (cols(width, span), (width, count), BF),
            (rows(span, width), (count, width), F32),
        ],
        scan_scratch, [here], "mixer",
    )
    final_state = final.transpose(0, 2, 1)

    wide = (count, width)
    done = (whole(), (8, LANES), F32)
    psend, pkeep, normed_ffn, normed_ffn_t, hid0, dgv0, duv0 = call(
        functools.partial(ffn_first_kernel, lo=lo, rt=span, first=first), 1,
        [(whole(), a) for a in (middle, norm_ffn, w_gate, w_up, dh)],
        [(whole(), (width // 2, 2 * width), BF)] * 2
        + [(whole(), wide, BF), (whole(), (width, count), BF)]
        + [(whole(), wide, BF)] * 3,
        [], [here], "ffn_first", (), 7,
    )
    pgot = swap(psend, "dp", ndp, first)
    gsend, gkeep, dsend, dkeep, hid, dn = call(
        functools.partial(ffn_rest_kernel, lo=lo * tall, rt=span, first=first), 1,
        [(whole(), a) for a in (normed_ffn, normed_ffn_t, cot, w_gate, w_up, dh, hid0, dgv0, duv0)],
        [(whole(), (width // 2, 2 * width), BF)] * 2
        + [(whole(), (hidden // 2, width), BF)] * 2
        + [(whole(), wide, BF), (whole(), wide, F32)],
        [pltpu.VMEM(wide, BF), pltpu.VMEM(wide, BF), pltpu.VMEM((tall, width, count), BF)], [here], "ffn_rest", (psend,), 7,
    )
    ggot, dgot = swap(gsend, "dp", ndp, first), swap(dsend, "dp", ndp, first)

    nblk = ndp // 2
    fast = ndp == 8 and nseq == 4 and per % (2 * TILE) == 0
    x_bit, y_bit = (PLACE, rest[0]), (PLACE, rest[1])
    z_bits = [(RANK, b) for b in bits_of(nseq)]

    def blocks(a, cols_n, tall_n=1):
        return a.reshape(nblk * tall_n, per, cols_n)

    order = ()
    if fast:
        p = [blocks(a, 2 * width) for a in (pkeep, pgot)]
        (pa_send, pa_keep), (pb_send, pb_keep) = combine(
            here, [(0, x_bit, [(p, 1, 0, 0, width)]), (1, y_bit, [(p, 1, 0, 1, width)])], "first_sum1", (gkeep,)
        )
        pa_got, pb_got = swap(pa_send, "dp", ndp, rest[0]), swap(pb_send, "dp", ndp, rest[1])
        g = [blocks(a, 2 * width) for a in (gkeep, ggot)]
        d = [blocks(a, width, tall) for a in (dkeep, dgot)]
        (fa_send, fa_keep), (fb_send, fb_keep) = combine(
            here, [(0, x_bit, [(g, 1, 0, 0, 2 * width)]), (1, y_bit, [(d, tall, i, 0, width) for i in range(tall)])],
            "ffn_sum1", (pa_keep,),
        )
        fa_got, fb_got = swap(fa_send, "dp", ndp, rest[0]), swap(fb_send, "dp", ndp, rest[1])
        order = (fa_keep,)

    dmiddle, dbranch, dog, dy_split = call(
        turn_kernel, segs,
        [
            (rows(span, width), dn), (rows(span, width), middle), (rows(span, width), cot), (whole(width), norm_ffn),
            (whole(width, width), w_out), (rows(span, width), y), (rows(span, width), og), (whole(width), norm_group),
            (whole(width, LANES), member), (whole(width, width), perm),
        ],
        [
            (rows(span, width), (count, width), F32),
            (rows(span, width), (count, width), BF),
            (rows(span, width), (count, width), BF),
            (rows(span, width), (count, width), BF),
        ],
        [], [], "turn", order,
    )
    order = ()
    if fast:
        pa, pb = add_pairs([(pa_keep, pa_got), (pb_keep, pb_got)], "first_sum2", (dog,))
        order = (pa,)

    chain, adj = call(
        chains_kernel, segs,
        [(rows(span, width), dy_split), (scan, lam_re), (scan, lam_im), (seg(4, CHUNKS, ch), chunk)],
        [(seg(2, CHUNKS, ch), (segs, 2, CHUNKS, ch), F32), (seg(2, ch), (segs, 2, ch), F32)],
        scan_scratch, [], "chains", order,
    )
    adjs = shift_all(adj, "seq", nseq)
    ntile = width // 3
    osend, okeep = call(
        functools.partial(grads_kernel, pairs=2), width // ntile,
        [
            (whole(width, count), normed_t), (cols(count, ntile), dog),
            (whole(width, count), gated_t), (cols(count, ntile), dbranch),
        ],
        [
            (cols(width // 2, 2 * ntile), (width // 2, 2 * width), BF),
            (cols(width // 2, 2 * ntile), (width // 2, 2 * width), BF),
        ],
        [], [], "mixer_grads", (chain,),
    )
    late, *adjs = lax.optimization_barrier((osend, *adjs))
    ogot = swap(late, "dp", ndp, first)
    order = ()
    if fast:
        def one(keep, got):
            return [([keep, got], 1, 0, 0, keep.shape[2])]

        def rows_of(keep, got):
            return one(*(a.reshape(2, per // 2, a.shape[2]) for a in (keep, got)))

        (fa_send, fa_keep), (fb_send, fb_keep) = combine(
            here,
            [
                (0, y_bit, [([pa], 1, 0, 0, width)] + one(fa_keep, fa_got)),
                (0, x_bit, [([pb], 1, 0, 0, width)] + one(fb_keep, fb_got)),
            ],
            "ffn_sum2", (osend, *adjs),
        )
        fa_got, fb_got = swap(fa_send, "dp", ndp, rest[1]), swap(fb_send, "dp", ndp, rest[0])
        order = (fa_keep,)

    dpre, sums = call(
        functools.partial(adjoint_kernel, ranks=nseq), segs,
        [(seg(4, ch), t) for t in totals] + [(seg(2, ch), a) for a in adjs]
        + [
            (seg(span, 3 * ch), pre), (whole(2, ch), trig), (scan, lam_re), (scan, lam_im),
            (rows(span, width), dy_split),
            (rows(span, width), y_split), (seg(2, ch), start),
            (seg(4, CHUNKS, ch), chunk), (seg(2, CHUNKS, ch), chain), (whole(width, width), perm),
        ],
        [(rows(span, 3 * ch), (count, 3 * ch), BF), (whole(2, ch), (2, ch), F32)],
        scan_scratch, [here], "adjoint", order,
    )
    into = 3 * ch + LANES
    isend, ikeep = call(
        functools.partial(input_grads_kernel, per=per), 1,
        [(whole(width, count), normed_t), (whole(count, 3 * ch), dpre), (whole(2, ch), sums)],
        [(whole(width // 2, into), (width // 2, into), BF)] * 2, [], [], "input_grads",
    )
    igot = swap(isend, "dp", ndp, first)
    order = ()
    if fast:
        lead, other = bits_of(nseq)

        def over(send, axis_n, bit):
            return swap(send, "seq", axis_n, bit)

        (fa_send, fa_keep), (fb_send, fb_keep) = combine(
            here, [(0, z_bits[0], rows_of(fa_keep, fa_got)), (0, z_bits[1], rows_of(fb_keep, fb_got))],
            "ffn_sum3", (isend,),
        )
        fa_got, fb_got = over(fa_send, nseq, lead), over(fb_send, nseq, other)
        o = [blocks(a, 2 * width) for a in (okeep, ogot)]
        i = [blocks(a, into) for a in (ikeep, igot)]
        (ra_send, ra_keep), (rb_send, rb_keep) = combine(
            here, [(0, x_bit, [(o, 1, 0, 0, 2 * width)]), (1, y_bit, [(i, 1, 0, 0, into)])], "mixer_sum1", (fa_keep,)
        )
        ra_got, rb_got = swap(ra_send, "dp", ndp, rest[0]), swap(rb_send, "dp", ndp, rest[1])
        order = (ra_keep,)

    grad_tokens, tokens_done = call(
        tokens_kernel, segs,
        [
            (rows(span, 3 * ch), dpre), (rows(span, width), dog), (whole(width, width), w_in),
            (whole(width, ch), w_forget), (whole(width, width), w_ogate), (rows(span, width), x),
            (whole(width), norm_mix), (rows(span, width), dmiddle), step_order,
        ],
        [(moved(span, width, dim=0), (count, width), BF), done],
        [], [], "tokens", order,
    )

    def output(*after):
        return call(
            out_kernel, segs,
            [(rows(span, width), a) for a in (middle, hid0, hid)] + [(whole(hidden, width), w_down), step_order],
            [(moved(span, width, dim=0), (count, width), BF), done], [], [], "out", after,
        )

    if fast:
        fa, fb = add_pairs([(fa_keep, fa_got), (fb_keep, fb_got)], "ffn_sum4", (tokens_done,))
        fa_got, fb_got = over(fa, nseq, other), over(fb, nseq, lead)
        (ra_send, ra_keep), (rb_send, rb_keep) = combine(
            here, [(0, y_bit, one(ra_keep, ra_got)), (0, x_bit, one(rb_keep, rb_got))], "mixer_sum2", (fa,)
        )
        ra_got, rb_got = swap(ra_send, "dp", ndp, rest[1]), swap(rb_send, "dp", ndp, rest[0])
        mixed_out, out_done = output(ra_keep)
        (ra_send, ra_keep), (rb_send, rb_keep) = combine(
            here, [(0, z_bits[0], rows_of(ra_keep, ra_got)), (0, z_bits[1], rows_of(rb_keep, rb_got))], "mixer_sum3", (out_done,)
        )
        ra_got, rb_got = over(ra_send, nseq, lead), over(rb_send, nseq, other)
        fa, fb = add_pairs([(fa, fa_got), (fb, fb_got)], "ffn_sum5", (ra_keep,))
        fa_got, fb_got = over(fa, nseq, lead), over(fb, nseq, other)
        ra, rb = add_pairs([(ra_keep, ra_got), (rb_keep, rb_got)], "mixer_sum4", (fa,))
        ra_got, rb_got = over(ra, nseq, other), over(rb, nseq, lead)

        def flat(*pairs):
            return [tuple(a.reshape(per // 2, a.shape[2]) for a in pair) for pair in pairs]

        moves = [(0, 0, width, 0, 0, 0), (0, width, width, 0, 0, width), (0, 2 * width, width, 1, 0, width)]
        moves += [(1, 0, width, 1, 0, 0)] + [(1, (1 + t) * width, width, 2, t * per, 0) for t in range(tall)]
        part_gate, part_up, part_down, part_ffn, ffn_done = finish(
            here, flat((fa, fa_got), (fb, fb_got)), z_bits, moves,
            [(ours(per, hidden), w_gate), (ours(per, hidden), w_up), (whole(width), norm_ffn)],
            [(full, (per, hidden)), (full, (per, hidden)), (full, (tall * per, width)), (full, (per,))],
            [(3, 2, [(0, 0), (1, 1)])], None, nseq, "ffn_out", (ra,),
        )
        ra, rb = add_pairs([(ra, ra_got), (rb, rb_got)], "mixer_sum5", (ffn_done,))
        ra_got, rb_got = over(ra, nseq, lead), over(rb, nseq, other)
        moves = [(0, n * ntile, ntile, n % 2, 0, (n // 2) * ntile) for n in range(2 * width // ntile)]
        moves += [(1, 0, width, 2, 0, 0), (1, width, ch, 3, 0, 0)]
        part_ogate, part_out, part_in, part_forget, part_mix, part_group, part_bias, part_phase, _ = finish(
            here, flat((ra, ra_got), (rb, rb_got)), z_bits, moves,
            [
                (ours(per, width), w_ogate), (ours(per, width), w_out), (ours(per, width), w_in), (ours(per, ch), w_forget),
                (whole(width), norm_mix), (whole(width), norm_group),
            ],
            [(full, (per, n)) for n in (width, width, width, ch)] + [(full, (n,)) for n in (per, per, mine, mine)],
            [(4, 4, [(0, 0), (2, 2), (3, 3)]), (5, 5, [(1, 1)])], (1, 3 * ch, 6), nseq, "mixer_out",
        )
    else:
        mixed_out, _ = output()

        def plain(keep, got, cols_n, tall_n=1):
            shape = [2] * len(rest) + [tall_n * per, cols_n]
            return plain_reduce([keep.reshape(shape), got.reshape(shape)], rest, ndp, nseq)

        guv = [plain(pkeep, pgot, 2 * width), plain(gkeep, ggot, 2 * width)]
        part_gate = jnp.concatenate([a[:, :width] for a in guv], axis=1)
        part_up = jnp.concatenate([a[:, width:] for a in guv], axis=1)
        part_down = plain(dkeep, dgot, width, tall)
        mix = plain(okeep, ogot, 2 * width)
        mix = [mix[:, n * ntile : (n + 1) * ntile] for n in range(2 * width // ntile)]
        part_ogate, part_out = jnp.concatenate(mix[0::2], axis=1), jnp.concatenate(mix[1::2], axis=1)
        both = plain(ikeep, igot, into)
        part_in, part_forget = both[:, :width], both[:, width : 3 * ch]
        shared = both[: 2 * ch // LANES, 3 * ch :].reshape(2, ch)
        part_bias, part_phase = lax.dynamic_slice_in_dim(shared, rank * mine, mine, axis=1)

        def own_rows(a):
            return lax.dynamic_slice_in_dim(a, lax.axis_index("dp") * per, per, axis=0).astype(F32)

        def gain_of(norm, *pairs):
            return sum(jnp.sum(own_rows(w) * gw, axis=1) for w, gw in pairs) / own_rows(norm)

        part_ffn = gain_of(norm_ffn, (w_gate, part_gate), (w_up, part_up))
        part_mix = gain_of(norm_mix, (w_in, part_in), (w_forget, part_forget), (w_ogate, part_ogate))
        part_group = gain_of(norm_group, (w_out, part_out))
    return (
        mixed_out.reshape(segs, span, width),
        grad_tokens.reshape(segs, span, width),
        final_state,
        part_mix, part_in, part_forget, part_bias, part_phase, part_ogate, part_group, part_out, part_ffn,
        part_gate, part_up, part_down,
    )


def solution(mesh):
    ndp, nseq = mesh.shape["dp"], mesh.shape["seq"]
    tok, vec, col = P("dp", "seq", None), P("dp"), P("dp", None)
    return jax.shard_map(
        functools.partial(local, ndp, nseq),
        mesh=mesh,
        in_specs=(tok, tok, P(), P(), P(), P(), P("seq"), P(), P(), P(), P(), P(), P(), P(), tok),
        out_specs=(tok, tok, tok, vec, col, col, P("seq"), P("seq"), col, vec, col, vec, col, col, col),
        check_vma=False,
    )
```

```python
import functools

import jax
import jax.numpy as jnp
from jax import lax
from jax.experimental import pallas as pl
from jax.experimental.pallas import tpu as pltpu
from jax.sharding import PartitionSpec as P

GROUPS = 8
CHUNKS = 8
LANES = 128
RANK, PLACE = 0, 1
MICROSECONDS = dict(
    project=4, summary=4, hidden_grad=2.5, mixer=8, ffn_first=6, ffn_rest=12, turn=7, chains=0.3, mixer_grads=0.01, adjoint=3.74, input_grads=0.3, tokens=0.3, ffn_sum4=8, out=3.5,
    ffn_sum1=1.3, mixer_sum1=1.0, ffn_sum2=3, ffn_sum3=20,
)
COST = 1.15e9
TILE = 16
epsilon = 1e-06
BF = jnp.bfloat16
F32 = jnp.float32
NT = ((1,), (1,))


def dot(a, b, dims=((1,), (0,))):
    return lax.dot_general(a, b, (dims, ((), ())), preferred_element_type=F32)


def silu_slope(values, logistic):
    return logistic * (1.0 + values * (1.0 - logistic))


def cmul(ar, ai, br, bi):
    return ar * br - ai * bi, ar * bi + ai * br


def row_mean(v):
    return jnp.mean(v, axis=-1, keepdims=True)


def split_dot(v, m, dims):
    high = v.astype(BF)
    low = (v - high.astype(F32)).astype(BF)
    return dot(high, m, dims) + dot(low, m, dims)


def group_mean(v, member):
    return split_dot(v, member, ((1,), (0,))) * (GROUPS / v.shape[1])


def group_spread(v, member):
    return split_dot(v, member, NT)


def bit_of(here_ref, which, bit):
    return lax.shift_right_logical(here_ref[which], bit.bit_length() - 1) & 1


def put_halves(ref, t, col, lo, bit):
    half = ref.shape[0] // 2
    for b in range(t.shape[0] // lo):
        at = jnp.where(bit == b % 2, half, 0) + (b // 2) * lo
        ref[pl.ds(pl.multiple_of(at, TILE), lo), col : col + t.shape[1]] = t[b * lo : (b + 1) * lo, :]


def at_step(t):
    return slice(CHUNKS * t, CHUNKS * (t + 1))


def apart(v, perm_ref):
    n = perm_ref.shape[0]
    parts = [dot(v[:, c : c + n], perm_ref[...]).astype(BF) for c in range(0, v.shape[1], n)]
    return jnp.concatenate([p[:, : n // 2] for p in parts] + [p[:, n // 2 :] for p in parts], axis=1)


def together(re, im, perm_ref):
    n = perm_ref.shape[0] // 2
    parts = [
        dot(jnp.concatenate([re[:, c : c + n], im[:, c : c + n]], axis=1), perm_ref[...], NT)
        for c in range(0, re.shape[1], n)
    ]
    return jnp.concatenate(parts, axis=1)


def reorder(order_ref, v, back=False):
    return dot(order_ref[...], v, ((0,), (0,)) if back else ((1,), (0,))).astype(BF)


def own_kernel(phase_ref, init_ref, infos_ref, here_ref, line_ref):
    own = phase_ref.shape[0]
    rank, place = lax.axis_index("seq"), lax.axis_index("dp")
    here_ref[RANK], here_ref[PLACE] = rank, place
    theta = phase_ref[...][None]
    line_ref[...] = jnp.zeros_like(line_ref)
    line_ref[0:1, :own] = jnp.cos(theta)
    line_ref[1:2, :own] = jnp.sin(theta)
    for n in range(init_ref.shape[0]):
        line_ref[2 + 2 * n : 4 + 2 * n, :own] = init_ref[n]
    placed = pltpu.roll(line_ref[...], own * rank, 1)
    for n in range(infos_ref.shape[0]):
        infos_ref[n] = placed[2 * n : 2 * n + 2, :]


def project_kernel(
    here_ref, x_ref, gain_ref, w_in_ref, w_forget_ref, bias_ref, perm_ref, order_ref, xs_ref, normed_ref, turned_ref,
    pre_ref, *, lo, first
):
    width = x_ref.shape[1]
    xs = reorder(order_ref, x_ref[...])
    xs_ref[...] = xs
    x = xs.astype(F32)
    normed = (x * lax.rsqrt(row_mean(x * x) + epsilon) * gain_ref[...][None]).astype(BF)
    normed_ref[...] = normed
    put_halves(turned_ref, normed.T, 0, lo, bit_of(here_ref, PLACE, first))
    mixed = dot(normed, w_in_ref[...]).astype(BF)
    pre_ref[:, :width] = apart(mixed, perm_ref)
    pre_ref[:, width:] = (dot(normed, w_forget_ref[...]) + bias_ref[...][None]).astype(BF)


def summary_kernel(*refs, ranks):
    pre_ref, infos = refs[0], refs[1 : 1 + ranks]
    trig_ref, chunk_ref, total_ref, lam_re, lam_im, drv_re, drv_im = refs[1 + ranks :]
    span, ch = lam_re.shape
    trig = infos[0][...]
    for info in infos[1:]:
        trig = trig + info[...]
    trig_ref[...] = trig
    pre = pre_ref[...].astype(F32)
    forget = jax.nn.sigmoid(pre[:, 2 * ch :])
    lam_re[...] = forget * trig[0:1, :]
    lam_im[...] = forget * trig[1:2, :]
    drv_re[...] = (1.0 - forget) * jax.nn.silu(pre[:, :ch])
    drv_im[...] = (1.0 - forget) * jax.nn.silu(pre[:, ch : 2 * ch])
    first = at_step(0)
    pr, pi, hr, hi = lam_re[first, :], lam_im[first, :], drv_re[first, :], drv_im[first, :]
    for t in range(1, span // CHUNKS):
        lr, li = lam_re[at_step(t), :], lam_im[at_step(t), :]
        pr, pi = cmul(lr, li, pr, pi)
        hr, hi = cmul(lr, li, hr, hi)
        hr, hi = hr + drv_re[at_step(t), :], hi + drv_im[at_step(t), :]
    chunk_ref[0], chunk_ref[1], chunk_ref[2], chunk_ref[3] = pr, pi, hr, hi
    tp_r, tp_i, th_r, th_i = pr[0:1], pi[0:1], hr[0:1], hi[0:1]
    for k in range(1, CHUNKS):
        lr, li = pr[k : k + 1], pi[k : k + 1]
        th_r, th_i = cmul(lr, li, th_r, th_i)
        th_r, th_i = th_r + hr[k : k + 1], th_i + hi[k : k + 1]
        tp_r, tp_i = cmul(lr, li, tp_r, tp_i)
    total_ref[...] = jnp.concatenate([tp_r, tp_i, th_r, th_i], axis=0)


def mixer_kernel(*refs, ranks, lo, first):
    scalars, refs = refs[0], refs[1:]
    totals, inits, refs = refs[:ranks], refs[ranks : 2 * ranks], refs[2 * ranks :]
    lam_re, lam_im, drv_re, drv_im, chunk_ref, perm_ref, x_ref, og_ref, gain_ref, member_ref, w_out_ref = refs[:11]
    y_ref, split_ref, start_ref, final_ref, turned_ref, middle_ref, st_re, st_im = refs[11:]
    span, ch = lam_re.shape
    rank, bit = scalars[RANK], bit_of(scalars, PLACE, first)
    init = inits[0][...]
    for info in inits[1:]:
        init = init + info[...]
    cr, ci = init[0:1], init[1:2]

    def after(k, cr, ci, take):
        total = totals[k][...]
        nr, ni = cmul(total[0:1], total[1:2], cr, ci)
        nr, ni = nr + total[2:3], ni + total[3:4]
        return jnp.where(take, nr, cr), jnp.where(take, ni, ci)

    for k in range(ranks - 1, 0, -1):
        cr, ci = after(k, cr, ci, k <= rank)
    start_ref[...] = jnp.concatenate([cr, ci], axis=0)
    er, ei = after(0, cr, ci, rank >= 0)
    for k in range(ranks - 1, 0, -1):
        er, ei = after(k, er, ei, k > rank)
    own = ch // ranks
    final_ref[...] = pltpu.roll(jnp.concatenate([er, ei] * 4, axis=0), (ch - own * rank) % ch, 1)[:2, :own]
    rows_r, rows_i = [cr], [ci]
    for k in range(CHUNKS - 1):
        cr, ci = cmul(chunk_ref[0, k : k + 1, :], chunk_ref[1, k : k + 1, :], cr, ci)
        cr, ci = cr + chunk_ref[2, k : k + 1, :], ci + chunk_ref[3, k : k + 1, :]
        rows_r.append(cr)
        rows_i.append(ci)
    hr, hi = jnp.concatenate(rows_r, axis=0), jnp.concatenate(rows_i, axis=0)
    for t in range(span // CHUNKS):
        hr, hi = cmul(lam_re[at_step(t), :], lam_im[at_step(t), :], hr, hi)
        hr, hi = hr + drv_re[at_step(t), :], hi + drv_im[at_step(t), :]
        st_re[at_step(t), :] = hr
        st_im[at_step(t), :] = hi
    re, im = st_re[...].astype(BF), st_im[...].astype(BF)
    split_ref[:, :ch], split_ref[:, ch:] = re, im
    yf = together(re, im, perm_ref)
    y_ref[...] = yf.astype(BF)
    member = member_ref[...]
    inv = group_spread(lax.rsqrt(group_mean(yf * yf, member) + epsilon), member)
    gated = (yf * inv * gain_ref[...][None] * jax.nn.silu(og_ref[...].astype(F32))).astype(BF)
    put_halves(turned_ref, gated.T, 0, lo, bit)
    middle_ref[...] = x_ref[...].astype(F32) + dot(gated, w_out_ref[...])


def hidden_tile(n_ref, rows, cut, wg_ref, wu_ref, dh_ref, hid_ref, dgv_ref, duv_ref, to):
    g, u = dot(n_ref[rows, :], wg_ref[:, cut]), dot(n_ref[rows, :], wu_ref[:, cut])
    dh = dh_ref[rows, cut].astype(F32)
    sig = jax.nn.sigmoid(g)
    act = g * sig
    hid_ref[rows, to] = (act * u).astype(BF)
    dgv_ref[rows, to] = (dh * u * silu_slope(g, sig)).astype(BF)
    duv_ref[rows, to] = (dh * act).astype(BF)


def two_halves(lhs_ref, rhs, send_ref, keep_ref, to):
    half = lhs_ref.shape[0] // 2
    send_ref[:, to] = dot(lhs_ref[:half, :], rhs).astype(BF)
    keep_ref[:, to] = dot(lhs_ref[half:, :], rhs).astype(BF)


def ffn_first_kernel(
    here_ref, middle_ref, gain_ref, wg_ref, wu_ref, dh_ref,
    gsend_ref, gkeep_ref, n_ref, nt_ref, hid_ref, dgv_ref, duv_ref,
    *, lo, rt, first,
):
    bit = bit_of(here_ref, PLACE, first)
    count, width = middle_ref.shape
    cut = slice(0, width)
    for r in range(0, count, rt):
        rows = slice(r, r + rt)
        v = middle_ref[rows, :]
        normed = (v * lax.rsqrt(row_mean(v * v) + epsilon) * gain_ref[...][None]).astype(BF)
        n_ref[rows, :] = normed
        put_halves(nt_ref, normed.T, r, lo, bit)
        hidden_tile(n_ref, rows, cut, wg_ref, wu_ref, dh_ref, hid_ref, dgv_ref, duv_ref, cut)
    two_halves(nt_ref, dgv_ref[...], gsend_ref, gkeep_ref, cut)
    two_halves(nt_ref, duv_ref[...], gsend_ref, gkeep_ref, slice(width, 2 * width))


def ffn_rest_kernel(
    here_ref, n_ref, nt_ref, cot_ref, wg_ref, wu_ref, dh_ref, hid0_ref,
    gsend_ref, gkeep_ref, dsend_ref, dkeep_ref, hid_ref, dgv_ref, duv_ref,
    ht_ref,
    *, lo, rt, first,
):
    bit = bit_of(here_ref, PLACE, first)
    count, width = n_ref.shape
    spans = [slice(r, r + rt) for r in range(0, count, rt)]
    cut, own = slice(width, 2 * width), slice(0, width)
    for rows in spans:
        hidden_tile(n_ref, rows, cut, wg_ref, wu_ref, dh_ref, hid_ref, dgv_ref, duv_ref, own)
    two_halves(nt_ref, dgv_ref[...], gsend_ref, gkeep_ref, own)
    two_halves(nt_ref, duv_ref[...], gsend_ref, gkeep_ref, cut)
    half = width // 2
    for j, ref in enumerate((hid0_ref, hid_ref)):
        for rows in spans:
            put_halves(ht_ref.at[j], ref[rows, :].T, rows.start, lo, bit)
    for j in range(2):
        out = slice(j * half, (j + 1) * half)
        dsend_ref[out, :] = dot(ht_ref[j, :half, :], cot_ref[...]).astype(BF)
        dkeep_ref[out, :] = dot(ht_ref[j, half:, :], cot_ref[...]).astype(BF)


def ffn_back_kernel(dgv0_ref, duv0_ref, dgv_ref, duv_ref, wg_ref, wu_ref, dn_ref):
    width = dn_ref.shape[1]
    own, cut = slice(0, width), slice(width, 2 * width)
    dn_ref[...] = (
        dot(dgv0_ref[...], wg_ref[:, own], NT)
        + dot(duv0_ref[...], wu_ref[:, own], NT)
        + dot(dgv_ref[...], wg_ref[:, cut], NT)
        + dot(duv_ref[...], wu_ref[:, cut], NT)
    )


def gate_kernel(normed_ref, w_ref, og_ref):
    og_ref[...] = dot(normed_ref[...], w_ref[...]).astype(BF)


def hidden_grad_kernel(cot_ref, wd_ref, order_ref, cots_ref, dh_ref):
    cots = reorder(order_ref, cot_ref[...])
    cots_ref[...] = cots
    dh_ref[...] = dot(cots, wd_ref[...], NT).astype(BF)


def turn_kernel(
    dn_ref, middle_ref, cot_ref, ffn_gain_ref, w_out_ref, y_ref, og_ref, gain_ref, member_ref, perm_ref,
    dmiddle_ref, dbranch_ref, dog_ref, split_ref,
):
    v, up = middle_ref[...], dn_ref[...]
    inv = lax.rsqrt(row_mean(v * v) + epsilon)
    unit = v * inv
    through = up * ffn_gain_ref[...][None]
    dmiddle = cot_ref[...].astype(F32) + inv * (through - unit * row_mean(through * unit))
    dmiddle_ref[...] = dmiddle
    dbranch = dmiddle.astype(BF)
    dbranch_ref[...] = dbranch
    dgated = dot(dbranch, w_out_ref[...], NT)
    og, yf, member, gain = og_ref[...].astype(F32), y_ref[...].astype(F32), member_ref[...], gain_ref[...][None]
    ginv = group_spread(lax.rsqrt(group_mean(yf * yf, member) + epsilon), member)
    gunit = yf * ginv
    sig = jax.nn.sigmoid(og)
    dog_ref[...] = (dgated * gunit * gain * silu_slope(og, sig)).astype(BF)
    through = dgated * og * sig * gain
    dy = (ginv * (through - gunit * group_spread(group_mean(through * gunit, member), member))).astype(BF)
    split_ref[...] = apart(dy, perm_ref)


def chains_kernel(split_ref, lam_re, lam_im, chunk_ref, chain_ref, total_ref, dy_re, dy_im):
    span, ch = lam_re.shape
    dy_re[...] = split_ref[:, :ch].astype(F32)
    dy_im[...] = split_ref[:, ch:].astype(F32)
    last = span // CHUNKS - 1
    gr, gi = dy_re[at_step(last), :], dy_im[at_step(last), :]
    ar, ai = cmul(lam_re[at_step(last), :], -lam_im[at_step(last), :], gr, gi)
    for t in range(last - 1, -1, -1):
        gr, gi = dy_re[at_step(t), :] + ar, dy_im[at_step(t), :] + ai
        ar, ai = cmul(lam_re[at_step(t), :], -lam_im[at_step(t), :], gr, gi)
    chain_ref[0], chain_ref[1] = ar, ai
    er, ei = ar[CHUNKS - 1 :], ai[CHUNKS - 1 :]
    for k in range(CHUNKS - 2, -1, -1):
        er, ei = cmul(chunk_ref[0, k : k + 1, :], -chunk_ref[1, k : k + 1, :], er, ei)
        er, ei = er + ar[k : k + 1], ei + ai[k : k + 1]
    total_ref[...] = jnp.concatenate([er, ei], axis=0)


def adjoint_kernel(*refs, ranks):
    scalars, refs = refs[0], refs[1:]
    totals, adjs, refs = refs[:ranks], refs[ranks : 2 * ranks], refs[2 * ranks :]
    pre_ref, trig_ref, lam_re, lam_im, dy_ref, split_ref, start_ref, chunk_ref, chain_ref, perm_ref = refs[:10]
    dpre_ref, sums_ref, dy_re, dy_im = refs[10:]
    span, ch = lam_re.shape
    rank = scalars[RANK]
    pre = pre_ref[...].astype(F32)
    trig = trig_ref[...]
    forget = jax.nn.sigmoid(pre[:, 2 * ch :])
    dy_re[...] = dy_ref[:, :ch].astype(F32)
    dy_im[...] = dy_ref[:, ch:].astype(F32)
    cr = jnp.zeros((1, ch), F32)
    ci = jnp.zeros((1, ch), F32)
    for k in range(1, ranks):
        total, adj = totals[k][...], adjs[k][...]
        nr, ni = cmul(total[0:1], -total[1:2], cr, ci)
        nr, ni = nr + adj[0:1], ni + adj[1:2]
        cr, ci = jnp.where(k > rank, nr, cr), jnp.where(k > rank, ni, ci)
    rows_r, rows_i = [cr], [ci]
    for k in range(CHUNKS - 1, 0, -1):
        cr, ci = cmul(chunk_ref[0, k : k + 1, :], -chunk_ref[1, k : k + 1, :], cr, ci)
        cr, ci = cr + chain_ref[0, k : k + 1, :], ci + chain_ref[1, k : k + 1, :]
        rows_r.append(cr)
        rows_i.append(ci)
    ar, ai = jnp.concatenate(rows_r[::-1], axis=0), jnp.concatenate(rows_i[::-1], axis=0)
    for t in range(span // CHUNKS - 1, -1, -1):
        gr, gi = dy_re[at_step(t), :] + ar, dy_im[at_step(t), :] + ai
        dy_re[at_step(t), :] = gr
        dy_im[at_step(t), :] = gi
        ar, ai = cmul(lam_re[at_step(t), :], -lam_im[at_step(t), :], gr, gi)
    gr, gi = dy_re[...], dy_im[...]

    def before(states, start):
        ends = pltpu.roll(states[span - CHUNKS :, :], 1, 0)
        ends = jnp.where(lax.broadcasted_iota(jnp.int32, ends.shape, 0) == 0, start, ends)
        return jnp.concatenate([ends, states[: span - CHUNKS, :]], axis=0)

    qr = before(split_ref[:, :ch].astype(F32), start_ref[0:1, :])
    qi = before(split_ref[:, ch:].astype(F32), start_ref[1:2, :])
    pin_re, pin_im = pre[:, :ch], pre[:, ch : 2 * ch]
    sig_re, sig_im = jax.nn.sigmoid(pin_re), jax.nn.sigmoid(pin_im)
    lr = gr * qr + gi * qi
    li = gi * qr - gr * qi
    turned_re = lr * trig[0:1, :] + li * trig[1:2, :]
    turned_im = li * trig[0:1, :] - lr * trig[1:2, :]
    df = turned_re - (gr * pin_re * sig_re + gi * pin_im * sig_im)
    keep = 1.0 - forget
    dre = (keep * gr * silu_slope(pin_re, sig_re)).astype(BF)
    dim = (keep * gi * silu_slope(pin_im, sig_im)).astype(BF)
    dpz = (forget * keep * df).astype(BF)
    dpre_ref[:, : 2 * ch] = together(dre, dim, perm_ref).astype(BF)
    dpre_ref[:, 2 * ch :] = dpz
    sums = jnp.concatenate(
        [
            jnp.sum(dpz.astype(F32), axis=0, keepdims=True),
            jnp.sum(forget * turned_im, axis=0, keepdims=True),
        ],
        axis=0,
    )

    @pl.when(pl.program_id(0) == 0)
    def _():
        sums_ref[...] = sums

    @pl.when(pl.program_id(0) > 0)
    def _():
        sums_ref[...] += sums


def grads_kernel(*refs, pairs):
    ins, (send_ref, keep_ref) = refs[: 2 * pairs], refs[2 * pairs :]
    at = 0
    for p in range(pairs):
        lhs_ref, rhs_ref = ins[2 * p], ins[2 * p + 1]
        half, n = lhs_ref.shape[0] // 2, rhs_ref.shape[1]
        send_ref[:, at : at + n] = dot(lhs_ref[:half, :], rhs_ref[...]).astype(BF)
        keep_ref[:, at : at + n] = dot(lhs_ref[half:, :], rhs_ref[...]).astype(BF)
        at += n


def out_kernel(middle_ref, hid0_ref, hid_ref, w_down_ref, order_ref, out_ref, done_ref):
    width = middle_ref.shape[1]
    branch = dot(hid0_ref[...], w_down_ref[:width, :]) + dot(hid_ref[...], w_down_ref[width:, :])
    out = (middle_ref[...] + branch).astype(BF)
    out_ref[...] = reorder(order_ref, out, True)
    done_ref[...] = jnp.zeros_like(done_ref)


def input_grads_kernel(lhs_ref, dpre_ref, sums_ref, send_ref, keep_ref, *, per):
    half, n = lhs_ref.shape[0] // 2, dpre_ref.shape[1]
    send_ref[:, :n] = dot(lhs_ref[:half, :], dpre_ref[...]).astype(BF)
    keep_ref[:, :n] = dot(lhs_ref[half:, :], dpre_ref[...]).astype(BF)
    parts = n // 3 // LANES
    flat = [sums_ref[k : k + 1, g * LANES : (g + 1) * LANES] for k in range(2) for g in range(parts)]
    flat.append(jnp.zeros((-2 * parts % 8, LANES), F32))
    flat = jnp.concatenate(flat, axis=0).astype(BF)
    shape = (half, flat.shape[0])
    row, k = lax.broadcasted_iota(jnp.int32, shape, 0), lax.broadcasted_iota(jnp.int32, shape, 1)
    beside = dot((row % per == k).astype(F32).astype(BF), flat).astype(BF)
    send_ref[:, n:] = beside
    keep_ref[:, n:] = beside


def tokens_kernel(
    dpre_ref, dog_ref, w_in_ref, w_forget_ref, w_ogate_ref, x_ref, gain_ref, dmiddle_ref, order_ref, out_ref, done_ref
):
    width = x_ref.shape[1]
    up = (
        dot(dpre_ref[:, :width], w_in_ref[...], NT)
        + dot(dpre_ref[:, width:], w_forget_ref[...], NT)
        + dot(dog_ref[...], w_ogate_ref[...], NT)
    )
    x = x_ref[...].astype(F32)
    inv = lax.rsqrt(row_mean(x * x) + epsilon)
    unit = x * inv
    through = up * gain_ref[...][None]
    out = (dmiddle_ref[...] + inv * (through - unit * row_mean(through * unit))).astype(BF)
    out_ref[...] = reorder(order_ref, out, True)
    done_ref[...] = jnp.zeros_like(done_ref)


def rows(*shape):
    return ("rows", shape)


def cols(*shape):
    return ("cols", shape)


def seg(*shape, shift=0, fixed=False):
    return ("seg", shape, shift, fixed)


def whole(*shape):
    return ("whole", shape)


def moved(*shape, dim):
    return ("moved", shape, dim)


def ours(*shape):
    return ("own", shape)


def full(*shape):
    return ("full", shape)


def spec_of(kind):
    if kind[0] == "smem":
        return pl.BlockSpec(memory_space=pltpu.SMEM)
    if kind[0] == "full":
        return pl.BlockSpec(kind[1], lambda s, *_: (0,) * len(kind[1]))
    if kind[0] == "own":
        return pl.BlockSpec(kind[1], lambda s, here: (here[PLACE], 0))
    if kind[0] not in ("moved",):
        return pl.BlockSpec(memory_space=pltpu.VMEM)
    _, shape, dim = kind
    return pl.BlockSpec(shape, lambda s, *_: tuple(s if d == dim else 0 for d in range(len(shape))))


def view_of(kind, ref):
    step = pl.program_id(0)
    if kind[0] == "rows":
        n = kind[1][0]
        return ref.at[pl.ds(pl.multiple_of(step * n, n), n)]
    if kind[0] == "cols":
        n = kind[1][1]
        return ref.at[:, pl.ds(pl.multiple_of(step * n, n), n)]
    if kind[0] == "seg":
        return ref.at[kind[2] if kind[3] else step + kind[2]]
    return ref


def size_of(shape, dtype):
    return functools.reduce(lambda p, q: p * q, shape) * jnp.dtype(dtype).itemsize


def call(kernel, steps, ins, outs, scratch, scalars, name, after=(), room=5):
    cost = int(COST * MICROSECONDS.get(name, 0.8))
    lead, extra = len(scalars), len(after)
    kinds_in, kinds_out = [k for k, _ in ins], [k for k, _, _ in outs]

    def body(*refs):
        given, refs = refs[: lead + len(ins)], refs[lead + len(ins) + extra :]
        kernel(
            *given[:lead],
            *[view_of(k, r) for k, r in zip(kinds_in, given[lead:], strict=True)],
            *[view_of(k, r) for k, r in zip(kinds_out, refs[: len(outs)], strict=True)],
            *refs[len(outs) :],
        )

    limit = room << 20
    limit += sum(2 * size_of(k[1], a.dtype) for k, a in ins if k[0] in ("moved", "own"))
    limit += sum(2 * size_of(k[1], d) for k, _, d in outs if k[0] in ("moved", "full"))
    limit += sum(size_of(m.shape, m.dtype) for m in scratch)
    return pl.pallas_call(
        body,
        grid_spec=pltpu.PrefetchScalarGridSpec(
            num_scalar_prefetch=lead,
            grid=(steps,),
            in_specs=[spec_of(k) for k in kinds_in] + [pl.BlockSpec(memory_space=pl.ANY)] * extra,
            out_specs=[spec_of(k) for k in kinds_out],
            scratch_shapes=scratch,
        ),
        out_shape=[jax.ShapeDtypeStruct(s, d) for _, s, d in outs],
        compiler_params=pltpu.CompilerParams(vmem_limit_bytes=limit),
        cost_estimate=pl.CostEstimate(flops=cost, bytes_accessed=1, transcendentals=0),
        name=name,
    )(*scalars, *[a for _, a in ins], *after)


def shift_all(payload, axis, n):
    return [payload] + [lax.ppermute(payload, axis, [(i, (i + k) % n) for i in range(n)]) for k in range(1, n)]


def own_bit(axis, bit):
    return lax.shift_right_logical(lax.axis_index(axis).astype(jnp.int32), jnp.int32(bit.bit_length() - 1)) & 1


def swap(v, axis, n, bit):
    return lax.ppermute(v, axis, [(i, i ^ bit) for i in range(n)])


def bits_of(n):
    return [1 << i for i in range((n - 1).bit_length())]


def combine_kernel(here_ref, *refs, plan, n_in, sums):
    ins, outs = refs[:n_in], refs[n_in:]
    for n, (a, b) in enumerate(sums):
        outs[2 * len(plan) + n][...] = (ins[a][...].astype(F32) + ins[b][...].astype(F32)).astype(BF)
    for n, (pos, bit, count, sources) in enumerate(plan):
        for flip in (1, 0):
            own = 1 - bit_of(here_ref, *bit) if flip else bit_of(here_ref, *bit)
            for i in range(count):
                low = i % (1 << pos)
                q = (i - low) * 2 + own * (1 << pos) + low
                at = 0
                for addends, mult, off, col, width in sources:
                    cut = slice(col * width, (col + 1) * width)
                    acc = ins[addends[0]][q * mult + off, :, cut].astype(F32)
                    for k in addends[1:]:
                        acc = acc + ins[k][q * mult + off, :, cut].astype(F32)
                    outs[2 * n + 1 - flip][i, :, at : at + width] = acc.astype(BF)
                    at += width


def combine(here, lanes_in, name, after=(), sums=()):
    arrays, outs, plan = [], [], []

    def operand(a):
        for k, b in enumerate(arrays):
            if a is b:
                return k
        arrays.append(a)
        return len(arrays) - 1

    for pos, bit, sources in lanes_in:
        addends, mult = sources[0][0], sources[0][1]
        per, count = addends[0].shape[1], addends[0].shape[0] // mult // 2
        plan.append((pos, bit, count, [([operand(a) for a in src[0]], *src[1:]) for src in sources]))
        shape = (count, per, sum(src[4] for src in sources))
        outs += [(whole(*shape), shape, BF)] * 2
    pairs = [tuple(operand(a) for a in pair) for pair in sums]
    outs += [(whole(*pair[0].shape), pair[0].shape, BF) for pair in sums]
    got = call(
        functools.partial(combine_kernel, plan=plan, n_in=len(arrays), sums=pairs), 1, [(whole(), a) for a in arrays], outs, [],
        [here], name, after, 4,
    )
    return [(got[2 * n], got[2 * n + 1]) for n in range(len(lanes_in))] + list(got[2 * len(lanes_in) :])


def add_kernel(*refs):
    n = len(refs) // 3
    for i in range(n):
        refs[2 * n + i][...] = (refs[2 * i][...].astype(F32) + refs[2 * i + 1][...].astype(F32)).astype(BF)


def add_pairs(pairs, name, after=()):
    ins = [(whole(*a.shape), a) for pair in pairs for a in pair]
    outs = [(whole(*p[0].shape), p[0].shape, BF) for p in pairs]
    return call(add_kernel, 1, ins, outs, [], [], name, after)


def own_part(row, at, n):
    width = row.shape[1]
    return pltpu.roll(jnp.concatenate([row] * 8, axis=0), (width - at) % width, 1)[0:1, :n]


def finish_kernel(here_ref, *refs, moves, bits, gains, n_out, vectors, ranks):
    lanes_n = len(bits)
    halves, done_ref, refs = refs[: 2 * lanes_n], refs[-1], refs[2 * lanes_n : -1]
    done_ref[...] = jnp.zeros_like(done_ref)
    ins, outs = refs[: len(refs) - n_out], refs[len(refs) - n_out :]
    half = halves[0].shape[0]

    def at(lane, h, cut):
        pick = bit_of(here_ref, *bits[lane]) == h
        return jnp.where(pick, halves[2 * lane][:, cut].astype(F32), halves[2 * lane + 1][:, cut].astype(F32))

    for lane, col, width, out, row, to in moves:
        for h in range(2):
            outs[out][row + h * half : row + (h + 1) * half, to : to + width] = at(lane, h, slice(col, col + width))
    for out, norm, terms in gains:
        acc = 0.0
        for weight, grad in terms:
            product = ins[weight][...].astype(F32) * outs[grad][...]
            ones = jnp.ones((8, product.shape[1]), BF)
            high = product.astype(BF)
            acc = acc + dot(ones, high, NT) + dot(ones, (product - high.astype(F32)).astype(BF), NT)
        per = acc.shape[1]
        outs[out][...] = (acc[0:1] / own_part(ins[norm][...][None], per * here_ref[PLACE], per))[0]
    if vectors:
        lane, col, first_out = vectors
        block = at(lane, 0, slice(col, col + LANES))
        n = outs[first_out].shape[0]
        parts = n * ranks // LANES
        for k in range(2):
            row = jnp.concatenate([block[k * parts + g : k * parts + g + 1] for g in range(parts)], axis=1)
            outs[first_out + k][...] = own_part(row, n * here_ref[RANK], n)[0]


def finish(here, halves, bits, moves, extra, outs, gains, vectors, ranks, name, after=()):
    ins = [(whole(*a.shape), a) for pair in halves for a in pair] + extra
    return call(
        functools.partial(
            finish_kernel, moves=moves, bits=bits, gains=gains, n_out=len(outs), vectors=vectors, ranks=ranks
        ),
        1, ins, [(k(*shape), shape, F32) for k, shape in outs] + [(whole(), (8, LANES), F32)], [], [here], name, after,
    )


def total(parts):
    out = parts[0].astype(F32)
    for p in parts[1:]:
        out = out + p.astype(F32)
    return out.astype(BF)


def halve(parts, dim, axis, n, bit):
    mine = own_bit(axis, bit)
    got = swap(total([lax.dynamic_index_in_dim(p, 1 - mine, dim, keepdims=False) for p in parts]), axis, n, bit)
    return [lax.dynamic_index_in_dim(p, mine, dim, keepdims=False) for p in parts] + [got]


def plain_reduce(parts, bits, ndp, nseq):
    left = sorted(bits, reverse=True)
    for b in bits:
        parts = halve(parts, left.index(b), "dp", ndp, b)
        left.remove(b)
    out = total(parts)
    for b in bits_of(nseq):
        out = total([out, swap(out, "seq", nseq, b)])
    return out.astype(F32)


def local(
    ndp, nseq,
    tokens, init_state, norm_mix, w_in, w_forget, forget_bias, phase, w_ogate,
    norm_group, w_out, norm_ffn, w_gate, w_up, w_down, cotangent,
):
    segs, span, width = tokens.shape
    ch = w_forget.shape[1]
    hidden = w_gate.shape[1]
    count = segs * span
    mine = ch // nseq
    per = width // ndp
    tall = hidden // width
    rank = lax.axis_index("seq").astype(jnp.int32)
    bits = bits_of(ndp)
    first = next(b for b in bits if (per * b) % TILE == 0)
    rest = [b for b in bits if b != first]
    lo = per * first
    scan = rows(span, ch)
    scanned = (scan, (count, ch), F32)
    scan_scratch = [pltpu.VMEM((span, ch), F32)] * 2

    infos, here = call(
        own_kernel, 1, [(full(mine), phase), (full(segs, 2, mine), init_state.transpose(0, 2, 1))],
        [(whole(), (1 + segs, 2, ch), F32), (("smem",), (2,), jnp.int32)],
        [pltpu.VMEM((-(-(2 + 2 * segs) // 8) * 8, ch), F32)], [], "own",
    )
    infos = shift_all(infos, "seq", nseq)

    col = jnp.arange(width)
    pair = jnp.arange(2 * LANES)
    perm = (pair[:, None] == 2 * (pair % LANES)[None, :] + (pair // LANES)[None, :]).astype(BF)
    member = ((col[:, None] // (width // GROUPS)) == jnp.arange(LANES)[None, :]).astype(BF)

    place_of = jnp.arange(span)
    step_order = ((place_of % CHUNKS) * (span // CHUNKS) + place_of // CHUNKS)[:, None] == place_of[None, :]
    step_order = (whole(span, span), step_order.astype(BF))

    x, normed, normed_t, pre = call(
        functools.partial(project_kernel, lo=lo, first=first), segs,
        [
            (rows(span, width), tokens.reshape(count, width)), (whole(width), norm_mix), (whole(width, width), w_in),
            (whole(width, ch), w_forget), (whole(ch), forget_bias), (whole(), perm), step_order,
        ],
        [
            (rows(span, width), (count, width), BF),
            (rows(span, width), (count, width), BF),
            (cols(width, span), (width, count), BF),
            (seg(span, 3 * ch), (segs, span, 3 * ch), BF),
        ],
        [], [here], "project",
    )
    trig, chunk, totals, lam_re, lam_im, drv_re, drv_im = call(
        functools.partial(summary_kernel, ranks=nseq), segs,
        [(seg(span, 3 * ch), pre)] + [(seg(2, ch, fixed=True), i) for i in infos],
        [
            (whole(2, ch), (2, ch), F32),
            (seg(4, CHUNKS, ch), (segs, 4, CHUNKS, ch), F32),
            (seg(4, ch), (segs, 4, ch), F32),
            scanned, scanned, scanned, scanned,
        ],
        [], [], "summary",
    )
    totals = shift_all(totals, "seq", nseq)
    (og,) = call(
        gate_kernel, 1, [(whole(count, width), normed), (whole(width, width), w_ogate)],
        [(whole(count, width), (count, width), BF)], [], [], "gate", (lam_re,),
    )
    cot, dh = call(
        hidden_grad_kernel, segs,
        [(rows(span, width), cotangent.reshape(count, width)), (whole(hidden, width), w_down), step_order],
        [(rows(span, width), (count, width), BF), (rows(span, hidden), (count, hidden), BF)], [], [], "hidden_grad",
        (lam_re,),
    )
    y, y_split, start, final, gated_t, middle = call(
        functools.partial(mixer_kernel, ranks=nseq, lo=lo, first=first), segs,
        [(seg(4, ch), t) for t in totals]
        + [(seg(2, ch, shift=1), i) for i in infos]
        + [
            (scan, lam_re), (scan, lam_im), (scan, drv_re), (scan, drv_im), (seg(4, CHUNKS, ch), chunk),
            (whole(), perm), (rows(span, width), x), (rows(span, width), og), (whole(width), norm_group),
            (whole(width, LANES), member), (whole(width, width), w_out),
        ],
        [
            (rows(span, width), (count, width), BF),
            (rows(span, width), (count, width), BF),
            (seg(2, ch), (segs, 2, ch), F32),
            (seg(2, mine), (segs, 2, mine), F32),
            (cols(width, span), (width, count), BF),
            (rows(span, width), (count, width), F32),
        ],
        scan_scratch, [here], "mixer",
    )
    final_state = final.transpose(0, 2, 1)

    wide = (count, width)
    done = (whole(), (8, LANES), F32)
    psend, pkeep, normed_ffn, normed_ffn_t, hid0, dgv0, duv0 = call(
        functools.partial(ffn_first_kernel, lo=lo, rt=span, first=first), 1,
        [(whole(), a) for a in (middle, norm_ffn, w_gate, w_up, dh)],
        [(whole(), (width // 2, 2 * width), BF)] * 2
        + [(whole(), wide, BF), (whole(), (width, count), BF)]
        + [(whole(), wide, BF)] * 3,
        [], [here], "ffn_first", (), 7,
    )
    pgot = swap(psend, "dp", ndp, first)
    gsend, gkeep, dsend, dkeep, hid, dgv1, duv1 = call(
        functools.partial(ffn_rest_kernel, lo=lo * tall, rt=span, first=first), 1,
        [(whole(), a) for a in (normed_ffn, normed_ffn_t, cot, w_gate, w_up, dh, hid0)],
        [(whole(), (width // 2, 2 * width), BF)] * 2 + [(whole(), (hidden // 2, width), BF)] * 2
        + [(whole(), wide, BF)] * 3,
        [pltpu.VMEM((tall, width, count), BF)], [here], "ffn_rest", (psend,), 7,
    )
    ggot, dgot = swap(gsend, "dp", ndp, first), swap(dsend, "dp", ndp, first)

    nblk = ndp // 2
    fast = ndp == 8 and nseq == 4 and per % (2 * TILE) == 0
    x_bit, y_bit = (PLACE, rest[0]), (PLACE, rest[1])
    z_bits = [(RANK, b) for b in bits_of(nseq)]

    def blocks(a, cols_n, tall_n=1):
        return a.reshape(nblk * tall_n, per, cols_n)

    def ffn_back(*after):
        return call(
            ffn_back_kernel, segs,
            [(rows(span, width), a) for a in (dgv0, duv0, dgv1, duv1)] + [(whole(), w_gate), (whole(), w_up)],
            [(rows(span, width), wide, F32)], [], [], "ffn_back", after,
        )[0]

    order = ()
    if fast:
        p = [blocks(a, 2 * width) for a in (pkeep, pgot)]
        (pa_send, pa_keep), (pb_send, pb_keep) = combine(
            here, [(0, x_bit, [(p, 1, 0, 0, width)]), (1, y_bit, [(p, 1, 0, 1, width)])], "first_sum1", (gkeep,)
        )
        pa_got, pb_got = swap(pa_send, "dp", ndp, rest[0]), swap(pb_send, "dp", ndp, rest[1])
        dn = ffn_back(pa_keep)
        g = [blocks(a, 2 * width) for a in (gkeep, ggot)]
        d = [blocks(a, width, tall) for a in (dkeep, dgot)]
        (fa_send, fa_keep), (fb_send, fb_keep) = combine(
            here, [(0, x_bit, [(g, 1, 0, 0, 2 * width)]), (1, y_bit, [(d, tall, i, 0, width) for i in range(tall)])],
            "ffn_sum1", (dn,),
        )
        fa_got, fb_got = swap(fa_send, "dp", ndp, rest[0]), swap(fb_send, "dp", ndp, rest[1])
        order = (fa_keep,)

    else:
        dn = ffn_back()

    dmiddle, dbranch, dog, dy_split = call(
        turn_kernel, segs,
        [
            (rows(span, width), dn), (rows(span, width), middle), (rows(span, width), cot), (whole(width), norm_ffn),
            (whole(width, width), w_out), (rows(span, width), y), (rows(span, width), og), (whole(width), norm_group),
            (whole(width, LANES), member), (whole(), perm),
        ],
        [
            (rows(span, width), (count, width), F32),
            (rows(span, width), (count, width), BF),
            (rows(span, width), (count, width), BF),
            (rows(span, width), (count, width), BF),
        ],
        [], [], "turn", order,
    )
    order = ()
    if fast:
        pa, pb = add_pairs([(pa_keep, pa_got), (pb_keep, pb_got)], "first_sum2", (dog,))
        order = (pa,)

    chain, adj = call(
        chains_kernel, segs,
        [(rows(span, width), dy_split), (scan, lam_re), (scan, lam_im), (seg(4, CHUNKS, ch), chunk)],
        [(seg(2, CHUNKS, ch), (segs, 2, CHUNKS, ch), F32), (seg(2, ch), (segs, 2, ch), F32)],
        scan_scratch, [], "chains", order,
    )
    adjs = shift_all(adj, "seq", nseq)
    order = ()
    if fast:
        def one(keep, got):
            return [([keep, got], 1, 0, 0, keep.shape[2])]

        def rows_of(keep, got):
            return one(*(a.reshape(2, per // 2, a.shape[2]) for a in (keep, got)))

        (fa_send, fa_keep), (fb_send, fb_keep) = combine(
            here,
            [
                (0, y_bit, [([pa], 1, 0, 0, width)] + one(fa_keep, fa_got)),
                (0, x_bit, [([pb], 1, 0, 0, width)] + one(fb_keep, fb_got)),
            ],
            "ffn_sum2", (chain,),
        )
        fa_got, fb_got = swap(fa_send, "dp", ndp, rest[1]), swap(fb_send, "dp", ndp, rest[0])
        order = (fa_keep,)

    ntile = width // 3
    osend, okeep = call(
        functools.partial(grads_kernel, pairs=2), width // ntile,
        [
            (whole(width, count), normed_t), (cols(count, ntile), dog),
            (whole(width, count), gated_t), (cols(count, ntile), dbranch),
        ],
        [
            (cols(width // 2, 2 * ntile), (width // 2, 2 * width), BF),
            (cols(width // 2, 2 * ntile), (width // 2, 2 * width), BF),
        ],
        [], [], "mixer_grads", order,
    )
    late, *adjs = lax.optimization_barrier((osend, *adjs))
    ogot = swap(late, "dp", ndp, first)

    dpre, sums = call(
        functools.partial(adjoint_kernel, ranks=nseq), segs,
        [(seg(4, ch), t) for t in totals] + [(seg(2, ch), a) for a in adjs]
        + [
            (seg(span, 3 * ch), pre), (whole(2, ch), trig), (scan, lam_re), (scan, lam_im),
            (rows(span, width), dy_split),
            (rows(span, width), y_split), (seg(2, ch), start),
            (seg(4, CHUNKS, ch), chunk), (seg(2, CHUNKS, ch), chain), (whole(), perm),
        ],
        [(rows(span, 3 * ch), (count, 3 * ch), BF), (whole(2, ch), (2, ch), F32)],
        scan_scratch, [here], "adjoint", (osend,),
    )
    into = 3 * ch + LANES
    isend, ikeep = call(
        functools.partial(input_grads_kernel, per=per), 1,
        [(whole(width, count), normed_t), (whole(count, 3 * ch), dpre), (whole(2, ch), sums)],
        [(whole(width // 2, into), (width // 2, into), BF)] * 2, [], [], "input_grads",
    )
    igot = swap(isend, "dp", ndp, first)
    order = ()
    if fast:
        lead, other = bits_of(nseq)

        def over(send, axis_n, bit):
            return swap(send, "seq", axis_n, bit)

        (fa_send, fa_keep), (fb_send, fb_keep) = combine(
            here, [(0, z_bits[0], rows_of(fa_keep, fa_got)), (0, z_bits[1], rows_of(fb_keep, fb_got))],
            "ffn_sum3", (isend,),
        )
        fa_got, fb_got = over(fa_send, nseq, lead), over(fb_send, nseq, other)
        o = [blocks(a, 2 * width) for a in (okeep, ogot)]
        i = [blocks(a, into) for a in (ikeep, igot)]
        (ra_send, ra_keep), (rb_send, rb_keep) = combine(
            here, [(0, x_bit, [(o, 1, 0, 0, 2 * width)]), (1, y_bit, [(i, 1, 0, 0, into)])], "mixer_sum1", (fa_keep,)
        )
        ra_got, rb_got = swap(ra_send, "dp", ndp, rest[0]), swap(rb_send, "dp", ndp, rest[1])
        order = (ra_keep,)

    grad_tokens, tokens_done = call(
        tokens_kernel, segs,
        [
            (rows(span, 3 * ch), dpre), (rows(span, width), dog), (whole(width, width), w_in),
            (whole(width, ch), w_forget), (whole(width, width), w_ogate), (rows(span, width), x),
            (whole(width), norm_mix), (rows(span, width), dmiddle), step_order,
        ],
        [(moved(span, width, dim=0), (count, width), BF), done],
        [], [], "tokens", order,
    )

    def output(*after):
        return call(
            out_kernel, segs,
            [(rows(span, width), a) for a in (middle, hid0, hid)] + [(whole(hidden, width), w_down), step_order],
            [(moved(span, width, dim=0), (count, width), BF), done], [], [], "out", after,
        )

    if fast:
        fa, fb = add_pairs([(fa_keep, fa_got), (fb_keep, fb_got)], "ffn_sum4", (tokens_done,))
        fa_got, fb_got = over(fa, nseq, other), over(fb, nseq, lead)
        (ra_send, ra_keep), (rb_send, rb_keep) = combine(
            here, [(0, y_bit, one(ra_keep, ra_got)), (0, x_bit, one(rb_keep, rb_got))], "mixer_sum2", (fa,)
        )
        ra_got, rb_got = swap(ra_send, "dp", ndp, rest[1]), swap(rb_send, "dp", ndp, rest[0])
        mixed_out, out_done = output(ra_keep)
        (ra_send, ra_keep), (rb_send, rb_keep) = combine(
            here, [(0, z_bits[0], rows_of(ra_keep, ra_got)), (0, z_bits[1], rows_of(rb_keep, rb_got))], "mixer_sum3", (out_done,)
        )
        ra_got, rb_got = over(ra_send, nseq, lead), over(rb_send, nseq, other)
        fa, fb = add_pairs([(fa, fa_got), (fb, fb_got)], "ffn_sum5", (ra_keep,))
        fa_got, fb_got = over(fa, nseq, lead), over(fb, nseq, other)
        ra, rb = add_pairs([(ra_keep, ra_got), (rb_keep, rb_got)], "mixer_sum4", (fa,))
        ra_got, rb_got = over(ra, nseq, other), over(rb, nseq, lead)

        ra, rb = add_pairs([(ra, ra_got), (rb, rb_got)], "mixer_sum5")
        ra_got, rb_got = over(ra, nseq, lead), over(rb, nseq, other)

        def flat(*pairs):
            return [tuple(a.reshape(per // 2, a.shape[2]) for a in pair) for pair in pairs]

        moves = [(0, 0, width, 0, 0, 0), (0, width, width, 0, 0, width), (0, 2 * width, width, 1, 0, width)]
        moves += [(1, 0, width, 1, 0, 0)] + [(1, (1 + t) * width, width, 2, t * per, 0) for t in range(tall)]
        part_gate, part_up, part_down, part_ffn, ffn_done = finish(
            here, flat((fa, fa_got), (fb, fb_got)), z_bits, moves,
            [(ours(per, hidden), w_gate), (ours(per, hidden), w_up), (whole(width), norm_ffn)],
            [(full, (per, hidden)), (full, (per, hidden)), (full, (tall * per, width)), (full, (per,))],
            [(3, 2, [(0, 0), (1, 1)])], None, nseq, "ffn_out", (ra,),
        )
        moves = [(0, n * ntile, ntile, n % 2, 0, (n // 2) * ntile) for n in range(2 * width // ntile)]
        moves += [(1, 0, width, 2, 0, 0), (1, width, ch, 3, 0, 0)]
        part_ogate, part_out, part_in, part_forget, part_mix, part_group, part_bias, part_phase, _ = finish(
            here, flat((ra, ra_got), (rb, rb_got)), z_bits, moves,
            [
                (ours(per, width), w_ogate), (ours(per, width), w_out), (ours(per, width), w_in), (ours(per, ch), w_forget),
                (whole(width), norm_mix), (whole(width), norm_group),
            ],
            [(full, (per, n)) for n in (width, width, width, ch)] + [(full, (n,)) for n in (per, per, mine, mine)],
            [(4, 4, [(0, 0), (2, 2), (3, 3)]), (5, 5, [(1, 1)])], (1, 3 * ch, 6), nseq, "mixer_out",
        )
    else:
        mixed_out, _ = output()

        def plain(keep, got, cols_n, tall_n=1):
            shape = [2] * len(rest) + [tall_n * per, cols_n]
            return plain_reduce([keep.reshape(shape), got.reshape(shape)], rest, ndp, nseq)

        guv = [plain(pkeep, pgot, 2 * width), plain(gkeep, ggot, 2 * width)]
        part_gate = jnp.concatenate([a[:, :width] for a in guv], axis=1)
        part_up = jnp.concatenate([a[:, width:] for a in guv], axis=1)
        part_down = plain(dkeep, dgot, width, tall)
        mix = plain(okeep, ogot, 2 * width)
        mix = [mix[:, n * ntile : (n + 1) * ntile] for n in range(2 * width // ntile)]
        part_ogate, part_out = jnp.concatenate(mix[0::2], axis=1), jnp.concatenate(mix[1::2], axis=1)
        both = plain(ikeep, igot, into)
        part_in, part_forget = both[:, :width], both[:, width : 3 * ch]
        shared = both[: 2 * ch // LANES, 3 * ch :].reshape(2, ch)
        part_bias, part_phase = lax.dynamic_slice_in_dim(shared, rank * mine, mine, axis=1)

        def own_rows(a):
            return lax.dynamic_slice_in_dim(a, lax.axis_index("dp") * per, per, axis=0).astype(F32)

        def gain_of(norm, *pairs):
            return sum(jnp.sum(own_rows(w) * gw, axis=1) for w, gw in pairs) / own_rows(norm)

        part_ffn = gain_of(norm_ffn, (w_gate, part_gate), (w_up, part_up))
        part_mix = gain_of(norm_mix, (w_in, part_in), (w_forget, part_forget), (w_ogate, part_ogate))
        part_group = gain_of(norm_group, (w_out, part_out))
    return (
        mixed_out.reshape(segs, span, width),
        grad_tokens.reshape(segs, span, width),
        final_state,
        part_mix, part_in, part_forget, part_bias, part_phase, part_ogate, part_group, part_out, part_ffn,
        part_gate, part_up, part_down,
    )


def solution(mesh):
    ndp, nseq = mesh.shape["dp"], mesh.shape["seq"]
    tok, vec, col = P("dp", "seq", None), P("dp"), P("dp", None)
    return jax.shard_map(
        functools.partial(local, ndp, nseq),
        mesh=mesh,
        in_specs=(tok, tok, P(), P(), P(), P(), P("seq"), P(), P(), P(), P(), P(), P(), P(), tok),
        out_specs=(tok, tok, tok, vec, col, col, P("seq"), P("seq"), col, vec, col, vec, col, col, col),
        check_vma=False,
    )
```

```python
import functools

import jax
import jax.numpy as jnp
from jax import lax
from jax.experimental import pallas as pl
from jax.experimental.pallas import tpu as pltpu
from jax.sharding import PartitionSpec as P

GROUPS = 8
CHUNKS = 8
LANES = 128
RANK, PLACE = 0, 1
MICROSECONDS = dict(
    project=4, summary=4, hidden_grad=2.5, mixer=8, ffn_first=6, ffn_rest=12, turn=7, chains=0.3, mixer_grads=0.01, adjoint=3.74, input_grads=0.3, tokens=0.3, ffn_sum4=8, out=3.5,
    ffn_sum1=1.3, mixer_sum1=1.0, ffn_sum2=3, ffn_sum3=20,
)
COST = 1.15e9
TILE = 16
epsilon = 1e-06
BF = jnp.bfloat16
F32 = jnp.float32
NT = ((1,), (1,))


def dot(a, b, dims=((1,), (0,))):
    return lax.dot_general(a, b, (dims, ((), ())), preferred_element_type=F32)


def silu_slope(values, logistic):
    return logistic * (1.0 + values * (1.0 - logistic))


def cmul(ar, ai, br, bi):
    return ar * br - ai * bi, ar * bi + ai * br


def row_mean(v):
    return jnp.mean(v, axis=-1, keepdims=True)


def split_dot(v, m, dims):
    high = v.astype(BF)
    low = (v - high.astype(F32)).astype(BF)
    return dot(high, m, dims) + dot(low, m, dims)


def group_mean(v, member):
    return split_dot(v, member, ((1,), (0,))) * (GROUPS / v.shape[1])


def group_spread(v, member):
    return split_dot(v, member, NT)


def bit_of(here_ref, which, bit):
    return lax.shift_right_logical(here_ref[which], bit.bit_length() - 1) & 1


def put_halves(ref, t, col, lo, bit):
    half = ref.shape[0] // 2
    for b in range(t.shape[0] // lo):
        at = jnp.where(bit == b % 2, half, 0) + (b // 2) * lo
        ref[pl.ds(pl.multiple_of(at, TILE), lo), col : col + t.shape[1]] = t[b * lo : (b + 1) * lo, :]


def at_step(t):
    return slice(CHUNKS * t, CHUNKS * (t + 1))


def apart(v, perm_ref):
    n = perm_ref.shape[0]
    parts = [dot(v[:, c : c + n], perm_ref[...]).astype(BF) for c in range(0, v.shape[1], n)]
    return jnp.concatenate([p[:, : n // 2] for p in parts] + [p[:, n // 2 :] for p in parts], axis=1)


def together(re, im, perm_ref):
    n = perm_ref.shape[0] // 2
    parts = [
        dot(jnp.concatenate([re[:, c : c + n], im[:, c : c + n]], axis=1), perm_ref[...], NT)
        for c in range(0, re.shape[1], n)
    ]
    return jnp.concatenate(parts, axis=1)


def reorder(order_ref, v, back=False):
    return dot(order_ref[...], v, ((0,), (0,)) if back else ((1,), (0,))).astype(BF)


def own_kernel(phase_ref, init_ref, infos_ref, here_ref, line_ref):
    own = phase_ref.shape[0]
    rank, place = lax.axis_index("seq"), lax.axis_index("dp")
    here_ref[RANK], here_ref[PLACE] = rank, place
    theta = phase_ref[...][None]
    line_ref[...] = jnp.zeros_like(line_ref)
    line_ref[0:1, :own] = jnp.cos(theta)
    line_ref[1:2, :own] = jnp.sin(theta)
    for n in range(init_ref.shape[0]):
        line_ref[2 + 2 * n : 4 + 2 * n, :own] = init_ref[n]
    placed = pltpu.roll(line_ref[...], own * rank, 1)
    for n in range(infos_ref.shape[0]):
        infos_ref[n] = placed[2 * n : 2 * n + 2, :]


def project_kernel(
    here_ref, x_ref, gain_ref, w_in_ref, w_forget_ref, bias_ref, perm_ref, order_ref, xs_ref, normed_ref, turned_ref,
    pre_ref, *, lo, first
):
    width = x_ref.shape[1]
    xs = reorder(order_ref, x_ref[...])
    xs_ref[...] = xs
    x = xs.astype(F32)
    normed = (x * lax.rsqrt(row_mean(x * x) + epsilon) * gain_ref[...][None]).astype(BF)
    normed_ref[...] = normed
    put_halves(turned_ref, normed.T, 0, lo, bit_of(here_ref, PLACE, first))
    mixed = dot(normed, w_in_ref[...]).astype(BF)
    pre_ref[:, :width] = apart(mixed, perm_ref)
    pre_ref[:, width:] = (dot(normed, w_forget_ref[...]) + bias_ref[...][None]).astype(BF)


def summary_kernel(*refs, ranks):
    pre_ref, infos = refs[0], refs[1 : 1 + ranks]
    trig_ref, chunk_ref, total_ref, lam_re, lam_im, drv_re, drv_im = refs[1 + ranks :]
    span, ch = lam_re.shape
    trig = infos[0][...]
    for info in infos[1:]:
        trig = trig + info[...]
    trig_ref[...] = trig
    pre = pre_ref[...].astype(F32)
    forget = jax.nn.sigmoid(pre[:, 2 * ch :])
    lam_re[...] = forget * trig[0:1, :]
    lam_im[...] = forget * trig[1:2, :]
    drv_re[...] = (1.0 - forget) * jax.nn.silu(pre[:, :ch])
    drv_im[...] = (1.0 - forget) * jax.nn.silu(pre[:, ch : 2 * ch])
    first = at_step(0)
    pr, pi, hr, hi = lam_re[first, :], lam_im[first, :], drv_re[first, :], drv_im[first, :]
    for t in range(1, span // CHUNKS):
        lr, li = lam_re[at_step(t), :], lam_im[at_step(t), :]
        pr, pi = cmul(lr, li, pr, pi)
        hr, hi = cmul(lr, li, hr, hi)
        hr, hi = hr + drv_re[at_step(t), :], hi + drv_im[at_step(t), :]
    chunk_ref[0], chunk_ref[1], chunk_ref[2], chunk_ref[3] = pr, pi, hr, hi
    tp_r, tp_i, th_r, th_i = pr[0:1], pi[0:1], hr[0:1], hi[0:1]
    for k in range(1, CHUNKS):
        lr, li = pr[k : k + 1], pi[k : k + 1]
        th_r, th_i = cmul(lr, li, th_r, th_i)
        th_r, th_i = th_r + hr[k : k + 1], th_i + hi[k : k + 1]
        tp_r, tp_i = cmul(lr, li, tp_r, tp_i)
    total_ref[...] = jnp.concatenate([tp_r, tp_i, th_r, th_i], axis=0)


def mixer_kernel(*refs, ranks, lo, first):
    scalars, refs = refs[0], refs[1:]
    totals, inits, refs = refs[:ranks], refs[ranks : 2 * ranks], refs[2 * ranks :]
    lam_re, lam_im, drv_re, drv_im, chunk_ref, perm_ref, x_ref, og_ref, gain_ref, member_ref, w_out_ref = refs[:11]
    y_ref, split_ref, start_ref, final_ref, turned_ref, middle_ref, ginv_ref, st_re, st_im = refs[11:]
    span, ch = lam_re.shape
    rank, bit = scalars[RANK], bit_of(scalars, PLACE, first)
    init = inits[0][...]
    for info in inits[1:]:
        init = init + info[...]
    cr, ci = init[0:1], init[1:2]

    def after(k, cr, ci, take):
        total = totals[k][...]
        nr, ni = cmul(total[0:1], total[1:2], cr, ci)
        nr, ni = nr + total[2:3], ni + total[3:4]
        return jnp.where(take, nr, cr), jnp.where(take, ni, ci)

    for k in range(ranks - 1, 0, -1):
        cr, ci = after(k, cr, ci, k <= rank)
    start_ref[...] = jnp.concatenate([cr, ci], axis=0)
    er, ei = after(0, cr, ci, rank >= 0)
    for k in range(ranks - 1, 0, -1):
        er, ei = after(k, er, ei, k > rank)
    own = ch // ranks
    final_ref[...] = pltpu.roll(jnp.concatenate([er, ei] * 4, axis=0), (ch - own * rank) % ch, 1)[:2, :own]
    rows_r, rows_i = [cr], [ci]
    for k in range(CHUNKS - 1):
        cr, ci = cmul(chunk_ref[0, k : k + 1, :], chunk_ref[1, k : k + 1, :], cr, ci)
        cr, ci = cr + chunk_ref[2, k : k + 1, :], ci + chunk_ref[3, k : k + 1, :]
        rows_r.append(cr)
        rows_i.append(ci)
    hr, hi = jnp.concatenate(rows_r, axis=0), jnp.concatenate(rows_i, axis=0)
    for t in range(span // CHUNKS):
        hr, hi = cmul(lam_re[at_step(t), :], lam_im[at_step(t), :], hr, hi)
        hr, hi = hr + drv_re[at_step(t), :], hi + drv_im[at_step(t), :]
        st_re[at_step(t), :] = hr
        st_im[at_step(t), :] = hi
    re, im = st_re[...].astype(BF), st_im[...].astype(BF)
    split_ref[:, :ch], split_ref[:, ch:] = re, im
    yf = together(re, im, perm_ref)
    y_ref[...] = yf.astype(BF)
    member = member_ref[...]
    inv = lax.rsqrt(group_mean(yf * yf, member) + epsilon)
    ginv_ref[...] = inv
    inv = group_spread(inv, member)
    gated = (yf * inv * gain_ref[...][None] * jax.nn.silu(og_ref[...].astype(F32))).astype(BF)
    put_halves(turned_ref, gated.T, 0, lo, bit)
    middle_ref[...] = x_ref[...].astype(F32) + dot(gated, w_out_ref[...])


def hidden_tile(n_ref, rows, cut, wg_ref, wu_ref, dh_ref, hid_ref, dgv_ref, duv_ref, to):
    g, u = dot(n_ref[rows, :], wg_ref[:, cut]), dot(n_ref[rows, :], wu_ref[:, cut])
    dh = dh_ref[rows, cut].astype(F32)
    sig = jax.nn.sigmoid(g)
    act = g * sig
    hid_ref[rows, to] = (act * u).astype(BF)
    dgv_ref[rows, to] = (dh * u * silu_slope(g, sig)).astype(BF)
    duv_ref[rows, to] = (dh * act).astype(BF)


def two_halves(lhs_ref, rhs, send_ref, keep_ref, to):
    half = lhs_ref.shape[0] // 2
    send_ref[:, to] = dot(lhs_ref[:half, :], rhs).astype(BF)
    keep_ref[:, to] = dot(lhs_ref[half:, :], rhs).astype(BF)


def ffn_first_kernel(
    here_ref, middle_ref, gain_ref, wg_ref, wu_ref, dh_ref,
    gsend_ref, gkeep_ref, n_ref, nt_ref, hid_ref, dgv_ref, duv_ref,
    *, lo, rt, first,
):
    bit = bit_of(here_ref, PLACE, first)
    count, width = middle_ref.shape
    cut = slice(0, width)
    for r in range(0, count, rt):
        rows = slice(r, r + rt)
        v = middle_ref[rows, :]
        normed = (v * lax.rsqrt(row_mean(v * v) + epsilon) * gain_ref[...][None]).astype(BF)
        n_ref[rows, :] = normed
        put_halves(nt_ref, normed.T, r, lo, bit)
        hidden_tile(n_ref, rows, cut, wg_ref, wu_ref, dh_ref, hid_ref, dgv_ref, duv_ref, cut)
    two_halves(nt_ref, dgv_ref[...], gsend_ref, gkeep_ref, cut)
    two_halves(nt_ref, duv_ref[...], gsend_ref, gkeep_ref, slice(width, 2 * width))


def ffn_rest_kernel(
    here_ref, n_ref, nt_ref, cot_ref, wg_ref, wu_ref, dh_ref, hid0_ref,
    gsend_ref, gkeep_ref, dsend_ref, dkeep_ref, hid_ref, dgv_ref, duv_ref,
    ht_ref,
    *, lo, rt, first,
):
    bit = bit_of(here_ref, PLACE, first)
    count, width = n_ref.shape
    spans = [slice(r, r + rt) for r in range(0, count, rt)]
    cut, own = slice(width, 2 * width), slice(0, width)
    for rows in spans:
        hidden_tile(n_ref, rows, cut, wg_ref, wu_ref, dh_ref, hid_ref, dgv_ref, duv_ref, own)
    two_halves(nt_ref, dgv_ref[...], gsend_ref, gkeep_ref, own)
    two_halves(nt_ref, duv_ref[...], gsend_ref, gkeep_ref, cut)
    half = width // 2
    for j, ref in enumerate((hid0_ref, hid_ref)):
        for rows in spans:
            put_halves(ht_ref.at[j], ref[rows, :].T, rows.start, lo, bit)
    for j in range(2):
        out = slice(j * half, (j + 1) * half)
        dsend_ref[out, :] = dot(ht_ref[j, :half, :], cot_ref[...]).astype(BF)
        dkeep_ref[out, :] = dot(ht_ref[j, half:, :], cot_ref[...]).astype(BF)


def ffn_back_kernel(dgv_ref, duv_ref, wg_ref, wu_ref, *refs, tile):
    before, dn_ref = refs[:-1], refs[-1]
    width = dn_ref.shape[1]
    cut = slice(tile * width, (tile + 1) * width)
    dn = dot(dgv_ref[...], wg_ref[:, cut], NT) + dot(duv_ref[...], wu_ref[:, cut], NT)
    for ref in before:
        dn = dn + ref[...]
    dn_ref[...] = dn


def gate_kernel(normed_ref, w_ref, og_ref):
    og_ref[...] = dot(normed_ref[...], w_ref[...]).astype(BF)


def hidden_grad_kernel(cot_ref, wd_ref, order_ref, cots_ref, dh_ref):
    cots = reorder(order_ref, cot_ref[...])
    cots_ref[...] = cots
    dh_ref[...] = dot(cots, wd_ref[...], NT).astype(BF)


def turn_kernel(
    dn_ref, middle_ref, cot_ref, ffn_gain_ref, w_out_ref, y_ref, ginv_ref, og_ref, gain_ref, member_ref, perm_ref,
    dmiddle_ref, dbranch_ref, dog_ref, split_ref,
):
    v, up = middle_ref[...], dn_ref[...]
    inv = lax.rsqrt(row_mean(v * v) + epsilon)
    unit = v * inv
    through = up * ffn_gain_ref[...][None]
    dmiddle = cot_ref[...].astype(F32) + inv * (through - unit * row_mean(through * unit))
    dmiddle_ref[...] = dmiddle
    dbranch = dmiddle.astype(BF)
    dbranch_ref[...] = dbranch
    dgated = dot(dbranch, w_out_ref[...], NT)
    og, yf, member, gain = og_ref[...].astype(F32), y_ref[...].astype(F32), member_ref[...], gain_ref[...][None]
    ginv = group_spread(ginv_ref[...], member)
    gunit = yf * ginv
    sig = jax.nn.sigmoid(og)
    dog_ref[...] = (dgated * gunit * gain * silu_slope(og, sig)).astype(BF)
    through = dgated * og * sig * gain
    dy = (ginv * (through - gunit * group_spread(group_mean(through * gunit, member), member))).astype(BF)
    split_ref[...] = apart(dy, perm_ref)


def chains_kernel(split_ref, lam_re, lam_im, chunk_ref, chain_ref, total_ref, dy_re, dy_im):
    span, ch = lam_re.shape
    dy_re[...] = split_ref[:, :ch].astype(F32)
    dy_im[...] = split_ref[:, ch:].astype(F32)
    last = span // CHUNKS - 1
    gr, gi = dy_re[at_step(last), :], dy_im[at_step(last), :]
    ar, ai = cmul(lam_re[at_step(last), :], -lam_im[at_step(last), :], gr, gi)
    for t in range(last - 1, -1, -1):
        gr, gi = dy_re[at_step(t), :] + ar, dy_im[at_step(t), :] + ai
        ar, ai = cmul(lam_re[at_step(t), :], -lam_im[at_step(t), :], gr, gi)
    chain_ref[0], chain_ref[1] = ar, ai
    er, ei = ar[CHUNKS - 1 :], ai[CHUNKS - 1 :]
    for k in range(CHUNKS - 2, -1, -1):
        er, ei = cmul(chunk_ref[0, k : k + 1, :], -chunk_ref[1, k : k + 1, :], er, ei)
        er, ei = er + ar[k : k + 1], ei + ai[k : k + 1]
    total_ref[...] = jnp.concatenate([er, ei], axis=0)


def adjoint_kernel(*refs, ranks):
    scalars, refs = refs[0], refs[1:]
    totals, adjs, refs = refs[:ranks], refs[ranks : 2 * ranks], refs[2 * ranks :]
    pre_ref, trig_ref, lam_re, lam_im, dy_ref, split_ref, start_ref, chunk_ref, chain_ref, perm_ref = refs[:10]
    dpre_ref, sums_ref, dy_re, dy_im = refs[10:]
    span, ch = lam_re.shape
    rank = scalars[RANK]
    pre = pre_ref[...].astype(F32)
    trig = trig_ref[...]
    forget = jax.nn.sigmoid(pre[:, 2 * ch :])
    dy_re[...] = dy_ref[:, :ch].astype(F32)
    dy_im[...] = dy_ref[:, ch:].astype(F32)
    cr = jnp.zeros((1, ch), F32)
    ci = jnp.zeros((1, ch), F32)
    for k in range(1, ranks):
        total, adj = totals[k][...], adjs[k][...]
        nr, ni = cmul(total[0:1], -total[1:2], cr, ci)
        nr, ni = nr + adj[0:1], ni + adj[1:2]
        cr, ci = jnp.where(k > rank, nr, cr), jnp.where(k > rank, ni, ci)
    rows_r, rows_i = [cr], [ci]
    for k in range(CHUNKS - 1, 0, -1):
        cr, ci = cmul(chunk_ref[0, k : k + 1, :], -chunk_ref[1, k : k + 1, :], cr, ci)
        cr, ci = cr + chain_ref[0, k : k + 1, :], ci + chain_ref[1, k : k + 1, :]
        rows_r.append(cr)
        rows_i.append(ci)
    ar, ai = jnp.concatenate(rows_r[::-1], axis=0), jnp.concatenate(rows_i[::-1], axis=0)
    for t in range(span // CHUNKS - 1, -1, -1):
        gr, gi = dy_re[at_step(t), :] + ar, dy_im[at_step(t), :] + ai
        dy_re[at_step(t), :] = gr
        dy_im[at_step(t), :] = gi
        ar, ai = cmul(lam_re[at_step(t), :], -lam_im[at_step(t), :], gr, gi)
    gr, gi = dy_re[...], dy_im[...]

    def before(states, start):
        ends = pltpu.roll(states[span - CHUNKS :, :], 1, 0)
        ends = jnp.where(lax.broadcasted_iota(jnp.int32, ends.shape, 0) == 0, start, ends)
        return jnp.concatenate([ends, states[: span - CHUNKS, :]], axis=0)

    qr = before(split_ref[:, :ch].astype(F32), start_ref[0:1, :])
    qi = before(split_ref[:, ch:].astype(F32), start_ref[1:2, :])
    pin_re, pin_im = pre[:, :ch], pre[:, ch : 2 * ch]
    sig_re, sig_im = jax.nn.sigmoid(pin_re), jax.nn.sigmoid(pin_im)
    lr = gr * qr + gi * qi
    li = gi * qr - gr * qi
    turned_re = lr * trig[0:1, :] + li * trig[1:2, :]
    turned_im = li * trig[0:1, :] - lr * trig[1:2, :]
    df = turned_re - (gr * pin_re * sig_re + gi * pin_im * sig_im)
    keep = 1.0 - forget
    dre = (keep * gr * silu_slope(pin_re, sig_re)).astype(BF)
    dim = (keep * gi * silu_slope(pin_im, sig_im)).astype(BF)
    dpz = (forget * keep * df).astype(BF)
    dpre_ref[:, : 2 * ch] = together(dre, dim, perm_ref).astype(BF)
    dpre_ref[:, 2 * ch :] = dpz
    sums = jnp.concatenate(
        [
            jnp.sum(dpz.astype(F32), axis=0, keepdims=True),
            jnp.sum(forget * turned_im, axis=0, keepdims=True),
        ],
        axis=0,
    )

    @pl.when(pl.program_id(0) == 0)
    def _():
        sums_ref[...] = sums

    @pl.when(pl.program_id(0) > 0)
    def _():
        sums_ref[...] += sums


def grads_kernel(*refs, pairs):
    ins, (send_ref, keep_ref) = refs[: 2 * pairs], refs[2 * pairs :]
    at = 0
    for p in range(pairs):
        lhs_ref, rhs_ref = ins[2 * p], ins[2 * p + 1]
        half, n = lhs_ref.shape[0] // 2, rhs_ref.shape[1]
        send_ref[:, at : at + n] = dot(lhs_ref[:half, :], rhs_ref[...]).astype(BF)
        keep_ref[:, at : at + n] = dot(lhs_ref[half:, :], rhs_ref[...]).astype(BF)
        at += n


def out_kernel(middle_ref, hid0_ref, hid_ref, w_down_ref, order_ref, out_ref, done_ref):
    width = middle_ref.shape[1]
    branch = dot(hid0_ref[...], w_down_ref[:width, :]) + dot(hid_ref[...], w_down_ref[width:, :])
    out = (middle_ref[...] + branch).astype(BF)
    out_ref[...] = reorder(order_ref, out, True)
    done_ref[...] = jnp.zeros_like(done_ref)


def input_grads_kernel(lhs_ref, dpre_ref, sums_ref, send_ref, keep_ref, *, per):
    half, n = lhs_ref.shape[0] // 2, dpre_ref.shape[1]
    send_ref[:, :n] = dot(lhs_ref[:half, :], dpre_ref[...]).astype(BF)
    keep_ref[:, :n] = dot(lhs_ref[half:, :], dpre_ref[...]).astype(BF)
    parts = n // 3 // LANES
    flat = [sums_ref[k : k + 1, g * LANES : (g + 1) * LANES] for k in range(2) for g in range(parts)]
    flat.append(jnp.zeros((-2 * parts % 8, LANES), F32))
    flat = jnp.concatenate(flat, axis=0).astype(BF)
    shape = (half, flat.shape[0])
    row, k = lax.broadcasted_iota(jnp.int32, shape, 0), lax.broadcasted_iota(jnp.int32, shape, 1)
    beside = dot((row % per == k).astype(F32).astype(BF), flat).astype(BF)
    send_ref[:, n:] = beside
    keep_ref[:, n:] = beside


def tokens_kernel(
    dpre_ref, dog_ref, w_in_ref, w_forget_ref, w_ogate_ref, x_ref, gain_ref, dmiddle_ref, order_ref, out_ref, done_ref
):
    width = x_ref.shape[1]
    up = (
        dot(dpre_ref[:, :width], w_in_ref[...], NT)
        + dot(dpre_ref[:, width:], w_forget_ref[...], NT)
        + dot(dog_ref[...], w_ogate_ref[...], NT)
    )
    x = x_ref[...].astype(F32)
    inv = lax.rsqrt(row_mean(x * x) + epsilon)
    unit = x * inv
    through = up * gain_ref[...][None]
    out = (dmiddle_ref[...] + inv * (through - unit * row_mean(through * unit))).astype(BF)
    out_ref[...] = reorder(order_ref, out, True)
    done_ref[...] = jnp.zeros_like(done_ref)


def rows(*shape):
    return ("rows", shape)


def cols(*shape):
    return ("cols", shape)


def seg(*shape, shift=0, fixed=False):
    return ("seg", shape, shift, fixed)


def whole(*shape):
    return ("whole", shape)


def moved(*shape, dim):
    return ("moved", shape, dim)


def ours(*shape):
    return ("own", shape)


def full(*shape):
    return ("full", shape)


def spec_of(kind):
    if kind[0] == "smem":
        return pl.BlockSpec(memory_space=pltpu.SMEM)
    if kind[0] == "full":
        return pl.BlockSpec(kind[1], lambda s, *_: (0,) * len(kind[1]))
    if kind[0] == "own":
        return pl.BlockSpec(kind[1], lambda s, here: (here[PLACE], 0))
    if kind[0] not in ("moved",):
        return pl.BlockSpec(memory_space=pltpu.VMEM)
    _, shape, dim = kind
    return pl.BlockSpec(shape, lambda s, *_: tuple(s if d == dim else 0 for d in range(len(shape))))


def view_of(kind, ref):
    step = pl.program_id(0)
    if kind[0] == "rows":
        n = kind[1][0]
        return ref.at[pl.ds(pl.multiple_of(step * n, n), n)]
    if kind[0] == "cols":
        n = kind[1][1]
        return ref.at[:, pl.ds(pl.multiple_of(step * n, n), n)]
    if kind[0] == "seg":
        return ref.at[kind[2] if kind[3] else step + kind[2]]
    return ref


def size_of(shape, dtype):
    return functools.reduce(lambda p, q: p * q, shape) * jnp.dtype(dtype).itemsize


def call(kernel, steps, ins, outs, scratch, scalars, name, after=(), room=5):
    cost = int(COST * MICROSECONDS.get(name, 0.8))
    lead, extra = len(scalars), len(after)
    kinds_in, kinds_out = [k for k, _ in ins], [k for k, _, _ in outs]

    def body(*refs):
        given, refs = refs[: lead + len(ins)], refs[lead + len(ins) + extra :]
        kernel(
            *given[:lead],
            *[view_of(k, r) for k, r in zip(kinds_in, given[lead:], strict=True)],
            *[view_of(k, r) for k, r in zip(kinds_out, refs[: len(outs)], strict=True)],
            *refs[len(outs) :],
        )

    limit = room << 20
    limit += sum(2 * size_of(k[1], a.dtype) for k, a in ins if k[0] in ("moved", "own"))
    limit += sum(2 * size_of(k[1], d) for k, _, d in outs if k[0] in ("moved", "full"))
    limit += sum(size_of(m.shape, m.dtype) for m in scratch)
    return pl.pallas_call(
        body,
        grid_spec=pltpu.PrefetchScalarGridSpec(
            num_scalar_prefetch=lead,
            grid=(steps,),
            in_specs=[spec_of(k) for k in kinds_in] + [pl.BlockSpec(memory_space=pl.ANY)] * extra,
            out_specs=[spec_of(k) for k in kinds_out],
            scratch_shapes=scratch,
        ),
        out_shape=[jax.ShapeDtypeStruct(s, d) for _, s, d in outs],
        compiler_params=pltpu.CompilerParams(vmem_limit_bytes=limit),
        cost_estimate=pl.CostEstimate(flops=cost, bytes_accessed=1, transcendentals=0),
        name=name,
    )(*scalars, *[a for _, a in ins], *after)


def shift_all(payload, axis, n):
    return [payload] + [lax.ppermute(payload, axis, [(i, (i + k) % n) for i in range(n)]) for k in range(1, n)]


def own_bit(axis, bit):
    return lax.shift_right_logical(lax.axis_index(axis).astype(jnp.int32), jnp.int32(bit.bit_length() - 1)) & 1


def swap(v, axis, n, bit):
    return lax.ppermute(v, axis, [(i, i ^ bit) for i in range(n)])


def bits_of(n):
    return [1 << i for i in range((n - 1).bit_length())]


def combine_kernel(here_ref, *refs, plan, n_in, sums):
    ins, outs = refs[:n_in], refs[n_in:]
    for n, (a, b) in enumerate(sums):
        outs[2 * len(plan) + n][...] = (ins[a][...].astype(F32) + ins[b][...].astype(F32)).astype(BF)
    for n, (pos, bit, count, sources) in enumerate(plan):
        for flip in (1, 0):
            own = 1 - bit_of(here_ref, *bit) if flip else bit_of(here_ref, *bit)
            for i in range(count):
                low = i % (1 << pos)
                q = (i - low) * 2 + own * (1 << pos) + low
                at = 0
                for addends, mult, off, col, width in sources:
                    cut = slice(col * width, (col + 1) * width)
                    acc = ins[addends[0]][q * mult + off, :, cut].astype(F32)
                    for k in addends[1:]:
                        acc = acc + ins[k][q * mult + off, :, cut].astype(F32)
                    outs[2 * n + 1 - flip][i, :, at : at + width] = acc.astype(BF)
                    at += width


def combine(here, lanes_in, name, after=(), sums=()):
    arrays, outs, plan = [], [], []

    def operand(a):
        for k, b in enumerate(arrays):
            if a is b:
                return k
        arrays.append(a)
        return len(arrays) - 1

    for pos, bit, sources in lanes_in:
        addends, mult = sources[0][0], sources[0][1]
        per, count = addends[0].shape[1], addends[0].shape[0] // mult // 2
        plan.append((pos, bit, count, [([operand(a) for a in src[0]], *src[1:]) for src in sources]))
        shape = (count, per, sum(src[4] for src in sources))
        outs += [(whole(*shape), shape, BF)] * 2
    pairs = [tuple(operand(a) for a in pair) for pair in sums]
    outs += [(whole(*pair[0].shape), pair[0].shape, BF) for pair in sums]
    got = call(
        functools.partial(combine_kernel, plan=plan, n_in=len(arrays), sums=pairs), 1, [(whole(), a) for a in arrays], outs, [],
        [here], name, after, 4,
    )
    return [(got[2 * n], got[2 * n + 1]) for n in range(len(lanes_in))] + list(got[2 * len(lanes_in) :])


def add_kernel(*refs):
    n = len(refs) // 3
    for i in range(n):
        refs[2 * n + i][...] = (refs[2 * i][...].astype(F32) + refs[2 * i + 1][...].astype(F32)).astype(BF)


def add_pairs(pairs, name, after=()):
    ins = [(whole(*a.shape), a) for pair in pairs for a in pair]
    outs = [(whole(*p[0].shape), p[0].shape, BF) for p in pairs]
    return call(add_kernel, 1, ins, outs, [], [], name, after)


def own_part(row, at, n):
    width = row.shape[1]
    return pltpu.roll(jnp.concatenate([row] * 8, axis=0), (width - at) % width, 1)[0:1, :n]


def finish_kernel(here_ref, *refs, moves, bits, gains, n_out, vectors, ranks):
    lanes_n = len(bits)
    halves, done_ref, refs = refs[: 2 * lanes_n], refs[-1], refs[2 * lanes_n : -1]
    done_ref[...] = jnp.zeros_like(done_ref)
    ins, outs = refs[: len(refs) - n_out], refs[len(refs) - n_out :]
    half = halves[0].shape[0]

    def at(lane, h, cut):
        pick = bit_of(here_ref, *bits[lane]) == h
        return jnp.where(pick, halves[2 * lane][:, cut].astype(F32), halves[2 * lane + 1][:, cut].astype(F32))

    for lane, col, width, out, row, to in moves:
        for h in range(2):
            outs[out][row + h * half : row + (h + 1) * half, to : to + width] = at(lane, h, slice(col, col + width))
    for out, norm, terms in gains:
        acc = 0.0
        for weight, grad in terms:
            product = ins[weight][...].astype(F32) * outs[grad][...]
            ones = jnp.ones((8, product.shape[1]), BF)
            high = product.astype(BF)
            acc = acc + dot(ones, high, NT) + dot(ones, (product - high.astype(F32)).astype(BF), NT)
        per = acc.shape[1]
        outs[out][...] = (acc[0:1] / own_part(ins[norm][...][None], per * here_ref[PLACE], per))[0]
    if vectors:
        lane, col, first_out = vectors
        block = at(lane, 0, slice(col, col + LANES))
        n = outs[first_out].shape[0]
        parts = n * ranks // LANES
        for k in range(2):
            row = jnp.concatenate([block[k * parts + g : k * parts + g + 1] for g in range(parts)], axis=1)
            outs[first_out + k][...] = own_part(row, n * here_ref[RANK], n)[0]


def finish(here, halves, bits, moves, extra, outs, gains, vectors, ranks, name, after=()):
    ins = [(whole(*a.shape), a) for pair in halves for a in pair] + extra
    return call(
        functools.partial(
            finish_kernel, moves=moves, bits=bits, gains=gains, n_out=len(outs), vectors=vectors, ranks=ranks
        ),
        1, ins, [(k(*shape), shape, F32) for k, shape in outs] + [(whole(), (8, LANES), F32)], [], [here], name, after,
    )


def total(parts):
    out = parts[0].astype(F32)
    for p in parts[1:]:
        out = out + p.astype(F32)
    return out.astype(BF)


def halve(parts, dim, axis, n, bit):
    mine = own_bit(axis, bit)
    got = swap(total([lax.dynamic_index_in_dim(p, 1 - mine, dim, keepdims=False) for p in parts]), axis, n, bit)
    return [lax.dynamic_index_in_dim(p, mine, dim, keepdims=False) for p in parts] + [got]


def plain_reduce(parts, bits, ndp, nseq):
    left = sorted(bits, reverse=True)
    for b in bits:
        parts = halve(parts, left.index(b), "dp", ndp, b)
        left.remove(b)
    out = total(parts)
    for b in bits_of(nseq):
        out = total([out, swap(out, "seq", nseq, b)])
    return out.astype(F32)


def local(
    ndp, nseq,
    tokens, init_state, norm_mix, w_in, w_forget, forget_bias, phase, w_ogate,
    norm_group, w_out, norm_ffn, w_gate, w_up, w_down, cotangent,
):
    segs, span, width = tokens.shape
    ch = w_forget.shape[1]
    hidden = w_gate.shape[1]
    count = segs * span
    mine = ch // nseq
    per = width // ndp
    tall = hidden // width
    rank = lax.axis_index("seq").astype(jnp.int32)
    bits = bits_of(ndp)
    first = next(b for b in bits if (per * b) % TILE == 0)
    rest = [b for b in bits if b != first]
    lo = per * first
    scan = rows(span, ch)
    scanned = (scan, (count, ch), F32)
    scan_scratch = [pltpu.VMEM((span, ch), F32)] * 2

    infos, here = call(
        own_kernel, 1, [(full(mine), phase), (full(segs, 2, mine), init_state.transpose(0, 2, 1))],
        [(whole(), (1 + segs, 2, ch), F32), (("smem",), (2,), jnp.int32)],
        [pltpu.VMEM((-(-(2 + 2 * segs) // 8) * 8, ch), F32)], [], "own",
    )
    infos = shift_all(infos, "seq", nseq)

    col = jnp.arange(width)
    pair = jnp.arange(2 * LANES)
    perm = (pair[:, None] == 2 * (pair % LANES)[None, :] + (pair // LANES)[None, :]).astype(BF)
    member = ((col[:, None] // (width // GROUPS)) == jnp.arange(LANES)[None, :]).astype(BF)

    place_of = jnp.arange(span)
    step_order = ((place_of % CHUNKS) * (span // CHUNKS) + place_of // CHUNKS)[:, None] == place_of[None, :]
    step_order = (whole(span, span), step_order.astype(BF))

    x, normed, normed_t, pre = call(
        functools.partial(project_kernel, lo=lo, first=first), segs,
        [
            (rows(span, width), tokens.reshape(count, width)), (whole(width), norm_mix), (whole(width, width), w_in),
            (whole(width, ch), w_forget), (whole(ch), forget_bias), (whole(), perm), step_order,
        ],
        [
            (rows(span, width), (count, width), BF),
            (rows(span, width), (count, width), BF),
            (cols(width, span), (width, count), BF),
            (seg(span, 3 * ch), (segs, span, 3 * ch), BF),
        ],
        [], [here], "project",
    )
    trig, chunk, totals, lam_re, lam_im, drv_re, drv_im = call(
        functools.partial(summary_kernel, ranks=nseq), segs,
        [(seg(span, 3 * ch), pre)] + [(seg(2, ch, fixed=True), i) for i in infos],
        [
            (whole(2, ch), (2, ch), F32),
            (seg(4, CHUNKS, ch), (segs, 4, CHUNKS, ch), F32),
            (seg(4, ch), (segs, 4, ch), F32),
            scanned, scanned, scanned, scanned,
        ],
        [], [], "summary",
    )
    totals = shift_all(totals, "seq", nseq)
    (og,) = call(
        gate_kernel, 1, [(whole(count, width), normed), (whole(width, width), w_ogate)],
        [(whole(count, width), (count, width), BF)], [], [], "gate", (lam_re,),
    )
    cot, dh = call(
        hidden_grad_kernel, segs,
        [(rows(span, width), cotangent.reshape(count, width)), (whole(hidden, width), w_down), step_order],
        [(rows(span, width), (count, width), BF), (rows(span, hidden), (count, hidden), BF)], [], [], "hidden_grad",
        (lam_re,),
    )
    y, y_split, start, final, gated_t, middle, ginv = call(
        functools.partial(mixer_kernel, ranks=nseq, lo=lo, first=first), segs,
        [(seg(4, ch), t) for t in totals]
        + [(seg(2, ch, shift=1), i) for i in infos]
        + [
            (scan, lam_re), (scan, lam_im), (scan, drv_re), (scan, drv_im), (seg(4, CHUNKS, ch), chunk),
            (whole(), perm), (rows(span, width), x), (rows(span, width), og), (whole(width), norm_group),
            (whole(width, LANES), member), (whole(width, width), w_out),
        ],
        [
            (rows(span, width), (count, width), BF),
            (rows(span, width), (count, width), BF),
            (seg(2, ch), (segs, 2, ch), F32),
            (seg(2, mine), (segs, 2, mine), F32),
            (cols(width, span), (width, count), BF),
            (rows(span, width), (count, width), F32),
            (rows(span, LANES), (count, LANES), F32),
        ],
        scan_scratch, [here], "mixer",
    )
    final_state = final.transpose(0, 2, 1)

    wide = (count, width)
    done = (whole(), (8, LANES), F32)
    psend, pkeep, normed_ffn, normed_ffn_t, hid0, dgv0, duv0 = call(
        functools.partial(ffn_first_kernel, lo=lo, rt=span, first=first), 1,
        [(whole(), a) for a in (middle, norm_ffn, w_gate, w_up, dh)],
        [(whole(), (width // 2, 2 * width), BF)] * 2
        + [(whole(), wide, BF), (whole(), (width, count), BF)]
        + [(whole(), wide, BF)] * 3,
        [], [here], "ffn_first", (), 7,
    )
    pgot = swap(psend, "dp", ndp, first)
    gsend, gkeep, dsend, dkeep, hid, dgv1, duv1 = call(
        functools.partial(ffn_rest_kernel, lo=lo * tall, rt=span, first=first), 1,
        [(whole(), a) for a in (normed_ffn, normed_ffn_t, cot, w_gate, w_up, dh, hid0)],
        [(whole(), (width // 2, 2 * width), BF)] * 2 + [(whole(), (hidden // 2, width), BF)] * 2
        + [(whole(), wide, BF)] * 3,
        [pltpu.VMEM((tall, width, count), BF)], [here], "ffn_rest", (psend,), 7,
    )
    ggot, dgot = swap(gsend, "dp", ndp, first), swap(dsend, "dp", ndp, first)

    nblk = ndp // 2
    fast = ndp == 8 and nseq == 4 and per % (2 * TILE) == 0
    x_bit, y_bit = (PLACE, rest[0]), (PLACE, rest[1])
    z_bits = [(RANK, b) for b in bits_of(nseq)]

    def blocks(a, cols_n, tall_n=1):
        return a.reshape(nblk * tall_n, per, cols_n)

    def ffn_back(tile, dgv, duv, before, *after):
        return call(
            functools.partial(ffn_back_kernel, tile=tile), segs,
            [(rows(span, width), a) for a in (dgv, duv)] + [(whole(), w_gate), (whole(), w_up)]
            + [(rows(span, width), a) for a in before],
            [(rows(span, width), wide, F32)], [], [], "ffn_back", after,
        )[0]

    order = ()
    if fast:
        p = [blocks(a, 2 * width) for a in (pkeep, pgot)]
        (pa_send, pa_keep), (pb_send, pb_keep) = combine(
            here, [(0, x_bit, [(p, 1, 0, 0, width)]), (1, y_bit, [(p, 1, 0, 1, width)])], "first_sum1", (gkeep,)
        )
        pa_got, pb_got = swap(pa_send, "dp", ndp, rest[0]), swap(pb_send, "dp", ndp, rest[1])
        dn = ffn_back(0, dgv0, duv0, (), pa_keep)
        g = [blocks(a, 2 * width) for a in (gkeep, ggot)]
        d = [blocks(a, width, tall) for a in (dkeep, dgot)]
        (fa_send, fa_keep), (fb_send, fb_keep) = combine(
            here, [(0, x_bit, [(g, 1, 0, 0, 2 * width)]), (1, y_bit, [(d, tall, i, 0, width) for i in range(tall)])],
            "ffn_sum1", (dn,),
        )
        fa_got, fb_got = swap(fa_send, "dp", ndp, rest[0]), swap(fb_send, "dp", ndp, rest[1])
        order = (fa_keep,)
    else:
        dn = ffn_back(0, dgv0, duv0, ())
    dn = ffn_back(1, dgv1, duv1, (dn,), *order)

    dmiddle, dbranch, dog, dy_split = call(
        turn_kernel, segs,
        [
            (rows(span, width), dn), (rows(span, width), middle), (rows(span, width), cot), (whole(width), norm_ffn),
            (whole(width, width), w_out), (rows(span, width), y), (rows(span, LANES), ginv), (rows(span, width), og),
            (whole(width), norm_group),
            (whole(width, LANES), member), (whole(), perm),
        ],
        [
            (rows(span, width), (count, width), F32),
            (rows(span, width), (count, width), BF),
            (rows(span, width), (count, width), BF),
            (rows(span, width), (count, width), BF),
        ],
        [], [], "turn", order,
    )
    order = ()
    if fast:
        pa, pb = add_pairs([(pa_keep, pa_got), (pb_keep, pb_got)], "first_sum2", (dog,))
        order = (pa,)

    chain, adj = call(
        chains_kernel, segs,
        [(rows(span, width), dy_split), (scan, lam_re), (scan, lam_im), (seg(4, CHUNKS, ch), chunk)],
        [(seg(2, CHUNKS, ch), (segs, 2, CHUNKS, ch), F32), (seg(2, ch), (segs, 2, ch), F32)],
        scan_scratch, [], "chains", order,
    )
    adjs = shift_all(adj, "seq", nseq)
    order = ()
    if fast:
        def one(keep, got):
            return [([keep, got], 1, 0, 0, keep.shape[2])]

        def rows_of(keep, got):
            return one(*(a.reshape(2, per // 2, a.shape[2]) for a in (keep, got)))

        (fa_send, fa_keep), (fb_send, fb_keep) = combine(
            here,
            [
                (0, y_bit, [([pa], 1, 0, 0, width)] + one(fa_keep, fa_got)),
                (0, x_bit, [([pb], 1, 0, 0, width)] + one(fb_keep, fb_got)),
            ],
            "ffn_sum2", (chain,),
        )
        fa_got, fb_got = swap(fa_send, "dp", ndp, rest[1]), swap(fb_send, "dp", ndp, rest[0])
        order = (fa_keep,)

    ntile = width // 3
    osend, okeep = call(
        functools.partial(grads_kernel, pairs=2), width // ntile,
        [
            (whole(width, count), normed_t), (cols(count, ntile), dog),
            (whole(width, count), gated_t), (cols(count, ntile), dbranch),
        ],
        [
            (cols(width // 2, 2 * ntile), (width // 2, 2 * width), BF),
            (cols(width // 2, 2 * ntile), (width // 2, 2 * width), BF),
        ],
        [], [], "mixer_grads", order,
    )
    late, *adjs = lax.optimization_barrier((osend, *adjs))
    ogot = swap(late, "dp", ndp, first)

    dpre, sums = call(
        functools.partial(adjoint_kernel, ranks=nseq), segs,
        [(seg(4, ch), t) for t in totals] + [(seg(2, ch), a) for a in adjs]
        + [
            (seg(span, 3 * ch), pre), (whole(2, ch), trig), (scan, lam_re), (scan, lam_im),
            (rows(span, width), dy_split),
            (rows(span, width), y_split), (seg(2, ch), start),
            (seg(4, CHUNKS, ch), chunk), (seg(2, CHUNKS, ch), chain), (whole(), perm),
        ],
        [(rows(span, 3 * ch), (count, 3 * ch), BF), (whole(2, ch), (2, ch), F32)],
        scan_scratch, [here], "adjoint", (osend,),
    )
    into = 3 * ch + LANES
    isend, ikeep = call(
        functools.partial(input_grads_kernel, per=per), 1,
        [(whole(width, count), normed_t), (whole(count, 3 * ch), dpre), (whole(2, ch), sums)],
        [(whole(width // 2, into), (width // 2, into), BF)] * 2, [], [], "input_grads",
    )
    igot = swap(isend, "dp", ndp, first)
    order = ()
    if fast:
        lead, other = bits_of(nseq)

        def over(send, axis_n, bit):
            return swap(send, "seq", axis_n, bit)

        (fa_send, fa_keep), (fb_send, fb_keep) = combine(
            here, [(0, z_bits[0], rows_of(fa_keep, fa_got)), (0, z_bits[1], rows_of(fb_keep, fb_got))],
            "ffn_sum3", (isend,),
        )
        fa_got, fb_got = over(fa_send, nseq, lead), over(fb_send, nseq, other)
        o = [blocks(a, 2 * width) for a in (okeep, ogot)]
        i = [blocks(a, into) for a in (ikeep, igot)]
        (ra_send, ra_keep), (rb_send, rb_keep) = combine(
            here,
            [
                (0, x_bit, [(o, 1, 0, 0, 2 * width - LANES)]),
                (1, y_bit, [(i, 1, 0, 0, into), (o, 1, 0, 2 * width // LANES - 1, LANES)]),
            ],
            "mixer_sum1", (fa_keep,)
        )
        ra_got, rb_got = swap(ra_send, "dp", ndp, rest[0]), swap(rb_send, "dp", ndp, rest[1])
        order = (ra_keep,)

    grad_tokens, tokens_done = call(
        tokens_kernel, segs,
        [
            (rows(span, 3 * ch), dpre), (rows(span, width), dog), (whole(width, width), w_in),
            (whole(width, ch), w_forget), (whole(width, width), w_ogate), (rows(span, width), x),
            (whole(width), norm_mix), (rows(span, width), dmiddle), step_order,
        ],
        [(moved(span, width, dim=0), (count, width), BF), done],
        [], [], "tokens", order,
    )

    def output(*after):
        return call(
            out_kernel, segs,
            [(rows(span, width), a) for a in (middle, hid0, hid)] + [(whole(hidden, width), w_down), step_order],
            [(moved(span, width, dim=0), (count, width), BF), done], [], [], "out", after,
        )

    if fast:
        fa, fb = add_pairs([(fa_keep, fa_got), (fb_keep, fb_got)], "ffn_sum4", (tokens_done,))
        fa_got, fb_got = over(fa, nseq, other), over(fb, nseq, lead)
        (ra_send, ra_keep), (rb_send, rb_keep) = combine(
            here, [(0, y_bit, one(ra_keep, ra_got)), (0, x_bit, one(rb_keep, rb_got))], "mixer_sum2", (fa,)
        )
        ra_got, rb_got = swap(ra_send, "dp", ndp, rest[1]), swap(rb_send, "dp", ndp, rest[0])
        mixed_out, out_done = output(ra_keep)
        (ra_send, ra_keep), (rb_send, rb_keep) = combine(
            here, [(0, z_bits[0], rows_of(ra_keep, ra_got)), (0, z_bits[1], rows_of(rb_keep, rb_got))], "mixer_sum3", (out_done,)
        )
        ra_got, rb_got = over(ra_send, nseq, lead), over(rb_send, nseq, other)
        fa, fb = add_pairs([(fa, fa_got), (fb, fb_got)], "ffn_sum5", (ra_keep,))
        fa_got, fb_got = over(fa, nseq, lead), over(fb, nseq, other)
        ra, rb = add_pairs([(ra_keep, ra_got), (rb_keep, rb_got)], "mixer_sum4", (fa,))
        ra_got, rb_got = over(ra, nseq, other), over(rb, nseq, lead)

        ra, rb = add_pairs([(ra, ra_got), (rb, rb_got)], "mixer_sum5")
        ra_got, rb_got = over(ra, nseq, lead), over(rb, nseq, other)

        def flat(*pairs):
            return [tuple(a.reshape(per // 2, a.shape[2]) for a in pair) for pair in pairs]

        moves = [(0, 0, width, 0, 0, 0), (0, width, width, 0, 0, width), (0, 2 * width, width, 1, 0, width)]
        moves += [(1, 0, width, 1, 0, 0)] + [(1, (1 + t) * width, width, 2, t * per, 0) for t in range(tall)]
        part_gate, part_up, part_down, part_ffn, ffn_done = finish(
            here, flat((fa, fa_got), (fb, fb_got)), z_bits, moves,
            [(ours(per, hidden), w_gate), (ours(per, hidden), w_up), (whole(width), norm_ffn)],
            [(full, (per, hidden)), (full, (per, hidden)), (full, (tall * per, width)), (full, (per,))],
            [(3, 2, [(0, 0), (1, 1)])], None, nseq, "ffn_out", (ra,),
        )
        moves = [(0, n * ntile, ntile, n % 2, 0, (n // 2) * ntile) for n in range(2 * width // ntile - 1)]
        moves += [(0, 2 * width - ntile, ntile - LANES, 1, 0, width - ntile), (1, into, LANES, 1, 0, width - LANES)]
        moves += [(1, 0, width, 2, 0, 0), (1, width, ch, 3, 0, 0)]
        part_ogate, part_out, part_in, part_forget, part_mix, part_group, part_bias, part_phase, _ = finish(
            here, flat((ra, ra_got), (rb, rb_got)), z_bits, moves,
            [
                (ours(per, width), w_ogate), (ours(per, width), w_out), (ours(per, width), w_in), (ours(per, ch), w_forget),
                (whole(width), norm_mix), (whole(width), norm_group),
            ],
            [(full, (per, n)) for n in (width, width, width, ch)] + [(full, (n,)) for n in (per, per, mine, mine)],
            [(4, 4, [(0, 0), (2, 2), (3, 3)]), (5, 5, [(1, 1)])], (1, 3 * ch, 6), nseq, "mixer_out",
        )
    else:
        mixed_out, _ = output()

        def plain(keep, got, cols_n, tall_n=1):
            shape = [2] * len(rest) + [tall_n * per, cols_n]
            return plain_reduce([keep.reshape(shape), got.reshape(shape)], rest, ndp, nseq)

        guv = [plain(pkeep, pgot, 2 * width), plain(gkeep, ggot, 2 * width)]
        part_gate = jnp.concatenate([a[:, :width] for a in guv], axis=1)
        part_up = jnp.concatenate([a[:, width:] for a in guv], axis=1)
        part_down = plain(dkeep, dgot, width, tall)
        mix = plain(okeep, ogot, 2 * width)
        mix = [mix[:, n * ntile : (n + 1) * ntile] for n in range(2 * width // ntile)]
        part_ogate, part_out = jnp.concatenate(mix[0::2], axis=1), jnp.concatenate(mix[1::2], axis=1)
        both = plain(ikeep, igot, into)
        part_in, part_forget = both[:, :width], both[:, width : 3 * ch]
        shared = both[: 2 * ch // LANES, 3 * ch :].reshape(2, ch)
        part_bias, part_phase = lax.dynamic_slice_in_dim(shared, rank * mine, mine, axis=1)

        def own_rows(a):
            return lax.dynamic_slice_in_dim(a, lax.axis_index("dp") * per, per, axis=0).astype(F32)

        def gain_of(norm, *pairs):
            return sum(jnp.sum(own_rows(w) * gw, axis=1) for w, gw in pairs) / own_rows(norm)

        part_ffn = gain_of(norm_ffn, (w_gate, part_gate), (w_up, part_up))
        part_mix = gain_of(norm_mix, (w_in, part_in), (w_forget, part_forget), (w_ogate, part_ogate))
        part_group = gain_of(norm_group, (w_out, part_out))
    return (
        mixed_out.reshape(segs, span, width),
        grad_tokens.reshape(segs, span, width),
        final_state,
        part_mix, part_in, part_forget, part_bias, part_phase, part_ogate, part_group, part_out, part_ffn,
        part_gate, part_up, part_down,
    )


def solution(mesh):
    ndp, nseq = mesh.shape["dp"], mesh.shape["seq"]
    tok, vec, col = P("dp", "seq", None), P("dp"), P("dp", None)
    return jax.shard_map(
        functools.partial(local, ndp, nseq),
        mesh=mesh,
        in_specs=(tok, tok, P(), P(), P(), P(), P("seq"), P(), P(), P(), P(), P(), P(), P(), tok),
        out_specs=(tok, tok, tok, vec, col, col, P("seq"), P("seq"), col, vec, col, vec, col, col, col),
        check_vma=False,
    )
```
